32 devices in a mesh: grp: 2 (over y), exp: 4 (over x, core), hid: 4 (over z).
Axes of the slice: x: 2, y: 2, z: 4, core: 2. Of those that a mesh axis runs over, the one named last changes fastest.
Arguments:
- tokens: bfloat16 [1024, 4096], P(('grp', 'exp'), 'hid'), parts along dimension 0, may hold values from -6 to 6
- grad_out: bfloat16 [1024, 4096], P(('grp', 'exp'), 'hid'), parts along dimension 0, may hold values from -3 to 3
- gates: bfloat16 [1024, 2], P(('grp', 'exp')), parts along dimension 0, may hold values from 0.049804688 to 1
- block_experts: int32 [8, 2], P('grp'), parts along dimension 0, may hold values from 0 to 3, all different within a row; in each aligned block of 4 rows (0 to 3, 4 to 7, ...) at most 2 rows name the same one
- w_gate: bfloat16 [4, 4096, 8192], P('exp', None, 'hid'), may hold values from -0.125 to 0.125
- w_up: bfloat16 [4, 4096, 8192], P('exp', None, 'hid'), may hold values from -0.125 to 0.125
- w_down: bfloat16 [4, 8192, 4096], P('exp', 'hid'), may hold values from -0.0625 to 0.0625
Outputs:
- d_tokens: bfloat16 [1024, 4096], P(('grp', 'exp'), 'hid'), parts along dimension 0
- d_gates: float32 [1024, 2], P(('grp', 'exp')), parts along dimension 0
The draws below stay inside these ranges and needn't reach their ends.
There are 2 independent parts, one for each index of `grp`. The reference program is written for one: setup_inputs(seed, part) draws one part's arguments, and reference() takes and returns one part's arrays. A program takes and returns all parts, laid end to end along the dimension named above; an argument that names none is the same for every part. Nothing has to cross between parts.
Inputs may be any that keep to these rules, and one draw needn't show every extreme that they name: `block_experts`: each row names two different experts for one block of 128 tokens; no expert is named by more than 2 of the 4 blocks, one expert by exactly 2, and every expert by some block.
All inputs are finite; a program needn't handle non-finite values.
Results may differ from the reference program's by a relative error of at most 0.0049.
Values may be sent and summed in bfloat16 or wider, within the bound.
A program may use at most 192 MiB of HBM per device.

```python
import math
import jax
import jax.numpy as jnp
import numpy as np
from jax import lax

D = 4096
FF = 8192
BLOCK = 128
EXPERTS = 4
TOKENS = 512
NBLK = 4
CAPB = 2


def raised(drawn, own_key, source, target, blocks, factor):
    owner, partner = [(jnp.arange(drawn.shape[position]) // (drawn.shape[position] // blocks)).reshape([-1 if axis == position else 1 for axis in range(drawn.ndim)]) for position in (source, target)]
    chosen = jax.random.permutation(own_key, blocks)[partner]
    strong = (owner == chosen) | (owner == (partner + blocks // 2) % blocks)
    return jnp.where(strong, factor * drawn, drawn)


def block_scale(key, shape, cuts, smallest, high):
    factor_of = 1.0
    for dim, blocks in cuts:
        steps = jax.random.uniform(jax.random.fold_in(jax.random.fold_in(key, 6), dim), (blocks,), jnp.float32, smallest / len(cuts), high / len(cuts))
        factor_of = factor_of * jnp.repeat(jnp.exp(steps), shape[dim] // blocks).reshape((-1,) + (1,) * (len(shape) - 1 - dim))
    return factor_of


def routed_block(stream_key, own, number, rows, number_of, top, most, lean):
    order = jax.random.permutation(stream_key, number_of)
    packed, common = portions_of(number_of, rows * top, most, lean, True), portions_of(number_of, rows * top, most, lean, False)
    places = jnp.arange(number_of)

    def named(sizes, rotation):
        used = int((sizes > 0).sum())
        fixed = max(1, used // 4)
        shifted = fixed + (places - fixed + rotation * (used - fixed)) % max(1, number_of - fixed)
        return jnp.zeros((number_of,), jnp.int32).at[order[jnp.where(places < fixed, places, shifted)]].set(jnp.asarray(sizes, jnp.int32))

    sizes = jnp.where(number % 4 == 0, named(packed, number // 4), named(common, number - number // 4 - 1))
    mixed = jax.random.permutation(jax.random.fold_in(own, 3), number_of)
    donor, receiver = mixed[0:number_of // 2 * 2:2], mixed[1:number_of // 2 * 2:2]
    margin = jnp.minimum(sizes[donor] - 1, most - sizes[receiver]) // 2
    margin = jnp.where((donor == order[0]) | (receiver == order[0]) | (sizes[receiver] == 0), 0, jnp.maximum(margin, 0))
    shifted = jax.random.randint(jax.random.fold_in(own, 4), (number_of // 2,), 0, 1 << 20) % (margin + 1)
    sizes = sizes.at[donor].add(-shifted).at[receiver].add(shifted)
    items = jnp.searchsorted(jnp.cumsum(sizes), jnp.arange(rows * top), side="right").astype(jnp.int32)
    grid = items.reshape(top, rows).T
    grid = grid[jax.random.permutation(jax.random.fold_in(own, 1), rows)]
    rotation = jax.random.randint(jax.random.fold_in(own, 2), (rows, 1), 0, top)
    return jnp.take_along_axis(grid, (jnp.arange(top)[None, :] + rotation) % top, axis=1)


def portions_of(number_of, total, limit, slope, full):
    loads = [(1 << 20) // math.isqrt(rank ** slope) + 1 for rank in range(1, number_of + 1)]
    largest = limit if full else min(limit, max(-(-total // number_of), total * loads[0] // sum(loads)))
    least = 1 if total - largest >= number_of - 1 else 0
    counts, surplus = [largest] + [least] * (number_of - 1), total - largest - least * (number_of - 1)
    while surplus > 0:
        candidates = [i for i in range(1, number_of) if counts[i] < largest] or [i for i in range(1, number_of) if counts[i] < limit]
        whole, left = sum([loads[i] for i in candidates]), surplus
        for i in candidates:
            more = min(limit - counts[i], max(1, left * loads[i] // whole), surplus)
            counts[i] = counts[i] + more
            surplus = surplus - more
    return np.array(counts)


def scatter_about(stream_key, extent, spread, bound, cuts=(), held_as=jnp.bfloat16):
    factor_of = block_scale(stream_key, extent, cuts, -0.22, 0.18) if cuts else 1.0
    values = jax.random.normal(stream_key, extent, jnp.float32) * spread * factor_of
    return jnp.minimum(jnp.maximum(values, -bound), bound).astype(held_as)


def heavy_noise(rng, shape, spread, limit, pieces, heavy, kind=jnp.bfloat16):
    entries = spread * jax.random.normal(rng, shape, jnp.float32)
    if pieces:
        entries = entries * block_scale(rng, shape, pieces, -0.22, 0.18)
    return jnp.clip(raised(entries, jax.random.fold_in(rng, 3), *heavy), -limit, limit).astype(kind)


def setup_inputs(seed: int = 0, part: int = 0) -> dict:
    key_list = jax.random.split(jax.random.key(seed), 8)
    part_splits = jax.random.split(jax.random.fold_in(key_list[7], part), 8)
    tokens = scatter_about(part_splits[0], (TOKENS, D), 1.0, 6.0, ((0, 4), (1, 4)))
    grad_out = scatter_about(part_splits[1], (TOKENS, D), 0.5, 3.0, ((0, 4), (1, 4)))
    gates = jnp.clip(0.049804688 + 0.9501953 * jax.random.uniform(part_splits[2], (TOKENS, 2), jnp.float32) ** block_scale(part_splits[2], (TOKENS, 2), ((0, 4),), -0.2, 0.2), 0.049804688, 1.0).astype(jnp.bfloat16)
    block_experts_keys = jax.random.split(jax.random.fold_in(part_splits[3], 1), NBLK // NBLK)
    block_experts_turns = jax.random.permutation(jax.random.fold_in(part_splits[3], 3), NBLK // NBLK)
    block_experts = jax.vmap(lambda own, number: routed_block(jax.random.fold_in(part_splits[3], 2), own, number, NBLK, EXPERTS, 2, CAPB, 2))(block_experts_keys, block_experts_turns).reshape((NBLK, 2))
    w_gate = heavy_noise(key_list[4], (EXPERTS, D, FF), D ** -0.5, 0.125, ((0, 4), (2, 4)), (2, 1, 4, 2.0))
    w_up = heavy_noise(key_list[5], (EXPERTS, D, FF), D ** -0.5, 0.125, ((0, 4), (2, 4)), (2, 1, 4, 2.0))
    w_down = scatter_about(key_list[6], (EXPERTS, FF, D), FF ** -0.5, 0.0625, ((0, 4), (1, 4)))
    return {"tokens": tokens, "grad_out": grad_out, "gates": gates, "block_experts": block_experts, "w_gate": w_gate, "w_up": w_up, "w_down": w_down}


def expert_pass(x_rows, dy_rows, gate_column, w_one, w_three, w_two):
    pre_gate = jnp.dot(x_rows, w_one, preferred_element_type=jnp.float32)
    pre_up = jnp.dot(x_rows, w_three, preferred_element_type=jnp.float32)
    d_hidden = jnp.dot(dy_rows, w_two.T, preferred_element_type=jnp.float32)
    sigmoid_gate = jax.nn.sigmoid(pre_gate)
    activated = pre_gate * sigmoid_gate
    score = jnp.sum(activated * pre_up * d_hidden, axis=1)
    scaled = gate_column[:, None] * d_hidden
    d_pre_gate = (scaled * pre_up * sigmoid_gate * (1.0 + pre_gate * (1.0 - sigmoid_gate))).astype(jnp.bfloat16)
    d_pre_up = (scaled * activated).astype(jnp.bfloat16)
    part = jnp.dot(d_pre_gate, w_one.T, preferred_element_type=jnp.float32)
    part = part + jnp.dot(d_pre_up, w_three.T, preferred_element_type=jnp.float32)
    return part, score


def reference(tokens, grad_out, gates, block_experts, w_gate, w_up, w_down):
    rows_x = tokens.reshape(NBLK, BLOCK, D)
    rows_dy = grad_out.reshape(NBLK, BLOCK, D)
    gate_rows = gates.astype(jnp.float32).reshape(NBLK, BLOCK, 2)

    def one_pair(pair_index):
        block_index = pair_index // 2
        slot_index = pair_index % 2
        expert = block_experts[block_index, slot_index]
        gate_column = jnp.take(gate_rows[block_index], slot_index, axis=1)
        return expert_pass(rows_x[block_index], rows_dy[block_index], gate_column,
                           w_gate[expert], w_up[expert], w_down[expert])

    parts, scores = lax.map(one_pair, jnp.arange(2 * NBLK, dtype=jnp.int32))
    parts = parts.reshape(NBLK, 2, BLOCK, D)
    d_tokens = (parts[:, 0] + parts[:, 1]).reshape(TOKENS, D).astype(jnp.bfloat16)
    d_gates = jnp.transpose(scores.reshape(NBLK, 2, BLOCK), (0, 2, 1)).reshape(TOKENS, 2)
    return d_tokens, d_gates
```

```python
import functools
import jax
import jax.numpy as jnp
from jax import lax
from jax.experimental import pallas as pl
from jax.experimental.pallas import tpu as pltpu
from jax.sharding import PartitionSpec as P

BLOCK = 128


HIGHEST = lax.Precision.HIGHEST
CONTRACT_LAST = (((1,), (1,)), ((), ()))
MESH = pl.DeviceIdType.MESH
TILE = 512


def passed_along(block, axis, distance):
    devices = range(lax.axis_size(axis))
    route = [((i - distance) % len(devices), i) for i in devices]
    return lax.ppermute(block, axis, route)


def routing(block_experts, own_index):
    blocks_all = block_experts.shape[0]
    capacity = blocks_all // 2
    matched = block_experts == own_index
    chosen = jnp.any(matched, axis=1)
    slot_of = matched[:, 1].astype(jnp.int32)
    order = jnp.arange(blocks_all, dtype=jnp.int32)
    position = jnp.sum((chosen[None, :] & (order[None, :] < order[:, None])).astype(jnp.int32), axis=1)
    placed = (position[None, :] == jnp.arange(capacity, dtype=jnp.int32)[:, None]) & chosen[None, :]
    placed_int = placed.astype(jnp.int32)
    list_block = jnp.sum(placed_int * jnp.arange(blocks_all, dtype=jnp.int32)[None, :], axis=1)
    list_slot = jnp.sum(placed_int * slot_of[None, :], axis=1)
    live = jnp.any(placed, axis=1)
    return list_block, list_slot, live


def layer_kernel(nz, ne, tok, width, tok_ref, dy_ref, gate_ref, pick_ref, slot_ref, home_ref, scat_ref,
                 w1_ref, w3_ref, w2_ref, out_ref, grad_gate_ref,
                 xb, db, gb, w1, w3, w2, pg, pu, dh, dpg_ref, dpu_ref, score_ref, sd_ref,
                 dense, cr, xs, xr, zs, zr, acc, scr, sxs, sxr, szs, szr,
                 s_up, s_dn, s_x, s_c, rsem, gs, gr, wsem, lsem,
                 css, crs, xss, xrs, zss, zrs, gcs, gcr, gxs, gxr, gzs, gzr):
    z = lax.axis_index("hid")
    e = lax.axis_index("exp")
    mate = e + 1 - 2 * lax.rem(e, 2)
    across = lax.rem(e + 2, ne)
    bufs = (xb, db)
    hidden = w1.shape[2]

    def weights(q, slot):
        rows = pl.ds(pl.multiple_of(q * width, width), width)
        return (
            pltpu.make_async_copy(w1_ref.at[0, rows, :], w1.at[slot], wsem.at[slot, 0]),
            pltpu.make_async_copy(w3_ref.at[0, rows, :], w3.at[slot], wsem.at[slot, 1]),
            pltpu.make_async_copy(w2_ref.at[0, :, rows], w2.at[slot], wsem.at[slot, 2]),
        )

    def send(a, zq, eq, ssem, dev):
        return pltpu.make_async_remote_copy(
            src_ref=bufs[a].at[zq, eq], dst_ref=bufs[a].at[zq, eq],
            send_sem=ssem, recv_sem=rsem.at[a, zq, eq],
            device_id=dev, device_id_type=MESH)

    def up(a, zq):
        return send(a, zq, e, s_up.at[a, zq], {"hid": z + 1})

    def down(a, zq):
        return send(a, zq, e, s_dn.at[a, zq], {"hid": z - 1})

    def over_x(a, zq):
        return send(a, zq, e, s_x.at[a, zq], {"exp": across})

    def to_mate(a, zq, eq, k):
        return send(a, zq, eq, s_c.at[a, zq, k], {"exp": mate})

    def arrived(a, zq, eq):
        send(a, zq, eq, s_x.at[a, zq], {"exp": across}).wait_recv()

    def gate_send(eq, k, dev):
        return pltpu.make_async_remote_copy(
            src_ref=gb.at[eq], dst_ref=gb.at[eq], send_sem=gs.at[k], recv_sem=gr.at[eq],
            device_id={"exp": dev}, device_id_type=MESH)

    own = (
        pltpu.make_async_copy(tok_ref, xb.at[z, e], lsem.at[0]),
        pltpu.make_async_copy(dy_ref, db.at[z, e], lsem.at[1]),
        pltpu.make_async_copy(gate_ref, gb.at[e], lsem.at[2]),
    )
    for c in own:
        c.start()
    for c in weights(z, 1):
        c.start()

    @pl.when(z > 0)
    def _():
        for c in weights(z - 1, 0):
            c.start()

    barrier = pltpu.get_barrier_semaphore()
    pl.semaphore_signal(barrier, inc=1, device_id={"exp": mate}, device_id_type=MESH)
    pl.semaphore_signal(barrier, inc=1, device_id={"exp": across}, device_id_type=MESH)

    for k in range(nz - 1):
        pl.semaphore_signal(barrier, inc=1, device_id={"hid": lax.rem(z + 1 + k, nz)}, device_id_type=MESH)
    pl.semaphore_wait(barrier, nz + 1)

    for c in own:
        c.wait()
    for a in range(2):
        @pl.when(z < nz - 1)
        def _():
            up(a, z).start()

        @pl.when(z > 0)
        def _():
            down(a, z).start()

        over_x(a, z).start()
        to_mate(a, z, e, 0).start()
    gate_send(e, 0, across).start()
    gate_send(e, 1, mate).start()

    pg[...] = jnp.zeros_like(pg)
    pu[...] = jnp.zeros_like(pu)
    dh[...] = jnp.zeros_like(dh)

    def pass_on(d):
        for a in range(2):
            @pl.when(z - d >= 0)
            def _():
                arrived(a, z - d, e)

                @pl.when(z < nz - 1)
                def _():
                    up(a, z - d).start()

                over_x(a, z - d).start()
                to_mate(a, z - d, e, 0).start()

            @pl.when(z + d < nz)
            def _():
                arrived(a, z + d, e)

                @pl.when(z > 0)
                def _():
                    down(a, z + d).start()

                over_x(a, z + d).start()
                to_mate(a, z + d, e, 0).start()

    mate_across = lax.rem(mate + 2, ne)

    def picked(a, zq):
        arrived(a, zq, across)
        to_mate(a, zq, across, 1).start()
        arrived(a, zq, mate)
        arrived(a, zq, mate_across)
        rows = bufs[a][zq].reshape(ne * tok, width)
        return jnp.dot(pick_ref[...], rows, preferred_element_type=jnp.float32).astype(jnp.bfloat16)

    def compute(zq, slot):
        pending = weights(zq, slot)
        xs = picked(0, zq)
        pending[0].wait()
        pending[1].wait()

        @pl.loop(0, hidden // TILE)
        def _(t):
            cols = pl.ds(pl.multiple_of(t * TILE, TILE), TILE)
            pg[:, cols] += jnp.dot(xs, w1[slot, :, cols], preferred_element_type=jnp.float32)
            pu[:, cols] += jnp.dot(xs, w3[slot, :, cols], preferred_element_type=jnp.float32)

        ds = picked(1, zq)
        pending[2].wait()

        @pl.loop(0, hidden // TILE)
        def _(t):
            cols = pl.ds(pl.multiple_of(t * TILE, TILE), TILE)
            dh[:, cols] += lax.dot_general(ds, w2[slot, cols, :], CONTRACT_LAST, preferred_element_type=jnp.float32)

    @pl.loop(0, nz)
    def _(d):
        @pl.when(d < nz - 1)
        def _():
            pass_on(d + 1)

        @pl.when((d > 0) & (z - d >= 0))
        def _():
            compute(z - d, 0)

            @pl.when(z - d - 1 >= 0)
            def _():
                for c in weights(z - d - 1, 0):
                    c.start()

        @pl.when(z + d < nz)
        def _():
            compute(z + d, 1)

            @pl.when(z + d + 1 < nz)
            def _():
                for c in weights(z + d + 1, 1):
                    c.start()

    core = lax.rem(e, 2)
    mate_core = 1 - core
    x = e // 2
    far = 1 - x

    def again(k, slot):
        q = lax.rem(z + 1 + k, nz)
        rows = pl.ds(pl.multiple_of(q * width, width), width)
        return (
            pltpu.make_async_copy(w1_ref.at[0, rows, :], w1.at[slot], wsem.at[slot, 0]),
            pltpu.make_async_copy(w3_ref.at[0, rows, :], w3.at[slot], wsem.at[slot, 1]),
        )

    def remote(src, dst, ssem, rsem, dev):
        return pltpu.make_async_remote_copy(
            src_ref=src, dst_ref=dst, send_sem=ssem, recv_sem=rsem, device_id=dev, device_id_type=MESH)

    def core_send(k, j):
        return remote(dense.at[k, mate_core + 2 * j], cr.at[k, j], css.at[k, j], crs.at[k, j], {"exp": mate})

    def x_send(k):
        return remote(xs.at[k], xr.at[k], xss.at[k], xrs.at[k], {"exp": across})

    def z_send(k):
        return remote(zs.at[k], zr.at[z], zss.at[k], zrs.at[z], {"hid": lax.rem(z + 1 + k, nz)})

    def gate_core(j):
        return remote(sd_ref.at[mate_core + 2 * j], scr.at[j], gcs.at[j], gcr.at[j], {"exp": mate})

    def gate_x():
        return remote(sxs, sxr, gxs.at[0], gxr.at[0], {"exp": across})

    def gate_z(k):
        return remote(szs, szr.at[z], gzs.at[k], gzr.at[z], {"hid": lax.rem(z + 1 + k, nz)})

    for k in range(2):
        for c in again(k, k):
            c.start()

    gate_send(across, 2, across).wait_recv()
    gate_send(across, 2, mate).start()
    gate_send(mate, 2, mate).wait_recv()
    gate_send(lax.rem(mate + 2, ne), 2, mate).wait_recv()
    gates = jnp.dot(pick_ref[...], gb[...].reshape(ne * tok, gb.shape[2]), preferred_element_type=jnp.float32)
    gate = jnp.sum(gates * slot_ref[...], axis=1, keepdims=True)
    score_ref[...] = jnp.zeros_like(score_ref)

    @pl.loop(0, hidden // 128)
    def _(t):
        cols = pl.ds(pl.multiple_of(t * 128, 128), 128)
        g = pg[:, cols]
        u = pu[:, cols]
        h = dh[:, cols]
        sig = 1.0 / (1.0 + jnp.exp(-g))
        act = g * sig
        score_ref[...] += act * u * h
        scaled = gate * h
        dpg_ref[:, cols] = (scaled * u * sig * (1.0 + g * (1.0 - sig))).astype(jnp.bfloat16)
        dpu_ref[:, cols] = (scaled * act).astype(jnp.bfloat16)

    score = jnp.sum(score_ref[...], axis=1, keepdims=True) * slot_ref[...]
    for home in range(ne):
        mine = score * home_ref[:, home : home + 1]
        placed = mine[:tok]
        for i in range(1, mine.shape[0] // tok):
            placed += mine[i * tok : (i + 1) * tok]
        sd_ref[home] = placed

    for j in range(2):
        gate_core(j).start()

    def multiply(k):
        slot = lax.rem(k, 2)
        for c in again(k, slot):
            c.wait()

        @pl.loop(0, width // 256)
        def _(t):
            rows = pl.ds(pl.multiple_of(t * 256, 256), 256)
            part = lax.dot_general(dpg_ref[...], w1[slot, rows, :], CONTRACT_LAST, preferred_element_type=jnp.float32)
            part += lax.dot_general(dpu_ref[...], w3[slot, rows, :], CONTRACT_LAST, preferred_element_type=jnp.float32)
            spread = jnp.dot(scat_ref[...], part.astype(jnp.bfloat16), preferred_element_type=jnp.float32)
            dense[k, :, :, rows] = spread.astype(jnp.bfloat16).reshape(ne, tok, 256)

        for j in range(2):
            core_send(k, j).start()

        @pl.when(k + 2 < nz)
        def _():
            for c in again(k + 2, slot):
                c.start()

    def to_x(k):
        for j in range(2):
            core_send(k, j).wait_recv()
        both = dense[k, core + 2 * far].astype(jnp.float32) + cr[k, far].astype(jnp.float32)
        xs[k] = both.astype(jnp.bfloat16)
        x_send(k).start()

    def total(k):
        x_send(k).wait_recv()
        return (
            dense[k, e].astype(jnp.float32) + cr[k, x].astype(jnp.float32) + xr[k].astype(jnp.float32)
        )

    def to_z(k):
        zs[k] = total(k).astype(jnp.bfloat16)
        z_send(k).start()

    @pl.loop(0, nz)
    def _(k):
        multiply(k)

        @pl.when(k >= 1)
        def _():
            to_x(k - 1)

        @pl.when(k == 0)
        def _():
            for j in range(2):
                gate_core(j).wait_recv()
            sxs[...] = sd_ref[core + 2 * far] + scr[far]
            gate_x().start()

        @pl.when(k == 1)
        def _():
            gate_x().wait_recv()
            own_sum = sd_ref[e] + scr[x] + sxr[...]
            szs[...] = own_sum
            szr[z] = own_sum
            for i in range(nz - 1):
                gate_z(i).start()

        @pl.when(k >= 2)
        def _():
            to_z(k - 2)

    to_x(nz - 1)
    to_z(nz - 2)
    acc[...] = total(nz - 1)
    for k in range(nz - 1):
        source = lax.rem(z + 1 + k, nz)
        remote(zs.at[k], zr.at[source], zss.at[k], zrs.at[source], {"hid": source}).wait_recv()
        acc[...] += zr[source].astype(jnp.float32)
        remote(szs, szr.at[source], gzs.at[k], gzr.at[source], {"hid": source}).wait_recv()
    out_ref[...] = acc[...].astype(jnp.bfloat16)
    gate_total = szr[0]
    for q in range(1, nz):
        gate_total += szr[q]
    grad_gate_ref[...] = gate_total

    for j in range(2):
        gate_core(j).wait_send()
    gate_x().wait_send()
    for k in range(nz):
        for j in range(2):
            core_send(k, j).wait_send()
        x_send(k).wait_send()
        if k < nz - 1:
            z_send(k).wait_send()
            gate_z(k).wait_send()

    @pl.loop(0, nz)
    def _(q):
        for a in range(2):
            @pl.when((q <= z) & (z < nz - 1))
            def _():
                up(a, q).wait_send()

            @pl.when((q >= z) & (z > 0))
            def _():
                down(a, q).wait_send()

            over_x(a, q).wait_send()
            to_mate(a, q, e, 0).wait_send()
            to_mate(a, q, across, 1).wait_send()
    gate_send(e, 0, across).wait_send()
    gate_send(e, 1, mate).wait_send()
    gate_send(across, 2, mate).wait_send()


def layer(tokens, grad_out, gates, pick, slots, homes, w_gate, w_up, w_down):
    nz, ne = lax.axis_size("hid"), lax.axis_size("exp")
    tok, width = tokens.shape
    hidden = w_gate.shape[2]
    used = pick.shape[0]
    hbm = pl.BlockSpec(memory_space=pl.ANY)
    vmem = pl.BlockSpec(memory_space=pltpu.VMEM)
    bf16, f32 = jnp.bfloat16, jnp.float32
    dma = pltpu.SemaphoreType.DMA
    return pl.pallas_call(
        functools.partial(layer_kernel, nz, ne, tok, width),
        out_shape=(
            jax.ShapeDtypeStruct((tok, width), bf16),
            jax.ShapeDtypeStruct((tok, 128), f32),
        ),
        in_specs=[hbm, hbm, hbm, vmem, vmem, vmem, vmem, hbm, hbm, hbm],
        out_specs=(vmem, vmem),
        scratch_shapes=[
            pltpu.VMEM((nz, ne, tok, width), bf16),
            pltpu.VMEM((nz, ne, tok, width), bf16),
            pltpu.VMEM((ne, tok, 128), bf16),
            pltpu.VMEM((2, width, hidden), bf16),
            pltpu.VMEM((2, width, hidden), bf16),
            pltpu.VMEM((2, hidden, width), bf16),
            pltpu.VMEM((used, hidden), f32),
            pltpu.VMEM((used, hidden), f32),
            pltpu.VMEM((used, hidden), f32),
            pltpu.VMEM((used, hidden), bf16),
            pltpu.VMEM((used, hidden), bf16),
            pltpu.VMEM((used, 128), f32),
            pltpu.VMEM((ne, tok, 128), f32),
            pltpu.VMEM((nz, ne, tok, width), bf16),
            pltpu.VMEM((nz, 2, tok, width), bf16),
            pltpu.VMEM((nz, tok, width), bf16),
            pltpu.VMEM((nz, tok, width), bf16),
            pltpu.VMEM((nz, tok, width), bf16),
            pltpu.VMEM((nz, tok, width), bf16),
            pltpu.VMEM((tok, width), f32),
            pltpu.VMEM((2, tok, 128), f32),
            pltpu.VMEM((tok, 128), f32),
            pltpu.VMEM((tok, 128), f32),
            pltpu.VMEM((tok, 128), f32),
            pltpu.VMEM((nz, tok, 128), f32),
            dma((2, nz)),
            dma((2, nz)),
            dma((2, nz)),
            dma((2, nz, 2)),
            dma((2, nz, ne)),
            dma((3,)),
            dma((ne,)),
            dma((2, 3)),
            dma((3,)),
            dma((nz, 2)),
            dma((nz, 2)),
            dma((nz,)),
            dma((nz,)),
            dma((nz,)),
            dma((nz,)),
            dma((2,)),
            dma((2,)),
            dma((1,)),
            dma((1,)),
            dma((nz,)),
            dma((nz,)),
        ],
        compiler_params=pltpu.CompilerParams(
            collective_id=0, has_side_effects=True, vmem_limit_bytes=60 * 1024 * 1024
        ),
        name="layer",
    )(tokens, grad_out, gates, pick, slots, homes, pick.T, w_gate, w_up, w_down)


def fast_local(tokens, grad_out, gates, block_experts, w_gate, w_up, w_down):
    n_experts = lax.axis_size("exp")
    own_index = lax.axis_index("exp")
    tok_dev, width_dev = tokens.shape
    blocks_all = block_experts.shape[0]
    per_home = tok_dev // BLOCK
    capacity = blocks_all // 2
    used_count = capacity * BLOCK
    list_block, list_slot, live = routing(block_experts, own_index)
    slot_hot = (list_slot[:, None] == jnp.arange(2, dtype=jnp.int32)[None, :]).astype(jnp.float32)
    slot_hot = slot_hot * live[:, None].astype(jnp.float32)
    row = jnp.where(live, list_block * BLOCK, -used_count * n_experts)[:, None] + jnp.arange(BLOCK, dtype=jnp.int32)[None, :]
    row = row.reshape(used_count, 1)
    pick = (row == jnp.arange(blocks_all * BLOCK, dtype=jnp.int32)[None, :]).astype(jnp.bfloat16)
    lane = jnp.arange(128, dtype=jnp.int32)[None, None, :]
    slots = ((list_slot[:, None, None] == lane) & live[:, None, None]).astype(jnp.float32)
    slots = jnp.broadcast_to(slots, (capacity, BLOCK, 128)).reshape(used_count, 128)
    gates_wide = jnp.pad(gates, ((0, 0), (0, 126)))
    homes = ((list_block[:, None, None] == lane) & live[:, None, None]).astype(jnp.float32)
    homes = jnp.broadcast_to(homes, (capacity, BLOCK, 128)).reshape(used_count, 128)
    grad, gate_lanes = layer(tokens, grad_out, gates_wide, pick, slots, homes, w_gate, w_up, w_down)
    return grad, gate_lanes[:, :2]


def combined(owned, score, list_block, live, slot_hot, tok_dev, width_dev, capacity):
    n_experts = lax.axis_size("exp")
    own_index = lax.axis_index("exp")
    per_home = tok_dev // BLOCK
    result_cols = owned.reshape(width_dev, capacity, BLOCK)
    score_blocks = score.reshape(capacity, BLOCK)

    def share(home):
        wanted = home * per_home + jnp.arange(per_home, dtype=jnp.int32)
        select = ((list_block[None, :] == wanted[:, None]) & live[None, :]).astype(jnp.float32)
        grad_part = jnp.einsum("bi,dir->dbr", select, result_cols, precision=HIGHEST).reshape(
            width_dev, tok_dev
        )
        gate_part = jnp.einsum(
            "bi,ik,ir->kbr", select, slot_hot, score_blocks, precision=HIGHEST
        ).reshape(2, tok_dev)
        return (grad_part, gate_part)

    zero_totals = (
        jnp.zeros((width_dev, tok_dev), jnp.float32),
        jnp.zeros((2, tok_dev), jnp.float32),
    )

    def single_turn(step, totals):
        grad_part, gate_part = share((own_index + 1 + step) % n_experts)
        return passed_along((totals[0] + grad_part, totals[1] + gate_part), "exp", -1)

    totals = lax.fori_loop(0, n_experts - 1, single_turn, zero_totals)
    grad_part, gate_part = share(own_index)
    grad_total = totals[0] + grad_part
    gate_total = totals[1] + gate_part
    return (grad_total.T.astype(jnp.bfloat16), gate_total.T)


def local(tokens, grad_out, gates, block_experts, w_gate, w_up, w_down):
    own_index = lax.axis_index("exp")
    tok_dev, width_dev = tokens.shape
    blocks_all = block_experts.shape[0]
    capacity = blocks_all // 2
    used_count = capacity * BLOCK
    list_block, list_slot, live = routing(block_experts, own_index)
    row_index = (list_block[:, None] * BLOCK + jnp.arange(BLOCK, dtype=jnp.int32)[None, :]).reshape(
        used_count
    )
    x_home, dy_home, gate_home = (
        lax.all_gather(tokens, "exp", axis=0, tiled=True),
        lax.all_gather(grad_out, "exp", axis=0, tiled=True),
        lax.all_gather(gates, "exp", axis=0, tiled=True),
    )
    gate_pick = (
        jnp.take(gate_home, row_index, axis=0).astype(jnp.float32).reshape(capacity, BLOCK, 2)
    )
    slot_hot = (list_slot[:, None] == jnp.arange(2, dtype=jnp.int32)[None, :]).astype(jnp.float32)
    slot_hot = slot_hot * live[:, None].astype(jnp.float32)
    gate_column = jnp.sum(gate_pick * slot_hot[:, None, :], axis=2).reshape(used_count)
    x_piece = jnp.take(lax.all_gather(x_home, "hid", axis=1, tiled=True), row_index, axis=0)
    dy_piece = jnp.take(lax.all_gather(dy_home, "hid", axis=1, tiled=True), row_index, axis=0)
    pre_gate = jnp.dot(x_piece, w_gate[0], preferred_element_type=jnp.float32)
    pre_up = jnp.dot(x_piece, w_up[0], preferred_element_type=jnp.float32)
    d_hidden = lax.dot_general(dy_piece, w_down[0], CONTRACT_LAST, preferred_element_type=jnp.float32)
    sigmoid_gate = jax.nn.sigmoid(pre_gate)
    activated = pre_gate * sigmoid_gate
    score_part = jnp.sum(activated * pre_up * d_hidden, axis=1)
    score = lax.psum(score_part, "hid")
    scaled = gate_column[:, None] * d_hidden
    d_pre_gate = (scaled * pre_up * sigmoid_gate * (1.0 + pre_gate * (1.0 - sigmoid_gate))).astype(
        jnp.bfloat16
    )
    d_pre_up = (scaled * activated).astype(jnp.bfloat16)
    first = lax.dot_general(w_gate[0], d_pre_gate, CONTRACT_LAST, preferred_element_type=jnp.float32)
    owned = lax.psum_scatter(
        first
        + lax.dot_general(w_up[0], d_pre_up, CONTRACT_LAST, preferred_element_type=jnp.float32),
        "hid",
        scatter_dimension=0,
        tiled=True,
    )
    return combined(owned, score, list_block, live, slot_hot, tok_dev, width_dev, capacity)


def solution(mesh):
    placed = (
        P(("grp", "exp"), "hid"),
        P(("grp", "exp"), "hid"),
        P(("grp", "exp"), None),
        P("grp", None),
        P("exp", None, "hid"),
        P("exp", None, "hid"),
        P("exp", "hid", None),
    )
    body = fast_local if (mesh.shape["exp"], mesh.shape["hid"]) == (4, 4) else local
    return jax.shard_map(
        body,
        mesh=mesh,
        in_specs=placed,
        out_specs=(P(("grp", "exp"), "hid"), P(("grp", "exp"), None)),
        check_vma=False,
    )
```

```python
import functools
import jax
import jax.numpy as jnp
from jax import lax
from jax.experimental import pallas as pl
from jax.experimental.pallas import tpu as pltpu
from jax.sharding import PartitionSpec as P

BLOCK = 128


HIGHEST = lax.Precision.HIGHEST
CONTRACT_LAST = (((1,), (1,)), ((), ()))
MESH = pl.DeviceIdType.MESH
TILE = 512


def passed_along(block, axis, distance):
    devices = range(lax.axis_size(axis))
    route = [((i - distance) % len(devices), i) for i in devices]
    return lax.ppermute(block, axis, route)


def routing(block_experts, own_index):
    blocks_all = block_experts.shape[0]
    capacity = blocks_all // 2
    matched = block_experts == own_index
    chosen = jnp.any(matched, axis=1)
    slot_of = matched[:, 1].astype(jnp.int32)
    order = jnp.arange(blocks_all, dtype=jnp.int32)
    position = jnp.sum((chosen[None, :] & (order[None, :] < order[:, None])).astype(jnp.int32), axis=1)
    placed = (position[None, :] == jnp.arange(capacity, dtype=jnp.int32)[:, None]) & chosen[None, :]
    placed_int = placed.astype(jnp.int32)
    list_block = jnp.sum(placed_int * jnp.arange(blocks_all, dtype=jnp.int32)[None, :], axis=1)
    list_slot = jnp.sum(placed_int * slot_of[None, :], axis=1)
    live = jnp.any(placed, axis=1)
    return list_block, list_slot, live


def layer_kernel(width, be_ref, tok_ref, dy_ref, gate_ref, w1_ref, w3_ref, w2_ref, out_ref, grad_gate_ref,
                 xb, db, gb, w1, w3, w2, xp, dp, pg, pu, dh, dpg_ref, dpu_ref, gcol, score_ref,
                 dense, cr, xs, xr, zs, ro, ri, sd, sr, szs, szr,
                 s_zi, s_zo, s_x, s_c, s_ex, rsem, wsem, lsem,
                 css, crs, xss, xrs, zss, ros, ris, gs, gr, gcs, gcr, gzs, gzr):
    nz, ne = 4, 4
    z = lax.axis_index("hid")
    e = lax.axis_index("exp")
    core = lax.rem(e, 2)
    side = e // 2
    mate = e + 1 - 2 * core
    across = lax.rem(e + 2, ne)
    mate_across = lax.rem(mate + 2, ne)
    upper = z // 2
    at_end = (z == 0) | (z == nz - 1)
    in_middle = (z == 1) | (z == 2)
    inward = z + 1 - 2 * upper
    outward = z - 1 + 2 * upper
    own_q = z + upper * (nz - 1 - 2 * z)
    bufs = (xb, db)
    own_refs = (tok_ref, dy_ref)
    picks = (xp, dp)
    hidden = w1.shape[2]
    tok = xb.shape[2]
    half = xr.shape[2]

    def real(q):
        return q + upper * (nz - 1 - 2 * q)

    order = (own_q, 1 - own_q, 2, 3)

    def load(ref, buf, j, i, slot):
        rows = pl.ds(pl.multiple_of(real(order[i]) * width, width), width)
        src = ref.at[0, :, rows] if j == 2 else ref.at[0, rows, :]
        return pltpu.make_async_copy(src, buf.at[slot], wsem.at[slot, j])

    def load_x(i, slot):
        return load(w1_ref, w1, 0, i, slot), load(w3_ref, w3, 1, i, slot)

    def load_d(i, slot):
        return load(w2_ref, w2, 2, i, slot)

    def remote(src, dst, ssem, rsem_, dev):
        return pltpu.make_async_remote_copy(
            src_ref=src, dst_ref=dst, send_sem=ssem, recv_sem=rsem_, device_id=dev, device_id_type=MESH)

    def send(a, q, eq, ssem, dev, src=None):
        zq = real(q)
        place = bufs[a].at[zq, eq]
        return remote(place if src is None else src, place, ssem, rsem.at[a, zq, eq], dev)

    def to_in(a, q, n, src=None):
        return send(a, q, e, s_zi.at[a, n], {"hid": inward}, src)

    def to_out(a, q, n, src=None):
        return send(a, q, e, s_zo.at[a, n], {"hid": outward}, src)

    def over_x(a, q, src=None):
        return send(a, q, e, s_x.at[a, real(q)], {"exp": across}, src)

    def to_mate(a, q, eq, k, src=None):
        return send(a, q, eq, s_c.at[a, real(q), k], {"exp": mate}, src)

    def across_in(a):
        return send(a, 0, across, s_ex.at[a], {"hid": inward})

    def across_out(a):
        return send(a, 3, across, s_ex.at[a], {"hid": outward})

    def arrived(a, q, eq):
        send(a, q, eq, s_ex.at[a], {"exp": mate}).wait_recv()

    partners = (mate, across, mate_across)

    def gate_send(k):
        return remote(gb.at[e], gb.at[e], gs.at[k], gr.at[e], {"exp": partners[k]})

    def gate_arrived(k):
        remote(gb.at[partners[k]], gb.at[partners[k]], gs.at[k], gr.at[partners[k]], {"exp": mate}).wait_recv()

    own = (
        pltpu.make_async_copy(tok_ref, xb.at[z, e], lsem.at[0]),
        pltpu.make_async_copy(dy_ref, db.at[z, e], lsem.at[1]),
    )
    for c in own:
        c.start()
    for i in range(2):
        for c in load_x(i, i):
            c.start()
        load_d(i, i).start()

    barrier = pltpu.get_barrier_semaphore()
    for dev in partners:
        pl.semaphore_signal(barrier, inc=1, device_id={"exp": dev}, device_id_type=MESH)
    for k in range(nz - 1):
        pl.semaphore_signal(barrier, inc=1, device_id={"hid": lax.rem(z + 1 + k, nz)}, device_id_type=MESH)
    gb[e] = jnp.concatenate([gate_ref[...].astype(jnp.float32), jnp.zeros((6, tok), jnp.float32)], axis=0)
    pl.semaphore_wait(barrier, nz + 2)

    for a in range(2):
        to_in(a, own_q, 0, own_refs[a]).start()

        @pl.when(in_middle)
        def _():
            to_out(a, own_q, 0, own_refs[a]).start()

        over_x(a, own_q, own_refs[a]).start()
        to_mate(a, own_q, e, 0, own_refs[a]).start()
    for k in range(3):
        gate_send(k).start()

    first, first_slot = jnp.int32(-1), jnp.int32(0)
    last, last_slot = jnp.int32(-1), jnp.int32(0)
    for b in range(ne):
        one, two = be_ref[0, b] == e, be_ref[1, b] == e
        here = one | two
        column = two.astype(jnp.int32)
        fresh = here & (first < 0)
        later = here & (first >= 0)
        last, last_slot = jnp.where(later, b, last), jnp.where(later, column, last_slot)
        first, first_slot = jnp.where(fresh, b, first), jnp.where(fresh, column, first_slot)
    listed = ((first, first_slot), (last, last_slot))
    homes = (e, mate, across, mate_across)
    shares = [[(block == home).astype(jnp.float32) for home in homes] for block, _ in listed]

    def pick(a, i):
        q = order[i]
        arrived(a, q, mate)
        arrived(a, q, mate_across)
        zq = real(q)
        for n, (block, _) in enumerate(listed):
            rows = bufs[a][zq, ne - 1]
            for home in range(ne - 1):
                rows = jnp.where(block == home, bufs[a][zq, home], rows)
            picks[a][n * tok : (n + 1) * tok, :] = rows

    def relay(step, a):
        @pl.when(at_end)
        def _():
            if step < 3:
                arrived(a, step + 1, e)
                if step < 2 or a == 0:
                    over_x(a, step + 1).start()
                to_mate(a, step + 1, e, 0).start()
            arrived(a, step, across)
            if step == 0:
                across_in(a).start()
            to_mate(a, step, across, 1).start()

        if step < 3:
            @pl.when(in_middle)
            def _():
                if step == 0:
                    arrived(a, 2, e)
                    to_out(a, 2, 1).start()
                    over_x(a, 2).start()
                    to_mate(a, 2, e, 0).start()
                    arrived(a, 0, e)
                    to_in(a, 0, 1).start()
                    to_mate(a, 0, e, 0).start()
                    arrived(a, 1, across)
                    to_mate(a, 1, across, 1).start()
                if step == 1:
                    arrived(a, 3, e)
                    to_out(a, 3, 2).start()
                    over_x(a, 3).start()
                    to_mate(a, 3, e, 0).start()
                    arrived(a, 2, across)
                    to_mate(a, 2, across, 1).start()
                    arrived(a, 0, across)
                    to_mate(a, 0, across, 1).start()
                if step == 2:
                    arrived(a, 3, across)
                    if a == 1:
                        across_out(a).start()
                    to_mate(a, 3, across, 1).start()

    def forward_x(i):
        slot = i % 2
        pick(0, i)
        for c in load_x(i, slot):
            c.wait()

        @pl.loop(0, hidden // TILE)
        def _(t):
            cols = pl.ds(pl.multiple_of(t * TILE, TILE), TILE)
            g = jnp.dot(xp[...], w1[slot, :, cols], preferred_element_type=jnp.float32)
            u = jnp.dot(xp[...], w3[slot, :, cols], preferred_element_type=jnp.float32)
            pg[:, cols] = g if i == 0 else pg[:, cols] + g
            pu[:, cols] = u if i == 0 else pu[:, cols] + u

        if i + 2 < nz:
            for c in load_x(i + 2, slot):
                c.start()

    def forward_d(i):
        slot = i % 2
        pick(1, i)
        load_d(i, slot).wait()

        @pl.loop(0, hidden // TILE)
        def _(t):
            cols = pl.ds(pl.multiple_of(t * TILE, TILE), TILE)
            h = lax.dot_general(dp[...], w2[slot, cols, :], CONTRACT_LAST, preferred_element_type=jnp.float32)
            dh[:, cols] = h if i == 0 else dh[:, cols] + h

        if i + 2 < nz:
            load_d(i + 2, slot).start()

    def gate_columns():
        for k in range(3):
            gate_arrived(k)
        eye = lax.broadcasted_iota(jnp.int32, (tok, tok), 0) == lax.broadcasted_iota(jnp.int32, (tok, tok), 1)
        for n, (block, column) in enumerate(listed):
            row = jnp.zeros((1, tok), jnp.float32)
            for home in range(ne):
                for k in range(2):
                    chosen = ((block == home) & (column == k)).astype(jnp.float32)
                    row = row + chosen * gb[home, k : k + 1, :]
            col = jnp.sum(jnp.where(eye, jnp.broadcast_to(row, (tok, tok)), 0.0), axis=1, keepdims=True)
            gcol[n * tok : (n + 1) * tok, :] = jnp.broadcast_to(col, (tok, 128))

    for c in own:
        c.wait()
    score_ref[...] = jnp.zeros_like(score_ref)
    for step in range(3):
        relay(step, 0)
        forward_x(step)
        relay(step, 1)
        forward_d(step)
        if step == 0:
            gate_columns()
    relay(3, 0)
    relay(3, 1)

    WIDE = 256

    def last_dots(t):
        cols = pl.ds(pl.multiple_of(t * WIDE, WIDE), WIDE)
        pg[:, cols] += jnp.dot(xp[...], w1[1, :, cols], preferred_element_type=jnp.float32)
        pu[:, cols] += jnp.dot(xp[...], w3[1, :, cols], preferred_element_type=jnp.float32)
        dh[:, cols] += lax.dot_general(dp[...], w2[1, cols, :], CONTRACT_LAST, preferred_element_type=jnp.float32)

    def pointwise(t):
        for c in range(WIDE // 128):
            cols = pl.ds(pl.multiple_of(t * WIDE + c * 128, 128), 128)
            for r in range(0, 2 * tok, 64):
                rows = pl.ds(r, 64)
                g = pg[rows, cols]
                u = pu[rows, cols]
                h = dh[rows, cols]
                sig = 1.0 / (1.0 + jnp.exp(-g))
                act = g * sig
                score_ref[rows, :] += act * u * h
                scaled = gcol[rows, :] * h
                dpg_ref[rows, cols] = (scaled * u * sig * (1.0 + g * (1.0 - sig))).astype(jnp.bfloat16)
                dpu_ref[rows, cols] = (scaled * act).astype(jnp.bfloat16)

    pick(0, 3)
    pick(1, 3)
    for c in load_x(3, 1):
        c.wait()
    load_d(3, 1).wait()
    last_dots(0)

    @pl.loop(1, hidden // WIDE)
    def _(t):
        pointwise(t - 1)
        last_dots(t)

    pointwise(hidden // WIDE - 1)

    def again(j, slot):
        zq = real(own_q + (3 - j) * (1 - 2 * own_q))
        rows = pl.ds(pl.multiple_of(zq * width, width), width)
        return (
            pltpu.make_async_copy(w1_ref.at[0, rows, :], w1.at[slot], wsem.at[slot, 0]),
            pltpu.make_async_copy(w3_ref.at[0, rows, :], w3.at[slot], wsem.at[slot, 1]),
        )

    def score_send(k):
        return remote(sd.at[k + 1], sr.at[k], gcs.at[k], gcr.at[k], {"exp": partners[k]})

    def gate_z(k):
        return remote(szs, szr.at[z], gzs.at[k], gzr.at[z], {"hid": lax.rem(z + 1 + k, nz)})

    eye = lax.broadcasted_iota(jnp.int32, (tok, tok), 0) == lax.broadcasted_iota(jnp.int32, (tok, tok), 1)
    line = lax.broadcasted_iota(jnp.int32, (8, tok), 0)
    placed = []
    for n, (_, column) in enumerate(listed):
        col = jnp.sum(score_ref[n * tok : (n + 1) * tok, :], axis=1, keepdims=True)
        row = jnp.sum(jnp.where(eye, jnp.broadcast_to(col, (tok, tok)), 0.0), axis=0, keepdims=True)
        placed.append(jnp.where(line == column, jnp.broadcast_to(row, (8, tok)), 0.0))
    for k in range(ne):
        sd[k] = shares[0][k] * placed[0] + shares[1][k] * placed[1]
    for k in range(3):
        score_send(k).start()

    def core_send(k):
        return remote(dense.at[k, 1], cr.at[k], css.at[k], crs.at[k], {"exp": mate})

    def x_send(k):
        return remote(xs.at[k], xr.at[k], xss.at[k], xrs.at[k], {"exp": across})

    def from_end(k):
        return remote(zs.at[k], ro.at[k], zss.at[k], ros.at[k], {"hid": inward})

    def from_middle(k):
        return remote(zs.at[k], ri.at[k], zss.at[k], ris.at[k], {"hid": inward})

    def to_end(k):
        return remote(zs.at[k], ri.at[k], zss.at[k], ris.at[k], {"hid": outward})

    def multiply(k):
        j = k // 2
        slot = lax.rem(j + 1, 2)

        @pl.when((lax.rem(k, 2) == 0) & (j >= 2))
        def _():
            for c in again(j, slot):
                c.wait()

        @pl.loop(0, half // 256)
        def _(t):
            rows = pl.ds(pl.multiple_of(lax.rem(k, 2) * half + t * 256, 256), 256)
            cols = pl.ds(pl.multiple_of(t * 256, 256), 256)
            part = lax.dot_general(dpg_ref[...], w1[slot, rows, :], CONTRACT_LAST, preferred_element_type=jnp.float32)
            part += lax.dot_general(dpu_ref[...], w3[slot, rows, :], CONTRACT_LAST, preferred_element_type=jnp.float32)
            for c in range(2):
                for far in range(2):
                    home = c + 2 * far
                    dense[k, c, far, :, cols] = (
                        shares[0][home] * part[:tok] + shares[1][home] * part[tok:]
                    ).astype(jnp.bfloat16)

        core_send(k).start()

        @pl.when((lax.rem(k, 2) == 1) & (j < 2))
        def _():
            for c in again(j + 2, slot):
                c.start()

    def to_x(k):
        core_send(k).wait_recv()
        both = dense[k, 0, 1].astype(jnp.float32) + cr[k, 1].astype(jnp.float32)
        xs[k] = both.astype(jnp.bfloat16)
        x_send(k).start()

    def total(k):
        x_send(k).wait_recv()
        return dense[k, 0, 0].astype(jnp.float32) + cr[k, 0].astype(jnp.float32) + xr[k].astype(jnp.float32)

    def to_z(k):
        share = total(k)

        @pl.when(at_end)
        def _():
            zs[k] = share.astype(jnp.bfloat16)
            from_end(k).start()

        @pl.when(in_middle & (k < 4))
        def _():
            from_end(k).wait_recv()
            zs[k] = (share + ro[k].astype(jnp.float32)).astype(jnp.bfloat16)
            from_middle(k).start()

        @pl.when(in_middle & (k >= 4))
        def _():
            from_middle(k - 4).wait_recv()
            zs[k] = (share + ri[k - 4].astype(jnp.float32)).astype(jnp.bfloat16)
            to_end(k).start()

    @pl.loop(0, 8)
    def _(k):
        multiply(k)

        @pl.when(k >= 1)
        def _():
            to_x(k - 1)

        @pl.when(k == 2)
        def _():
            mine = sd[0]
            for i in range(3):
                score_send(i).wait_recv()
                mine += sr[i]
            szs[...] = mine
            szr[z] = mine
            for i in range(nz - 1):
                gate_z(i).start()

        @pl.when((k == 4) | (k == 6))
        def _():
            to_z((k - 4) // 2)

    to_x(7)

    @pl.loop(2, 6)
    def _(k):
        to_z(k)

    for k in (6, 7):
        share = total(k)
        cols = pl.ds((k - 6) * half, half)

        @pl.when(at_end)
        def _():
            to_end(k - 2).wait_recv()
            out_ref[:, cols] = (share + ri[k - 2].astype(jnp.float32)).astype(jnp.bfloat16)

        @pl.when(in_middle)
        def _():
            from_end(k - 2).wait_recv()
            from_middle(k - 4).wait_recv()
            out_ref[:, cols] = (
                share + ro[k - 2].astype(jnp.float32) + ri[k - 4].astype(jnp.float32)
            ).astype(jnp.bfloat16)

    for k in range(nz - 1):
        source = lax.rem(z + 1 + k, nz)
        remote(szs, szr.at[source], gzs.at[k], gzr.at[source], {"hid": source}).wait_recv()
    gate_total = szr[0]
    for q in range(1, nz):
        gate_total += szr[q]
    grad_gate_ref[...] = gate_total[:2]

    for k in range(3):
        gate_send(k).wait_send()
        score_send(k).wait_send()
        gate_z(k).wait_send()

    @pl.loop(0, 8)
    def _(k):
        core_send(k).wait_send()
        x_send(k).wait_send()

        @pl.when(k < 6)
        def _():
            from_end(k).wait_send()

    for a in range(2):
        to_in(a, own_q, 0).wait_send()

        @pl.when(at_end)
        def _():
            across_in(a).wait_send()
            for q in range(4):
                if q < 3 or a == 0:
                    over_x(a, q).wait_send()

        @pl.when(in_middle)
        def _():
            to_in(a, 0, 1).wait_send()
            for q in range(1, 4):
                to_out(a, q, q - 1).wait_send()
                over_x(a, q).wait_send()
            if a == 1:
                across_out(a).wait_send()

        for q in range(4):
            to_mate(a, q, e, 0).wait_send()
            to_mate(a, q, across, 1).wait_send()


def layer(block_experts, tokens, grad_out, gates, w_gate, w_up, w_down):
    nz, ne = 4, 4
    tok, width = tokens.shape
    hidden = w_gate.shape[2]
    used = 2 * BLOCK
    half = width // 2
    hbm = pl.BlockSpec(memory_space=pl.ANY)
    vmem = pl.BlockSpec(memory_space=pltpu.VMEM)
    smem = pl.BlockSpec(memory_space=pltpu.SMEM)
    bf16, f32 = jnp.bfloat16, jnp.float32
    dma = pltpu.SemaphoreType.DMA
    return pl.pallas_call(
        functools.partial(layer_kernel, width),
        out_shape=(
            jax.ShapeDtypeStruct((tok, width), bf16),
            jax.ShapeDtypeStruct((2, tok), f32),
        ),
        in_specs=[smem, hbm, hbm, vmem, hbm, hbm, hbm],
        out_specs=(vmem, vmem),
        scratch_shapes=[
            pltpu.VMEM((nz, ne, tok, width), bf16),
            pltpu.VMEM((nz, ne, tok, width), bf16),
            pltpu.VMEM((ne, 8, tok), f32),
            pltpu.VMEM((2, width, hidden), bf16),
            pltpu.VMEM((2, width, hidden), bf16),
            pltpu.VMEM((2, hidden, width), bf16),
            pltpu.VMEM((used, width), bf16),
            pltpu.VMEM((used, width), bf16),
            pltpu.VMEM((used, hidden), f32),
            pltpu.VMEM((used, hidden), f32),
            pltpu.VMEM((used, hidden), f32),
            pltpu.VMEM((used, hidden), bf16),
            pltpu.VMEM((used, hidden), bf16),
            pltpu.VMEM((used, 128), f32),
            pltpu.VMEM((used, 128), f32),
            pltpu.VMEM((8, 2, 2, tok, half), bf16),
            pltpu.VMEM((8, 2, tok, half), bf16),
            pltpu.VMEM((8, tok, half), bf16),
            pltpu.VMEM((8, tok, half), bf16),
            pltpu.VMEM((6, tok, half), bf16),
            pltpu.VMEM((6, tok, half), bf16),
            pltpu.VMEM((6, tok, half), bf16),
            pltpu.VMEM((ne, 8, tok), f32),
            pltpu.VMEM((3, 8, tok), f32),
            pltpu.VMEM((8, tok), f32),
            pltpu.VMEM((nz, 8, tok), f32),
            dma((2, 2)),
            dma((2, 3)),
            dma((2, nz)),
            dma((2, nz, 2)),
            dma((2,)),
            dma((2, nz, ne)),
            dma((2, 3)),
            dma((2,)),
            dma((8,)),
            dma((8,)),
            dma((8,)),
            dma((8,)),
            dma((6,)),
            dma((6,)),
            dma((6,)),
            dma((3,)),
            dma((ne,)),
            dma((3,)),
            dma((3,)),
            dma((3,)),
            dma((nz,)),
        ],
        compiler_params=pltpu.CompilerParams(
            collective_id=0, has_side_effects=True, vmem_limit_bytes=60 * 1024 * 1024
        ),
        name="layer",
    )(block_experts, tokens, grad_out, gates, w_gate, w_up, w_down)


def fast_local(tokens, grad_out, gates, block_experts, w_gate, w_up, w_down):
    grad, gate_rows = layer(block_experts.T, tokens, grad_out, gates.T, w_gate, w_up, w_down)
    return grad, gate_rows.T


def combined(owned, score, list_block, live, slot_hot, tok_dev, width_dev, capacity):
    n_experts = lax.axis_size("exp")
    own_index = lax.axis_index("exp")
    per_home = tok_dev // BLOCK
    result_cols = owned.reshape(width_dev, capacity, BLOCK)
    score_blocks = score.reshape(capacity, BLOCK)

    def share(home):
        wanted = home * per_home + jnp.arange(per_home, dtype=jnp.int32)
        select = ((list_block[None, :] == wanted[:, None]) & live[None, :]).astype(jnp.float32)
        grad_part = jnp.einsum("bi,dir->dbr", select, result_cols, precision=HIGHEST).reshape(
            width_dev, tok_dev
        )
        gate_part = jnp.einsum(
            "bi,ik,ir->kbr", select, slot_hot, score_blocks, precision=HIGHEST
        ).reshape(2, tok_dev)
        return (grad_part, gate_part)

    zero_totals = (
        jnp.zeros((width_dev, tok_dev), jnp.float32),
        jnp.zeros((2, tok_dev), jnp.float32),
    )

    def single_turn(step, totals):
        grad_part, gate_part = share((own_index + 1 + step) % n_experts)
        return passed_along((totals[0] + grad_part, totals[1] + gate_part), "exp", -1)

    totals = lax.fori_loop(0, n_experts - 1, single_turn, zero_totals)
    grad_part, gate_part = share(own_index)
    grad_total = totals[0] + grad_part
    gate_total = totals[1] + gate_part
    return (grad_total.T.astype(jnp.bfloat16), gate_total.T)


def local(tokens, grad_out, gates, block_experts, w_gate, w_up, w_down):
    own_index = lax.axis_index("exp")
    tok_dev, width_dev = tokens.shape
    blocks_all = block_experts.shape[0]
    capacity = blocks_all // 2
    used_count = capacity * BLOCK
    list_block, list_slot, live = routing(block_experts, own_index)
    row_index = (list_block[:, None] * BLOCK + jnp.arange(BLOCK, dtype=jnp.int32)[None, :]).reshape(
        used_count
    )
    x_home, dy_home, gate_home = (
        lax.all_gather(tokens, "exp", axis=0, tiled=True),
        lax.all_gather(grad_out, "exp", axis=0, tiled=True),
        lax.all_gather(gates, "exp", axis=0, tiled=True),
    )
    gate_pick = (
        jnp.take(gate_home, row_index, axis=0).astype(jnp.float32).reshape(capacity, BLOCK, 2)
    )
    slot_hot = (list_slot[:, None] == jnp.arange(2, dtype=jnp.int32)[None, :]).astype(jnp.float32)
    slot_hot = slot_hot * live[:, None].astype(jnp.float32)
    gate_column = jnp.sum(gate_pick * slot_hot[:, None, :], axis=2).reshape(used_count)
    x_piece = jnp.take(lax.all_gather(x_home, "hid", axis=1, tiled=True), row_index, axis=0)
    dy_piece = jnp.take(lax.all_gather(dy_home, "hid", axis=1, tiled=True), row_index, axis=0)
    pre_gate = jnp.dot(x_piece, w_gate[0], preferred_element_type=jnp.float32)
    pre_up = jnp.dot(x_piece, w_up[0], preferred_element_type=jnp.float32)
    d_hidden = lax.dot_general(dy_piece, w_down[0], CONTRACT_LAST, preferred_element_type=jnp.float32)
    sigmoid_gate = jax.nn.sigmoid(pre_gate)
    activated = pre_gate * sigmoid_gate
    score_part = jnp.sum(activated * pre_up * d_hidden, axis=1)
    score = lax.psum(score_part, "hid")
    scaled = gate_column[:, None] * d_hidden
    d_pre_gate = (scaled * pre_up * sigmoid_gate * (1.0 + pre_gate * (1.0 - sigmoid_gate))).astype(
        jnp.bfloat16
    )
    d_pre_up = (scaled * activated).astype(jnp.bfloat16)
    first = lax.dot_general(w_gate[0], d_pre_gate, CONTRACT_LAST, preferred_element_type=jnp.float32)
    owned = lax.psum_scatter(
        first
        + lax.dot_general(w_up[0], d_pre_up, CONTRACT_LAST, preferred_element_type=jnp.float32),
        "hid",
        scatter_dimension=0,
        tiled=True,
    )
    return combined(owned, score, list_block, live, slot_hot, tok_dev, width_dev, capacity)


def solution(mesh):
    placed = (
        P(("grp", "exp"), "hid"),
        P(("grp", "exp"), "hid"),
        P(("grp", "exp"), None),
        P("grp", None),
        P("exp", None, "hid"),
        P("exp", None, "hid"),
        P("exp", "hid", None),
    )
    body = fast_local if (mesh.shape["exp"], mesh.shape["hid"]) == (4, 4) else local
    return jax.shard_map(
        body,
        mesh=mesh,
        in_specs=placed,
        out_specs=(P(("grp", "exp"), "hid"), P(("grp", "exp"), None)),
        check_vma=False,
    )
```

```python
import functools
import jax
import jax.numpy as jnp
from jax import lax
from jax.experimental import pallas as pl
from jax.experimental.pallas import tpu as pltpu
from jax.sharding import PartitionSpec as P

BLOCK = 128


HIGHEST = lax.Precision.HIGHEST
CONTRACT_LAST = (((1,), (1,)), ((), ()))
MESH = pl.DeviceIdType.MESH
TILE = 512


def passed_along(block, axis, distance):
    devices = range(lax.axis_size(axis))
    route = [((i - distance) % len(devices), i) for i in devices]
    return lax.ppermute(block, axis, route)


def routing(block_experts, own_index):
    blocks_all = block_experts.shape[0]
    capacity = blocks_all // 2
    matched = block_experts == own_index
    chosen = jnp.any(matched, axis=1)
    slot_of = matched[:, 1].astype(jnp.int32)
    order = jnp.arange(blocks_all, dtype=jnp.int32)
    position = jnp.sum((chosen[None, :] & (order[None, :] < order[:, None])).astype(jnp.int32), axis=1)
    placed = (position[None, :] == jnp.arange(capacity, dtype=jnp.int32)[:, None]) & chosen[None, :]
    placed_int = placed.astype(jnp.int32)
    list_block = jnp.sum(placed_int * jnp.arange(blocks_all, dtype=jnp.int32)[None, :], axis=1)
    list_slot = jnp.sum(placed_int * slot_of[None, :], axis=1)
    live = jnp.any(placed, axis=1)
    return list_block, list_slot, live


def layer_kernel(width, be_ref, tok_ref, dy_ref, gate_ref, w1_ref, w3_ref, w2_ref, out_ref, grad_gate_ref,
                 xb, db, gb, w1, w3, w2, xp, dp, pg, pu, dh, dpg_ref, dpu_ref, gcol, score_ref,
                 dense, cr, xs, xr, zs, ro, ri, sd, sr, szs, szr,
                 s_zi, s_zo, s_x, s_c, s_ex, s_xh, s_ch, rsem, hsem, wsem, lsem,
                 css, crs, xss, xrs, zss, ros, ris, gs, gr, gcs, gcr, gzs, gzr):
    nz, ne = 4, 4
    z = lax.axis_index("hid")
    e = lax.axis_index("exp")
    core = lax.rem(e, 2)
    side = e // 2
    mate = e + 1 - 2 * core
    across = lax.rem(e + 2, ne)
    mate_across = lax.rem(mate + 2, ne)
    upper = z // 2
    at_end = (z == 0) | (z == nz - 1)
    in_middle = (z == 1) | (z == 2)
    inward = z + 1 - 2 * upper
    outward = z - 1 + 2 * upper
    own_q = z + upper * (nz - 1 - 2 * z)
    bufs = (xb, db)
    own_refs = (tok_ref, dy_ref)
    picks = (xp, dp)
    hidden = w1.shape[2]
    tok = xb.shape[2]
    half = xr.shape[2]

    def real(q):
        return q + upper * (nz - 1 - 2 * q)

    order = (own_q, 1 - own_q, 2, 3)

    def load(ref, buf, j, i, slot):
        rows = pl.ds(pl.multiple_of(real(order[i]) * width, width), width)
        src = ref.at[0, :, rows] if j == 2 else ref.at[0, rows, :]
        return pltpu.make_async_copy(src, buf.at[slot], wsem.at[slot, j])

    def load_x(i, slot):
        return load(w1_ref, w1, 0, i, slot), load(w3_ref, w3, 1, i, slot)

    def load_d(i, slot):
        return load(w2_ref, w2, 2, i, slot)

    def remote(src, dst, ssem, rsem_, dev):
        return pltpu.make_async_remote_copy(
            src_ref=src, dst_ref=dst, send_sem=ssem, recv_sem=rsem_, device_id=dev, device_id_type=MESH)

    def send(a, q, eq, ssem, dev, src=None):
        zq = real(q)
        place = bufs[a].at[zq, eq]
        return remote(place if src is None else src, place, ssem, rsem.at[a, zq, eq], dev)

    def to_in(a, q, n, src=None):
        return send(a, q, e, s_zi.at[a, n], {"hid": inward}, src)

    def to_out(a, q, n, src=None):
        return send(a, q, e, s_zo.at[a, n], {"hid": outward}, src)

    def over_x(a, q, src=None):
        return send(a, q, e, s_x.at[a, real(q)], {"exp": across}, src)

    def to_mate(a, q, eq, k, src=None):
        return send(a, q, eq, s_c.at[a, real(q), k], {"exp": mate}, src)

    def across_in(a):
        return send(a, 0, across, s_ex.at[a], {"hid": inward})

    def part_of(a, q, eq, r):
        return bufs[a].at[real(q), eq, pl.ds(r * (tok // 2), tok // 2)]

    def send_part(a, q, eq, r, ssem, rsem_, dev):
        return remote(part_of(a, q, eq, r), part_of(a, q, eq, r), ssem, rsem_, dev)

    def part_in(a, r):
        return send_part(a, 0, e, r, s_zi.at[a, 1 + r], hsem.at[a, r, 0], {"hid": inward})

    def part_out(a, r):
        return send_part(a, 3, e, r, s_zo.at[a, 2 + r], hsem.at[a, r, 0], {"hid": outward})

    def part_x(a, r):
        return send_part(a, 3, e, r, s_xh.at[a, r], hsem.at[a, r, 1], {"exp": across})

    def part_mate(a, r):
        return send_part(a, 3, across, r, s_ch.at[a, r], rsem.at[a, real(3), across], {"exp": mate})

    def across_out(a):
        return send_part(a, 3, across, 1, s_ex.at[a], hsem.at[a, 1, 1], {"hid": outward})

    def part_arrived(a, r, c):
        send_part(a, 3, across if c else e, r, s_ex.at[a], hsem.at[a, r, c], {"exp": mate}).wait_recv()

    def arrived(a, q, eq):
        send(a, q, eq, s_ex.at[a], {"exp": mate}).wait_recv()

    partners = (mate, across, mate_across)

    def gate_send(k):
        return remote(gb.at[e], gb.at[e], gs.at[k], gr.at[e], {"exp": partners[k]})

    def gate_arrived(k):
        remote(gb.at[partners[k]], gb.at[partners[k]], gs.at[k], gr.at[partners[k]], {"exp": mate}).wait_recv()

    own = (
        pltpu.make_async_copy(tok_ref, xb.at[z, e], lsem.at[0]),
        pltpu.make_async_copy(dy_ref, db.at[z, e], lsem.at[1]),
    )
    for c in own:
        c.start()
    for i in range(2):
        for c in load_x(i, i):
            c.start()
        load_d(i, i).start()

    barrier = pltpu.get_barrier_semaphore()
    for dev in partners:
        pl.semaphore_signal(barrier, inc=1, device_id={"exp": dev}, device_id_type=MESH)
    for k in range(nz - 1):
        pl.semaphore_signal(barrier, inc=1, device_id={"hid": lax.rem(z + 1 + k, nz)}, device_id_type=MESH)
    gb[e] = jnp.concatenate([gate_ref[...].astype(jnp.float32), jnp.zeros((6, tok), jnp.float32)], axis=0)
    pl.semaphore_wait(barrier, nz + 2)

    for a in range(2):
        to_in(a, own_q, 0, own_refs[a]).start()

        @pl.when(in_middle)
        def _():
            to_out(a, own_q, 0, own_refs[a]).start()

        over_x(a, own_q, own_refs[a]).start()
        to_mate(a, own_q, e, 0, own_refs[a]).start()
    for k in range(3):
        gate_send(k).start()

    first, first_slot = jnp.int32(-1), jnp.int32(0)
    last, last_slot = jnp.int32(-1), jnp.int32(0)
    for b in range(ne):
        one, two = be_ref[0, b] == e, be_ref[1, b] == e
        here = one | two
        column = two.astype(jnp.int32)
        fresh = here & (first < 0)
        later = here & (first >= 0)
        last, last_slot = jnp.where(later, b, last), jnp.where(later, column, last_slot)
        first, first_slot = jnp.where(fresh, b, first), jnp.where(fresh, column, first_slot)
    listed = ((first, first_slot), (last, last_slot))
    homes = (e, mate, across, mate_across)
    shares = [[(block == home).astype(jnp.float32) for home in homes] for block, _ in listed]

    def pick(a, i):
        q = order[i]
        arrived(a, q, mate)
        arrived(a, q, mate_across)
        zq = real(q)
        for n, (block, _) in enumerate(listed):
            rows = bufs[a][zq, ne - 1]
            for home in range(ne - 1):
                rows = jnp.where(block == home, bufs[a][zq, home], rows)
            picks[a][n * tok : (n + 1) * tok, :] = rows

    def relay(step, a):
        @pl.when(at_end)
        def _():
            if step < 2:
                arrived(a, step + 1, e)
                over_x(a, step + 1).start()
                to_mate(a, step + 1, e, 0).start()
            if step == 2:
                part_arrived(a, 0, 0)
                part_x(a, 0).start()
            if step < 3:
                arrived(a, step, across)
                if step == 0:
                    across_in(a).start()
                to_mate(a, step, across, 1).start()
            if step == 2:
                part_arrived(a, 1, 0)
                to_mate(a, 3, e, 0).start()
            if step == 3:
                for r in range(2):
                    part_arrived(a, r, 1)
                    part_mate(a, r).start()

        if step < 3:
            @pl.when(in_middle)
            def _():
                if step == 0:
                    arrived(a, 0, e)
                    for r in range(2):
                        part_in(a, r).start()
                    to_mate(a, 0, e, 0).start()
                    arrived(a, 2, e)
                    to_out(a, 2, 1).start()
                    over_x(a, 2).start()
                    to_mate(a, 2, e, 0).start()
                    arrived(a, 1, across)
                    to_mate(a, 1, across, 1).start()
                if step == 1:
                    for r in range(2):
                        part_arrived(a, r, 0)
                        part_out(a, r).start()
                        part_x(a, r).start()
                    to_mate(a, 3, e, 0).start()
                    arrived(a, 2, across)
                    to_mate(a, 2, across, 1).start()
                    arrived(a, 0, across)
                    to_mate(a, 0, across, 1).start()
                if step == 2:
                    for r in range(2):
                        part_arrived(a, r, 1)
                    across_out(a).start()
                    to_mate(a, 3, across, 1).start()

    def forward_x(i):
        slot = i % 2
        pick(0, i)
        for c in load_x(i, slot):
            c.wait()

        @pl.loop(0, hidden // TILE)
        def _(t):
            cols = pl.ds(pl.multiple_of(t * TILE, TILE), TILE)
            g = jnp.dot(xp[...], w1[slot, :, cols], preferred_element_type=jnp.float32)
            u = jnp.dot(xp[...], w3[slot, :, cols], preferred_element_type=jnp.float32)
            pg[:, cols] = g if i == 0 else pg[:, cols] + g
            pu[:, cols] = u if i == 0 else pu[:, cols] + u

        if i + 2 < nz:
            for c in load_x(i + 2, slot):
                c.start()

    def forward_d(i):
        slot = i % 2
        pick(1, i)
        load_d(i, slot).wait()

        @pl.loop(0, hidden // TILE)
        def _(t):
            cols = pl.ds(pl.multiple_of(t * TILE, TILE), TILE)
            h = lax.dot_general(dp[...], w2[slot, cols, :], CONTRACT_LAST, preferred_element_type=jnp.float32)
            dh[:, cols] = h if i == 0 else dh[:, cols] + h

        if i + 2 < nz:
            load_d(i + 2, slot).start()

    def gate_columns():
        for k in range(3):
            gate_arrived(k)
        eye = lax.broadcasted_iota(jnp.int32, (tok, tok), 0) == lax.broadcasted_iota(jnp.int32, (tok, tok), 1)
        for n, (block, column) in enumerate(listed):
            row = jnp.zeros((1, tok), jnp.float32)
            for home in range(ne):
                for k in range(2):
                    chosen = ((block == home) & (column == k)).astype(jnp.float32)
                    row = row + chosen * gb[home, k : k + 1, :]
            col = jnp.sum(jnp.where(eye, jnp.broadcast_to(row, (tok, tok)), 0.0), axis=1, keepdims=True)
            gcol[n * tok : (n + 1) * tok, :] = jnp.broadcast_to(col, (tok, 128))

    for c in own:
        c.wait()
    score_ref[...] = jnp.zeros_like(score_ref)
    for step in range(3):
        relay(step, 0)
        forward_x(step)
        relay(step, 1)
        forward_d(step)
        if step == 0:
            gate_columns()

    WIDE = 256

    def last_dots(t):
        cols = pl.ds(pl.multiple_of(t * WIDE, WIDE), WIDE)
        dh[:, cols] += lax.dot_general(dp[...], w2[1, cols, :], CONTRACT_LAST, preferred_element_type=jnp.float32)

    def pointwise(t):
        for c in range(WIDE // 128):
            cols = pl.ds(pl.multiple_of(t * WIDE + c * 128, 128), 128)
            for r in range(0, 2 * tok, 64):
                rows = pl.ds(r, 64)
                g = pg[rows, cols]
                u = pu[rows, cols]
                h = dh[rows, cols]
                sig = 1.0 / (1.0 + jnp.exp(-g))
                act = g * sig
                score_ref[rows, :] += act * u * h
                scaled = gcol[rows, :] * h
                dpg_ref[rows, cols] = (scaled * u * sig * (1.0 + g * (1.0 - sig))).astype(jnp.bfloat16)
                dpu_ref[rows, cols] = (scaled * act).astype(jnp.bfloat16)

    def last_x(t):
        cols = pl.ds(pl.multiple_of(t * TILE, TILE), TILE)
        pg[:, cols] += jnp.dot(xp[...], w1[1, :, cols], preferred_element_type=jnp.float32)
        pu[:, cols] += jnp.dot(xp[...], w3[1, :, cols], preferred_element_type=jnp.float32)

    relay(3, 0)
    pick(0, 3)
    for c in load_x(3, 1):
        c.wait()
    pl.loop(0, hidden // TILE // 2)(last_x)
    relay(3, 1)
    pl.loop(hidden // TILE // 2, hidden // TILE)(last_x)
    pick(1, 3)
    load_d(3, 1).wait()
    last_dots(0)

    @pl.loop(1, hidden // WIDE)
    def _(t):
        pointwise(t - 1)
        last_dots(t)

    pointwise(hidden // WIDE - 1)

    def again(j, slot):
        zq = real(own_q + (3 - j) * (1 - 2 * own_q))
        rows = pl.ds(pl.multiple_of(zq * width, width), width)
        return (
            pltpu.make_async_copy(w1_ref.at[0, rows, :], w1.at[slot], wsem.at[slot, 0]),
            pltpu.make_async_copy(w3_ref.at[0, rows, :], w3.at[slot], wsem.at[slot, 1]),
        )

    def score_send(k):
        return remote(sd.at[k + 1], sr.at[k], gcs.at[k], gcr.at[k], {"exp": partners[k]})

    def gate_z(k):
        return remote(szs, szr.at[z], gzs.at[k], gzr.at[z], {"hid": lax.rem(z + 1 + k, nz)})

    eye = lax.broadcasted_iota(jnp.int32, (tok, tok), 0) == lax.broadcasted_iota(jnp.int32, (tok, tok), 1)
    line = lax.broadcasted_iota(jnp.int32, (8, tok), 0)
    placed = []
    for n, (_, column) in enumerate(listed):
        col = jnp.sum(score_ref[n * tok : (n + 1) * tok, :], axis=1, keepdims=True)
        row = jnp.sum(jnp.where(eye, jnp.broadcast_to(col, (tok, tok)), 0.0), axis=0, keepdims=True)
        placed.append(jnp.where(line == column, jnp.broadcast_to(row, (8, tok)), 0.0))
    for k in range(ne):
        sd[k] = shares[0][k] * placed[0] + shares[1][k] * placed[1]
    for k in range(3):
        score_send(k).start()

    def core_send(k):
        return remote(dense.at[k, 1], cr.at[k], css.at[k], crs.at[k], {"exp": mate})

    def x_send(k):
        return remote(xs.at[k], xr.at[k], xss.at[k], xrs.at[k], {"exp": across})

    def from_end(k):
        return remote(zs.at[k], ro.at[k], zss.at[k], ros.at[k], {"hid": inward})

    def from_middle(k):
        return remote(zs.at[k], ri.at[k], zss.at[k], ris.at[k], {"hid": inward})

    def to_end(k):
        return remote(zs.at[k], ri.at[k], zss.at[k], ris.at[k], {"hid": outward})

    def multiply(k):
        j = k // 2
        slot = lax.rem(j + 1, 2)

        @pl.when((lax.rem(k, 2) == 0) & (j >= 2))
        def _():
            for c in again(j, slot):
                c.wait()

        @pl.loop(0, half // 256)
        def _(t):
            rows = pl.ds(pl.multiple_of(lax.rem(k, 2) * half + t * 256, 256), 256)
            cols = pl.ds(pl.multiple_of(t * 256, 256), 256)
            part = lax.dot_general(dpg_ref[...], w1[slot, rows, :], CONTRACT_LAST, preferred_element_type=jnp.float32)
            part += lax.dot_general(dpu_ref[...], w3[slot, rows, :], CONTRACT_LAST, preferred_element_type=jnp.float32)
            for c in range(2):
                for far in range(2):
                    home = c + 2 * far
                    dense[k, c, far, :, cols] = (
                        shares[0][home] * part[:tok] + shares[1][home] * part[tok:]
                    ).astype(jnp.bfloat16)

        core_send(k).start()

        @pl.when((lax.rem(k, 2) == 1) & (j < 2))
        def _():
            for c in again(j + 2, slot):
                c.start()

    def to_x(k):
        core_send(k).wait_recv()
        both = dense[k, 0, 1].astype(jnp.float32) + cr[k, 1].astype(jnp.float32)
        xs[k] = both.astype(jnp.bfloat16)
        x_send(k).start()

    def total(k):
        x_send(k).wait_recv()
        return dense[k, 0, 0].astype(jnp.float32) + cr[k, 0].astype(jnp.float32) + xr[k].astype(jnp.float32)

    def to_z(k):
        share = total(k)

        @pl.when(at_end)
        def _():
            zs[k] = share.astype(jnp.bfloat16)
            from_end(k).start()

        @pl.when(in_middle & (k < 4))
        def _():
            from_end(k).wait_recv()
            zs[k] = (share + ro[k].astype(jnp.float32)).astype(jnp.bfloat16)
            from_middle(k).start()

        @pl.when(in_middle & (k >= 4))
        def _():
            from_middle(k - 4).wait_recv()
            zs[k] = (share + ri[k - 4].astype(jnp.float32)).astype(jnp.bfloat16)
            to_end(k).start()

    @pl.loop(0, 8)
    def _(k):
        multiply(k)

        @pl.when(k >= 1)
        def _():
            to_x(k - 1)

        @pl.when(k == 2)
        def _():
            mine = sd[0]
            for i in range(3):
                score_send(i).wait_recv()
                mine += sr[i]
            szs[...] = mine
            szr[z] = mine
            for i in range(nz - 1):
                gate_z(i).start()

        @pl.when((k == 4) | (k == 6))
        def _():
            to_z((k - 4) // 2)

    to_x(7)

    @pl.loop(2, 6)
    def _(k):
        to_z(k)

    for k in (6, 7):
        share = total(k)
        cols = pl.ds((k - 6) * half, half)

        @pl.when(at_end)
        def _():
            to_end(k - 2).wait_recv()
            out_ref[:, cols] = (share + ri[k - 2].astype(jnp.float32)).astype(jnp.bfloat16)

        @pl.when(in_middle)
        def _():
            from_end(k - 2).wait_recv()
            from_middle(k - 4).wait_recv()
            out_ref[:, cols] = (
                share + ro[k - 2].astype(jnp.float32) + ri[k - 4].astype(jnp.float32)
            ).astype(jnp.bfloat16)

    for k in range(nz - 1):
        source = lax.rem(z + 1 + k, nz)
        remote(szs, szr.at[source], gzs.at[k], gzr.at[source], {"hid": source}).wait_recv()
    gate_total = szr[0]
    for q in range(1, nz):
        gate_total += szr[q]
    grad_gate_ref[...] = gate_total[:2]

    for k in range(3):
        gate_send(k).wait_send()
        score_send(k).wait_send()
        gate_z(k).wait_send()

    @pl.loop(0, 8)
    def _(k):
        core_send(k).wait_send()
        x_send(k).wait_send()

        @pl.when(k < 6)
        def _():
            from_end(k).wait_send()

    for a in range(2):
        to_in(a, own_q, 0).wait_send()

        @pl.when(at_end)
        def _():
            across_in(a).wait_send()
            for q in range(3):
                over_x(a, q).wait_send()
                to_mate(a, q, across, 1).wait_send()
            part_x(a, 0).wait_send()
            for r in range(2):
                part_mate(a, r).wait_send()

        @pl.when(in_middle)
        def _():
            to_out(a, 1, 0).wait_send()
            to_out(a, 2, 1).wait_send()
            over_x(a, 1).wait_send()
            over_x(a, 2).wait_send()
            for r in range(2):
                part_in(a, r).wait_send()
                part_out(a, r).wait_send()
                part_x(a, r).wait_send()
            across_out(a).wait_send()
            for q in range(4):
                to_mate(a, q, across, 1).wait_send()

        for q in range(4):
            to_mate(a, q, e, 0).wait_send()


def layer(block_experts, tokens, grad_out, gates, w_gate, w_up, w_down):
    nz, ne = 4, 4
    tok, width = tokens.shape
    hidden = w_gate.shape[2]
    used = 2 * BLOCK
    half = width // 2
    hbm = pl.BlockSpec(memory_space=pl.ANY)
    vmem = pl.BlockSpec(memory_space=pltpu.VMEM)
    smem = pl.BlockSpec(memory_space=pltpu.SMEM)
    bf16, f32 = jnp.bfloat16, jnp.float32
    dma = pltpu.SemaphoreType.DMA
    return pl.pallas_call(
        functools.partial(layer_kernel, width),
        out_shape=(
            pltpu.VMEM((tok, width), bf16),
            pltpu.VMEM((2, tok), f32),
        ),
        in_specs=[smem, hbm, hbm, vmem, hbm, hbm, hbm],
        out_specs=(vmem, vmem),
        scratch_shapes=[
            pltpu.VMEM((nz, ne, tok, width), bf16),
            pltpu.VMEM((nz, ne, tok, width), bf16),
            pltpu.VMEM((ne, 8, tok), f32),
            pltpu.VMEM((2, width, hidden), bf16),
            pltpu.VMEM((2, width, hidden), bf16),
            pltpu.VMEM((2, hidden, width), bf16),
            pltpu.VMEM((used, width), bf16),
            pltpu.VMEM((used, width), bf16),
            pltpu.VMEM((used, hidden), f32),
            pltpu.VMEM((used, hidden), f32),
            pltpu.VMEM((used, hidden), f32),
            pltpu.VMEM((used, hidden), bf16),
            pltpu.VMEM((used, hidden), bf16),
            pltpu.VMEM((used, 128), f32),
            pltpu.VMEM((used, 128), f32),
            pltpu.VMEM((8, 2, 2, tok, half), bf16),
            pltpu.VMEM((8, 2, tok, half), bf16),
            pltpu.VMEM((8, tok, half), bf16),
            pltpu.VMEM((8, tok, half), bf16),
            pltpu.VMEM((6, tok, half), bf16),
            pltpu.VMEM((6, tok, half), bf16),
            pltpu.VMEM((6, tok, half), bf16),
            pltpu.VMEM((ne, 8, tok), f32),
            pltpu.VMEM((3, 8, tok), f32),
            pltpu.VMEM((8, tok), f32),
            pltpu.VMEM((nz, 8, tok), f32),
            dma((2, 3)),
            dma((2, 4)),
            dma((2, nz)),
            dma((2, nz, 2)),
            dma((2,)),
            dma((2, 2)),
            dma((2, 2)),
            dma((2, nz, ne)),
            dma((2, 2, 2)),
            dma((2, 3)),
            dma((2,)),
            dma((8,)),
            dma((8,)),
            dma((8,)),
            dma((8,)),
            dma((6,)),
            dma((6,)),
            dma((6,)),
            dma((3,)),
            dma((ne,)),
            dma((3,)),
            dma((3,)),
            dma((3,)),
            dma((nz,)),
        ],
        compiler_params=pltpu.CompilerParams(
            collective_id=0, has_side_effects=True, vmem_limit_bytes=60 * 1024 * 1024
        ),
        name="layer",
    )(block_experts, tokens, grad_out, gates, w_gate, w_up, w_down)


def finish_kernel(grad_ref, gate_ref, grad_out_ref, gate_out_ref, sems):
    copies = (
        pltpu.make_async_copy(grad_ref, grad_out_ref, sems.at[0]),
        pltpu.make_async_copy(gate_ref, gate_out_ref, sems.at[1]),
    )
    for c in copies:
        c.start()
    for c in copies:
        c.wait()


def finish(grad, gate_rows):
    vmem = pl.BlockSpec(memory_space=pltpu.VMEM)
    hbm = pl.BlockSpec(memory_space=pl.ANY)
    return pl.pallas_call(
        finish_kernel,
        out_shape=(
            jax.ShapeDtypeStruct(grad.shape, grad.dtype),
            jax.ShapeDtypeStruct(gate_rows.shape, gate_rows.dtype),
        ),
        in_specs=[vmem, vmem],
        out_specs=(hbm, hbm),
        scratch_shapes=[pltpu.SemaphoreType.DMA((2,))],
        compiler_params=pltpu.CompilerParams(vmem_limit_bytes=1024 * 1024),
        name="finish",
    )(grad, gate_rows)


def fast_local(tokens, grad_out, gates, block_experts, w_gate, w_up, w_down):
    grad, gate_rows = layer(block_experts.T, tokens, grad_out, gates.T, w_gate, w_up, w_down)
    grad, gate_rows = finish(grad, gate_rows)
    return grad, gate_rows.T


def combined(owned, score, list_block, live, slot_hot, tok_dev, width_dev, capacity):
    n_experts = lax.axis_size("exp")
    own_index = lax.axis_index("exp")
    per_home = tok_dev // BLOCK
    result_cols = owned.reshape(width_dev, capacity, BLOCK)
    score_blocks = score.reshape(capacity, BLOCK)

    def share(home):
        wanted = home * per_home + jnp.arange(per_home, dtype=jnp.int32)
        select = ((list_block[None, :] == wanted[:, None]) & live[None, :]).astype(jnp.float32)
        grad_part = jnp.einsum("bi,dir->dbr", select, result_cols, precision=HIGHEST).reshape(
            width_dev, tok_dev
        )
        gate_part = jnp.einsum(
            "bi,ik,ir->kbr", select, slot_hot, score_blocks, precision=HIGHEST
        ).reshape(2, tok_dev)
        return (grad_part, gate_part)

    zero_totals = (
        jnp.zeros((width_dev, tok_dev), jnp.float32),
        jnp.zeros((2, tok_dev), jnp.float32),
    )

    def single_turn(step, totals):
        grad_part, gate_part = share((own_index + 1 + step) % n_experts)
        return passed_along((totals[0] + grad_part, totals[1] + gate_part), "exp", -1)

    totals = lax.fori_loop(0, n_experts - 1, single_turn, zero_totals)
    grad_part, gate_part = share(own_index)
    grad_total = totals[0] + grad_part
    gate_total = totals[1] + gate_part
    return (grad_total.T.astype(jnp.bfloat16), gate_total.T)


def local(tokens, grad_out, gates, block_experts, w_gate, w_up, w_down):
    own_index = lax.axis_index("exp")
    tok_dev, width_dev = tokens.shape
    blocks_all = block_experts.shape[0]
    capacity = blocks_all // 2
    used_count = capacity * BLOCK
    list_block, list_slot, live = routing(block_experts, own_index)
    row_index = (list_block[:, None] * BLOCK + jnp.arange(BLOCK, dtype=jnp.int32)[None, :]).reshape(
        used_count
    )
    x_home, dy_home, gate_home = (
        lax.all_gather(tokens, "exp", axis=0, tiled=True),
        lax.all_gather(grad_out, "exp", axis=0, tiled=True),
        lax.all_gather(gates, "exp", axis=0, tiled=True),
    )
    gate_pick = (
        jnp.take(gate_home, row_index, axis=0).astype(jnp.float32).reshape(capacity, BLOCK, 2)
    )
    slot_hot = (list_slot[:, None] == jnp.arange(2, dtype=jnp.int32)[None, :]).astype(jnp.float32)
    slot_hot = slot_hot * live[:, None].astype(jnp.float32)
    gate_column = jnp.sum(gate_pick * slot_hot[:, None, :], axis=2).reshape(used_count)
    x_piece = jnp.take(lax.all_gather(x_home, "hid", axis=1, tiled=True), row_index, axis=0)
    dy_piece = jnp.take(lax.all_gather(dy_home, "hid", axis=1, tiled=True), row_index, axis=0)
    pre_gate = jnp.dot(x_piece, w_gate[0], preferred_element_type=jnp.float32)
    pre_up = jnp.dot(x_piece, w_up[0], preferred_element_type=jnp.float32)
    d_hidden = lax.dot_general(dy_piece, w_down[0], CONTRACT_LAST, preferred_element_type=jnp.float32)
    sigmoid_gate = jax.nn.sigmoid(pre_gate)
    activated = pre_gate * sigmoid_gate
    score_part = jnp.sum(activated * pre_up * d_hidden, axis=1)
    score = lax.psum(score_part, "hid")
    scaled = gate_column[:, None] * d_hidden
    d_pre_gate = (scaled * pre_up * sigmoid_gate * (1.0 + pre_gate * (1.0 - sigmoid_gate))).astype(
        jnp.bfloat16
    )
    d_pre_up = (scaled * activated).astype(jnp.bfloat16)
    first = lax.dot_general(w_gate[0], d_pre_gate, CONTRACT_LAST, preferred_element_type=jnp.float32)
    owned = lax.psum_scatter(
        first
        + lax.dot_general(w_up[0], d_pre_up, CONTRACT_LAST, preferred_element_type=jnp.float32),
        "hid",
        scatter_dimension=0,
        tiled=True,
    )
    return combined(owned, score, list_block, live, slot_hot, tok_dev, width_dev, capacity)


def solution(mesh):
    placed = (
        P(("grp", "exp"), "hid"),
        P(("grp", "exp"), "hid"),
        P(("grp", "exp"), None),
        P("grp", None),
        P("exp", None, "hid"),
        P("exp", None, "hid"),
        P("exp", "hid", None),
    )
    body = fast_local if (mesh.shape["exp"], mesh.shape["hid"]) == (4, 4) else local
    return jax.shard_map(
        body,
        mesh=mesh,
        in_specs=placed,
        out_specs=(P(("grp", "exp"), "hid"), P(("grp", "exp"), None)),
        check_vma=False,
    )
```

```python
import functools
import jax
import jax.numpy as jnp
from jax import lax
from jax.experimental import pallas as pl
from jax.experimental.pallas import tpu as pltpu
from jax.sharding import PartitionSpec as P

BLOCK = 128


HIGHEST = lax.Precision.HIGHEST
CONTRACT_LAST = (((1,), (1,)), ((), ()))
MESH = pl.DeviceIdType.MESH
TILE = 512


def passed_along(block, axis, distance):
    devices = range(lax.axis_size(axis))
    route = [((i - distance) % len(devices), i) for i in devices]
    return lax.ppermute(block, axis, route)


def routing(block_experts, own_index):
    blocks_all = block_experts.shape[0]
    capacity = blocks_all // 2
    matched = block_experts == own_index
    chosen = jnp.any(matched, axis=1)
    slot_of = matched[:, 1].astype(jnp.int32)
    order = jnp.arange(blocks_all, dtype=jnp.int32)
    position = jnp.sum((chosen[None, :] & (order[None, :] < order[:, None])).astype(jnp.int32), axis=1)
    placed = (position[None, :] == jnp.arange(capacity, dtype=jnp.int32)[:, None]) & chosen[None, :]
    placed_int = placed.astype(jnp.int32)
    list_block = jnp.sum(placed_int * jnp.arange(blocks_all, dtype=jnp.int32)[None, :], axis=1)
    list_slot = jnp.sum(placed_int * slot_of[None, :], axis=1)
    live = jnp.any(placed, axis=1)
    return list_block, list_slot, live


def layer_kernel(width, be_ref, tok_ref, dy_ref, gate_ref, w1_ref, w3_ref, w2_ref, out_ref, grad_gate_ref,
                 xb, db, gb, w1, w3, w2, xp, dp, pg, pu, dh, dpg_ref, dpu_ref, gcol, score_ref,
                 dense, cr, xr, ro, ri, rb, sd, sr, szs, szr,
                 s_zi, s_zo, s_x, s_c, s_ex, s_zih, s_zoh, s_xh, s_ch, rsem, hsem, msem, wsem, lsem,
                 css, crs, xss, xrs, zss, ros, ris, rbs, gs, gr, gcs, gcr, gzs, gzr):
    nz, ne = 4, 4
    z = lax.axis_index("hid")
    e = lax.axis_index("exp")
    core = lax.rem(e, 2)
    mate = e + 1 - 2 * core
    across = lax.rem(e + 2, ne)
    mate_across = lax.rem(mate + 2, ne)
    partners = (mate, across, mate_across)
    upper = z // 2
    at_end = (z == 0) | (z == nz - 1)
    in_middle = (z == 1) | (z == 2)
    inward = z + 1 - 2 * upper
    outward = z - 1 + 2 * upper
    own_q = z + upper * (nz - 1 - 2 * z)
    bufs = (xb, db)
    own_refs = (tok_ref, dy_ref)
    picks = (xp, dp)
    hidden = w1.shape[2]
    tok = xb.shape[2]
    part = tok // 2

    barrier = pltpu.get_barrier_semaphore()
    for dev in partners:
        pl.semaphore_signal(barrier, inc=1, device_id={"exp": dev}, device_id_type=MESH)
    for k in range(nz - 1):
        pl.semaphore_signal(barrier, inc=1, device_id={"hid": lax.rem(z + 1 + k, nz)}, device_id_type=MESH)

    def real(q):
        return q + upper * (nz - 1 - 2 * q)

    order = (own_q, 1 - own_q, 2, 3)

    def load(ref, buf, j, i, slot):
        rows = pl.ds(pl.multiple_of(real(order[i]) * width, width), width)
        src = ref.at[0, :, rows] if j == 2 else ref.at[0, rows, :]
        return pltpu.make_async_copy(src, buf.at[slot], wsem.at[slot, j])

    def load_x(i):
        return load(w1_ref, w1, 0, i, i % 3), load(w3_ref, w3, 1, i, i % 3)

    def load_d(i):
        return load(w2_ref, w2, 2, i, i % 2)

    def remote(src, dst, ssem, rsem_, dev):
        return pltpu.make_async_remote_copy(
            src_ref=src, dst_ref=dst, send_sem=ssem, recv_sem=rsem_, device_id=dev, device_id_type=MESH)

    def send(a, q, eq, ssem, dev, src=None):
        zq = real(q)
        place = bufs[a].at[zq, eq]
        return remote(place if src is None else src, place, ssem, rsem.at[a, zq, eq], dev)

    def to_in(a):
        return send(a, 0, e, s_zi.at[a], {"hid": inward}, own_refs[a])

    def to_out(a):
        return send(a, 1, e, s_zo.at[a], {"hid": outward}, own_refs[a])

    def over_x(a, q, n, src=None):
        return send(a, q, e, s_x.at[a, n], {"exp": across}, src)

    def to_mate(a, q, eq, k, src=None):
        return send(a, q, eq, s_c.at[a, real(q), k], {"exp": mate}, src)

    def across_in(a):
        return send(a, 0, across, s_ex.at[a], {"hid": inward})

    def arrived(a, q, eq):
        send(a, q, eq, s_ex.at[a], {"exp": mate}).wait_recv()

    def send_part(a, q, eq, r, ssem, rsem_, dev, src=None):
        rows = pl.ds(r * part, part)
        place = bufs[a].at[real(q), eq, rows]
        return remote(place if src is None else src.at[rows], place, ssem, rsem_, dev)

    def part_in(q, a, r):
        src = own_refs[a] if q == 1 else None
        n = 1 - q
        return send_part(a, q, e, r, s_zih.at[2 * n + a, r], hsem.at[2 * n + a, r, 0], {"hid": inward}, src)

    def part_out(q, a, r):
        n = 2 * (q - 2) + a
        return send_part(a, q, e, r, s_zoh.at[n, r], hsem.at[n, r, 0], {"hid": outward})

    def part_x(q, a, r):
        n = 2 * (q - 2) + a
        return send_part(a, q, e, r, s_xh.at[n, r], hsem.at[n, r, 1], {"exp": across})

    def part_mate(q, a, r, c):
        n = 2 * (q - 2) + a
        return send_part(a, q, across if c else e, r, s_ch.at[n, r, c], msem.at[n, r, c], {"exp": mate})

    def across_out(a):
        return send_part(a, 2, across, 1, s_ex.at[a], hsem.at[a, 1, 1], {"hid": outward})

    def part_arrived(q, a, r, c):
        n = 2 * (q - 2) + a
        send_part(a, q, across if c else e, r, s_ex.at[a], hsem.at[n, r, c], {"exp": mate}).wait_recv()

    def part_from_mate(q, a, r, c):
        n = 2 * (q - 2) + a
        send_part(a, q, mate_across if c else mate, r, s_ex.at[a], msem.at[n, r, c], {"exp": mate}).wait_recv()

    def gate_send(k):
        return remote(gb.at[e], gb.at[e], gs.at[k], gr.at[e], {"exp": partners[k]})

    def gate_arrived(k):
        remote(gb.at[partners[k]], gb.at[partners[k]], gs.at[k], gr.at[partners[k]], {"exp": mate}).wait_recv()

    own = (
        pltpu.make_async_copy(tok_ref, xb.at[z, e], lsem.at[0]),
        pltpu.make_async_copy(dy_ref, db.at[z, e], lsem.at[1]),
    )
    for c in own:
        c.start()
    for i in range(2):
        for c in load_x(i):
            c.start()
        load_d(i).start()
    for c in load_x(2):
        c.start()
    gb[e] = jnp.concatenate([gate_ref[...].astype(jnp.float32), jnp.zeros((6, tok), jnp.float32)], axis=0)
    pl.semaphore_wait(barrier, nz + 2)

    @pl.when(at_end)
    def _():
        for a in range(2):
            to_in(a).start()

    @pl.when(in_middle)
    def _():
        for r in range(2):
            for a in range(2):
                part_in(1, a, r).start()
        for a in range(2):
            to_out(a).start()

    for a in range(2):
        over_x(a, own_q, 0, own_refs[a]).start()
        to_mate(a, own_q, e, 0, own_refs[a]).start()
    for k in range(3):
        gate_send(k).start()

    first, first_slot = jnp.int32(-1), jnp.int32(0)
    last, last_slot = jnp.int32(-1), jnp.int32(0)
    for b in range(ne):
        one, two = be_ref[0, b] == e, be_ref[1, b] == e
        here = one | two
        column = two.astype(jnp.int32)
        fresh = here & (first < 0)
        later = here & (first >= 0)
        last, last_slot = jnp.where(later, b, last), jnp.where(later, column, last_slot)
        first, first_slot = jnp.where(fresh, b, first), jnp.where(fresh, column, first_slot)
    listed = ((first, first_slot), (last, last_slot))
    homes = (e, mate, across, mate_across)
    shares = [[(block == home).astype(jnp.float32) for home in homes] for block, _ in listed]

    def pick(a, i, r):
        zq = real(order[i])
        rows = pl.ds(r * part, part)
        for n, (block, _) in enumerate(listed):
            chosen = bufs[a][zq, ne - 1, rows]
            for home in range(ne - 1):
                chosen = jnp.where(block == home, bufs[a][zq, home, rows], chosen)
            picks[a][pl.ds((2 * r + n) * part, part), :] = chosen

    def pick_whole(a, i):
        arrived(a, order[i], mate)
        arrived(a, order[i], mate_across)
        for r in range(2):
            pick(a, i, r)

    def pick_part(a, i, r):
        for c in range(2):
            part_from_mate(i, a, r, c)
        pick(a, i, r)

    def relay_own(q, a, r):
        part_arrived(q, a, r, 0)

        @pl.when(in_middle)
        def _():
            part_out(q, a, r).start()

        part_x(q, a, r).start()
        part_mate(q, a, r, 0).start()

    def relay_far(q, a, r):
        part_arrived(q, a, r, 1)
        part_mate(q, a, r, 1).start()

    def relay_whole(a, q, eq, k):
        arrived(a, q, eq)
        to_mate(a, q, eq, k).start()

    def relay_0(a):
        @pl.when(at_end)
        def _():
            arrived(a, 1, e)
            over_x(a, 1, 1).start()
            to_mate(a, 1, e, 0).start()
            arrived(a, 0, across)
            across_in(a).start()
            to_mate(a, 0, across, 1).start()

        @pl.when(in_middle)
        def _():
            relay_own(2, 0, a)
            arrived(a, 0, e)
            if a == 0:
                part_in(0, 0, 0).start()
            else:
                part_in(0, 1, 0).start()
                part_in(0, 0, 1).start()
                part_in(0, 1, 1).start()
            to_mate(a, 0, e, 0).start()
            relay_own(2, 1, a)
            relay_whole(a, 1, across, 1)

    def relay_1(r):
        @pl.when(at_end)
        def _():
            for a in range(2):
                part_arrived(2, a, r, 0)
                if r == 0:
                    part_x(2, a, r).start()
                part_mate(2, a, r, 0).start()
            relay_whole(r, 1, across, 1)

        @pl.when(in_middle)
        def _():
            for a in range(2):
                relay_own(3, a, r)
                relay_far(2, a, r)
            if r == 1:
                for a in range(2):
                    across_out(a).start()
            relay_whole(r, 0, across, 1)

    def relay_2():
        @pl.when(at_end)
        def _():
            for a in range(2):
                part_arrived(3, a, 0, 0)
                part_x(3, a, 0).start()
                part_mate(3, a, 0, 0).start()
                relay_far(2, a, 0)

    def relay_3(a):
        @pl.when(at_end)
        def _():
            part_arrived(3, a, 1, 0)
            part_x(3, a, 1).start()
            part_mate(3, a, 1, 0).start()

        relay_far(3, a, 0)

    def relay_4():
        for a in range(2):
            relay_far(3, a, 1)

            @pl.when(at_end)
            def _():
                relay_far(2, a, 1)

    def dots_x(i, r, begin, end):
        slot = i % 3
        rows = pl.ds(0, 2 * tok) if r is None else pl.ds(r * tok, tok)

        @pl.loop(begin, end)
        def _(t):
            cols = pl.ds(pl.multiple_of(t * TILE, TILE), TILE)
            g = jnp.dot(xp[rows, :], w1[slot, :, cols], preferred_element_type=jnp.float32)
            u = jnp.dot(xp[rows, :], w3[slot, :, cols], preferred_element_type=jnp.float32)
            pg[rows, cols] = g if i == 0 else pg[rows, cols] + g
            pu[rows, cols] = u if i == 0 else pu[rows, cols] + u

    def dots_d(i, r):
        slot = i % 2
        rows = pl.ds(0, 2 * tok) if r is None else pl.ds(r * tok, tok)

        @pl.loop(0, hidden // TILE)
        def _(t):
            cols = pl.ds(pl.multiple_of(t * TILE, TILE), TILE)
            h = lax.dot_general(dp[rows, :], w2[slot, cols, :], CONTRACT_LAST, preferred_element_type=jnp.float32)
            dh[rows, cols] = h if i == 0 else dh[rows, cols] + h

    tiles = hidden // TILE

    def forward_x(i):
        pick_whole(0, i)
        for c in load_x(i):
            c.wait()
        dots_x(i, None, 0, tiles)
        if i == 0:
            for c in load_x(3):
                c.start()

    def forward_d(i):
        pick_whole(1, i)
        load_d(i).wait()
        dots_d(i, None)
        load_d(i + 2).start()

    eye = lax.broadcasted_iota(jnp.int32, (tok, tok), 0) == lax.broadcasted_iota(jnp.int32, (tok, tok), 1)

    def gate_columns():
        for k in range(3):
            gate_arrived(k)
        for n, (block, column) in enumerate(listed):
            row = jnp.zeros((1, tok), jnp.float32)
            for home in range(ne):
                for k in range(2):
                    chosen = ((block == home) & (column == k)).astype(jnp.float32)
                    row = row + chosen * gb[home, k : k + 1, :]
            col = jnp.sum(jnp.where(eye, jnp.broadcast_to(row, (tok, tok)), 0.0), axis=1, keepdims=True)
            wide = jnp.broadcast_to(col, (tok, 128))
            for r in range(2):
                gcol[pl.ds((2 * r + n) * part, part), :] = wide[r * part : (r + 1) * part]

    WIDE = 256

    def last_dots(t, r):
        rows = pl.ds(r * tok, tok)
        cols = pl.ds(pl.multiple_of(t * WIDE, WIDE), WIDE)
        dh[rows, cols] += lax.dot_general(dp[rows, :], w2[1, cols, :], CONTRACT_LAST, preferred_element_type=jnp.float32)

    def pointwise(t, r):
        for c in range(WIDE // 128):
            cols = pl.ds(pl.multiple_of(t * WIDE + c * 128, 128), 128)
            for n in range(2):
                rows = pl.ds((2 * r + n) * part, part)
                g = pg[rows, cols]
                u = pu[rows, cols]
                h = dh[rows, cols]
                sig = 1.0 / (1.0 + jnp.exp(-g))
                act = g * sig
                score_ref[rows, :] += act * u * h
                scaled = gcol[rows, :] * h
                dpg_ref[rows, cols] = (scaled * u * sig * (1.0 + g * (1.0 - sig))).astype(jnp.bfloat16)
                dpu_ref[rows, cols] = (scaled * act).astype(jnp.bfloat16)

    def last_d(r):
        pick_part(1, 3, r)
        if r == 0:
            load_d(3).wait()
        last_dots(0, r)

        @pl.loop(1, hidden // WIDE)
        def _(t):
            pointwise(t - 1, r)
            last_dots(t, r)

        pointwise(hidden // WIDE - 1, r)

    def again():
        rows = pl.ds(pl.multiple_of(z * width, width), width)
        return (
            pltpu.make_async_copy(w1_ref.at[0, rows, :], w1.at[0], wsem.at[0, 0]),
            pltpu.make_async_copy(w3_ref.at[0, rows, :], w3.at[0], wsem.at[0, 1]),
        )

    def score_send(k):
        return remote(sd.at[k + 1], sr.at[k], gcs.at[k], gcr.at[k], {"exp": partners[k]})

    def gate_z(k):
        return remote(szs, szr.at[z], gzs.at[k], gzr.at[z], {"hid": lax.rem(z + 1 + k, nz)})

    def core_send(k):
        return remote(dense.at[k, 1], cr.at[k], css.at[k], crs.at[k], {"exp": mate})

    def x_send(k):
        return remote(dense.at[k, 0, 1], xr.at[k], xss.at[k], xrs.at[k], {"exp": across})

    def from_end(k):
        return remote(dense.at[k, 0, 0], ro.at[k], zss.at[k], ros.at[k], {"hid": inward})

    def from_middle(k):
        return remote(dense.at[k, 0, 0], ri.at[k], zss.at[k], ris.at[k], {"hid": inward})

    def to_end(k):
        return remote(dense.at[k, 0, 0], ri.at[k], zss.at[k], ris.at[k], {"hid": outward})

    def straight(k, dest):
        return remote(dense.at[k, 0, 0], rb.at[z], zss.at[k], rbs.at[z], {"hid": dest})

    def multiply(k):
        late = k // 6
        j = lax.rem(k, 3) + late * (3 - lax.rem(k, 3))
        r = k // 3 - 2 * late + k // 7
        slot = lax.rem(3 - j, 3)
        rows = pl.ds(pl.multiple_of(r * tok, tok), tok)

        @pl.loop(0, width // 256)
        def _(t):
            cols = pl.ds(pl.multiple_of(t * 256, 256), 256)
            grad = lax.dot_general(dpg_ref[rows, :], w1[slot, cols, :], CONTRACT_LAST, preferred_element_type=jnp.float32)
            grad += lax.dot_general(dpu_ref[rows, :], w3[slot, cols, :], CONTRACT_LAST, preferred_element_type=jnp.float32)
            for c in range(2):
                for far in range(2):
                    home = c + 2 * far
                    dense[k, c, far, :, cols] = (
                        shares[0][home] * grad[:part] + shares[1][home] * grad[part:]
                    ).astype(jnp.bfloat16)

        core_send(k).start()

    def to_x(k):
        core_send(k).wait_recv()
        both = dense[k, 0, 1].astype(jnp.float32) + cr[k, 1].astype(jnp.float32)
        dense[k, 0, 1] = both.astype(jnp.bfloat16)
        x_send(k).start()

    def total(k):
        x_send(k).wait_recv()
        return dense[k, 0, 0].astype(jnp.float32) + cr[k, 0].astype(jnp.float32) + xr[k].astype(jnp.float32)

    def end_to_z(k):
        @pl.when(at_end)
        def _():
            dense[k, 0, 0] = total(k).astype(jnp.bfloat16)
            from_end(k).start()

    def middle_to_z(k):
        @pl.when(in_middle)
        def _():
            share = total(k)
            if k < 2:
                from_end(k).wait_recv()
                dense[k, 0, 0] = (share + ro[k].astype(jnp.float32)).astype(jnp.bfloat16)
                from_middle(k).start()
            else:
                from_middle(0).wait_recv()
                dense[k, 0, 0] = (share + ri[0].astype(jnp.float32)).astype(jnp.bfloat16)
                to_end(k).start()

    for c in own:
        c.wait()
    score_ref[...] = jnp.zeros_like(score_ref)
    relay_0(0)
    forward_x(0)
    relay_0(1)
    forward_d(0)
    gate_columns()
    relay_1(0)
    forward_x(1)
    relay_1(1)
    forward_d(1)
    relay_2()
    pick_part(0, 2, 0)
    for c in load_x(2):
        c.wait()
    dots_x(2, 0, 0, tiles)
    pick_part(1, 2, 0)
    load_d(2).wait()
    dots_d(2, 0)
    relay_3(0)
    pick_part(0, 3, 0)
    for c in load_x(3):
        c.wait()
    dots_x(3, 0, 0, tiles // 2)
    relay_3(1)
    dots_x(3, 0, tiles // 2, tiles)
    last_d(0)

    multiply(0)
    multiply(1)
    to_x(0)
    relay_4()
    multiply(2)
    to_x(1)
    pick_part(0, 2, 1)
    dots_x(2, 1, 0, tiles)
    to_x(2)
    pick_part(1, 2, 1)
    dots_d(2, 1)
    pick_part(0, 3, 1)
    dots_x(3, 1, 0, tiles)
    end_to_z(0)
    last_d(1)

    line = lax.broadcasted_iota(jnp.int32, (8, tok), 0)
    placed = []
    for n, (_, column) in enumerate(listed):
        both = jnp.concatenate(
            [score_ref[n * part : (n + 1) * part, :], score_ref[tok + n * part : tok + (n + 1) * part, :]], axis=0)
        col = jnp.sum(both, axis=1, keepdims=True)
        row = jnp.sum(jnp.where(eye, jnp.broadcast_to(col, (tok, tok)), 0.0), axis=0, keepdims=True)
        placed.append(jnp.where(line == column, jnp.broadcast_to(row, (8, tok)), 0.0))
    for k in range(ne):
        sd[k] = shares[0][k] * placed[0] + shares[1][k] * placed[1]

    @pl.loop(3, 8)
    def _(k):
        @pl.when(k == 6)
        def _():
            for c in again():
                c.wait()

        multiply(k)

        @pl.when(k > 3)
        def _():
            to_x(k - 1)

        @pl.when(k == 3)
        def _():
            for c in again():
                c.start()
            for i in range(3):
                score_send(i).start()
            end_to_z(1)

        @pl.when(k == 4)
        def _():
            end_to_z(2)

        @pl.when(k == 5)
        def _():
            middle_to_z(0)
            mine = sd[0]
            for i in range(3):
                score_send(i).wait_recv()
                mine += sr[i]
            szs[...] = mine
            szr[z] = mine
            for i in range(nz - 1):
                gate_z(i).start()

    to_x(7)
    middle_to_z(1)
    for k, q in ((3, 3), (4, 2), (5, 1 - own_q)):
        dense[k, 0, 0] = total(k).astype(jnp.bfloat16)
        straight(k, real(q)).start()
        if k == 3:
            middle_to_z(2)

    share = total(6)

    @pl.when(at_end)
    def _():
        to_end(2).wait_recv()
        out_ref[:part, :] = (share + ri[2].astype(jnp.float32)).astype(jnp.bfloat16)

    @pl.when(in_middle)
    def _():
        from_end(2).wait_recv()
        from_middle(1).wait_recv()
        out_ref[:part, :] = (share + ro[2].astype(jnp.float32) + ri[1].astype(jnp.float32)).astype(jnp.bfloat16)

    for k in range(nz - 1):
        source = lax.rem(z + 1 + k, nz)
        remote(szs, szr.at[source], gzs.at[k], gzr.at[source], {"hid": source}).wait_recv()
    gate_total = szr[0]
    for q in range(1, nz):
        gate_total += szr[q]
    grad_gate_ref[...] = gate_total[:2]

    for k in range(3):
        gate_send(k).wait_send()
        score_send(k).wait_send()
        gate_z(k).wait_send()
    for a in range(2):
        @pl.when(at_end)
        def _():
            to_in(a).wait_send()
            across_in(a).wait_send()
            over_x(a, 1, 1).wait_send()
            part_x(2, a, 0).wait_send()
            part_x(3, a, 0).wait_send()
            part_x(3, a, 1).wait_send()

        @pl.when(in_middle)
        def _():
            to_out(a).wait_send()
            across_out(a).wait_send()
            for r in range(2):
                for q in range(2):
                    part_in(q, a, r).wait_send()
                    part_out(q + 2, a, r).wait_send()
                    part_x(q + 2, a, r).wait_send()

        over_x(a, own_q, 0).wait_send()
        for q in range(2):
            to_mate(a, q, e, 0).wait_send()
            to_mate(a, q, across, 1).wait_send()
            for r in range(2):
                for c in range(2):
                    part_mate(q + 2, a, r, c).wait_send()

    share = total(7)
    for k in range(nz - 1):
        source = lax.rem(z + 1 + k, nz)
        remote(dense.at[3, 0, 0], rb.at[source], zss.at[3], rbs.at[source], {"hid": source}).wait_recv()
        share += rb[source].astype(jnp.float32)
    out_ref[part:, :] = share.astype(jnp.bfloat16)

    @pl.loop(0, 8)
    def _(k):
        core_send(k).wait_send()
        x_send(k).wait_send()

        @pl.when(k < 6)
        def _():
            remote(dense.at[k, 0, 0], rb.at[z], zss.at[k], rbs.at[z], {"hid": inward}).wait_send()


def layer(block_experts, tokens, grad_out, gates, w_gate, w_up, w_down):
    nz, ne = 4, 4
    tok, width = tokens.shape
    hidden = w_gate.shape[2]
    used = 2 * BLOCK
    part = tok // 2
    hbm = pl.BlockSpec(memory_space=pl.ANY)
    vmem = pl.BlockSpec(memory_space=pltpu.VMEM)
    smem = pl.BlockSpec(memory_space=pltpu.SMEM)
    bf16, f32 = jnp.bfloat16, jnp.float32
    dma = pltpu.SemaphoreType.DMA
    return pl.pallas_call(
        functools.partial(layer_kernel, width),
        out_shape=(
            pltpu.VMEM((tok, width), bf16),
            pltpu.VMEM((2, tok), f32),
        ),
        in_specs=[smem, hbm, hbm, vmem, hbm, hbm, hbm],
        out_specs=(vmem, vmem),
        scratch_shapes=[
            pltpu.VMEM((nz, ne, tok, width), bf16),
            pltpu.VMEM((nz, ne, tok, width), bf16),
            pltpu.VMEM((ne, 8, tok), f32),
            pltpu.VMEM((3, width, hidden), bf16),
            pltpu.VMEM((3, width, hidden), bf16),
            pltpu.VMEM((2, hidden, width), bf16),
            pltpu.VMEM((used, width), bf16),
            pltpu.VMEM((used, width), bf16),
            pltpu.VMEM((used, hidden), f32),
            pltpu.VMEM((used, hidden), f32),
            pltpu.VMEM((used, hidden), f32),
            pltpu.VMEM((used, hidden), bf16),
            pltpu.VMEM((used, hidden), bf16),
            pltpu.VMEM((used, 128), f32),
            pltpu.VMEM((used, 128), f32),
            pltpu.VMEM((8, 2, 2, part, width), bf16),
            pltpu.VMEM((8, 2, part, width), bf16),
            pltpu.VMEM((8, part, width), bf16),
            pltpu.VMEM((3, part, width), bf16),
            pltpu.VMEM((3, part, width), bf16),
            pltpu.VMEM((nz, part, width), bf16),
            pltpu.VMEM((ne, 8, tok), f32),
            pltpu.VMEM((3, 8, tok), f32),
            pltpu.VMEM((8, tok), f32),
            pltpu.VMEM((nz, 8, tok), f32),
            dma((2,)),
            dma((2,)),
            dma((2, 2)),
            dma((2, nz, 2)),
            dma((2,)),
            dma((4, 2)),
            dma((4, 2)),
            dma((4, 2)),
            dma((4, 2, 2)),
            dma((2, nz, ne)),
            dma((4, 2, 2)),
            dma((4, 2, 2)),
            dma((3, 3)),
            dma((2,)),
            dma((8,)),
            dma((8,)),
            dma((8,)),
            dma((8,)),
            dma((6,)),
            dma((3,)),
            dma((3,)),
            dma((nz,)),
            dma((3,)),
            dma((ne,)),
            dma((3,)),
            dma((3,)),
            dma((3,)),
            dma((nz,)),
        ],
        compiler_params=pltpu.CompilerParams(
            collective_id=0, has_side_effects=True, vmem_limit_bytes=60 * 1024 * 1024
        ),
        name="layer",
    )(block_experts, tokens, grad_out, gates, w_gate, w_up, w_down)


def finish_kernel(grad_ref, gate_ref, grad_out_ref, gate_out_ref, sems):
    copies = (
        pltpu.make_async_copy(grad_ref, grad_out_ref, sems.at[0]),
        pltpu.make_async_copy(gate_ref, gate_out_ref, sems.at[1]),
    )
    for c in copies:
        c.start()
    for c in copies:
        c.wait()


def finish(grad, gate_rows):
    vmem = pl.BlockSpec(memory_space=pltpu.VMEM)
    hbm = pl.BlockSpec(memory_space=pl.ANY)
    return pl.pallas_call(
        finish_kernel,
        out_shape=(
            jax.ShapeDtypeStruct(grad.shape, grad.dtype),
            jax.ShapeDtypeStruct(gate_rows.shape, gate_rows.dtype),
        ),
        in_specs=[vmem, vmem],
        out_specs=(hbm, hbm),
        scratch_shapes=[pltpu.SemaphoreType.DMA((2,))],
        compiler_params=pltpu.CompilerParams(vmem_limit_bytes=1024 * 1024),
        name="finish",
    )(grad, gate_rows)


def fast_local(tokens, grad_out, gates, block_experts, w_gate, w_up, w_down):
    grad, gate_rows = layer(block_experts.T, tokens, grad_out, gates.T, w_gate, w_up, w_down)
    grad, gate_rows = finish(grad, gate_rows)
    return grad, gate_rows.T


def combined(owned, score, list_block, live, slot_hot, tok_dev, width_dev, capacity):
    n_experts = lax.axis_size("exp")
    own_index = lax.axis_index("exp")
    per_home = tok_dev // BLOCK
    result_cols = owned.reshape(width_dev, capacity, BLOCK)
    score_blocks = score.reshape(capacity, BLOCK)

    def share(home):
        wanted = home * per_home + jnp.arange(per_home, dtype=jnp.int32)
        select = ((list_block[None, :] == wanted[:, None]) & live[None, :]).astype(jnp.float32)
        grad_part = jnp.einsum("bi,dir->dbr", select, result_cols, precision=HIGHEST).reshape(
            width_dev, tok_dev
        )
        gate_part = jnp.einsum(
            "bi,ik,ir->kbr", select, slot_hot, score_blocks, precision=HIGHEST
        ).reshape(2, tok_dev)
        return (grad_part, gate_part)

    zero_totals = (
        jnp.zeros((width_dev, tok_dev), jnp.float32),
        jnp.zeros((2, tok_dev), jnp.float32),
    )

    def single_turn(step, totals):
        grad_part, gate_part = share((own_index + 1 + step) % n_experts)
        return passed_along((totals[0] + grad_part, totals[1] + gate_part), "exp", -1)

    totals = lax.fori_loop(0, n_experts - 1, single_turn, zero_totals)
    grad_part, gate_part = share(own_index)
    grad_total = totals[0] + grad_part
    gate_total = totals[1] + gate_part
    return (grad_total.T.astype(jnp.bfloat16), gate_total.T)


def local(tokens, grad_out, gates, block_experts, w_gate, w_up, w_down):
    own_index = lax.axis_index("exp")
    tok_dev, width_dev = tokens.shape
    blocks_all = block_experts.shape[0]
    capacity = blocks_all // 2
    used_count = capacity * BLOCK
    list_block, list_slot, live = routing(block_experts, own_index)
    row_index = (list_block[:, None] * BLOCK + jnp.arange(BLOCK, dtype=jnp.int32)[None, :]).reshape(
        used_count
    )
    x_home, dy_home, gate_home = (
        lax.all_gather(tokens, "exp", axis=0, tiled=True),
        lax.all_gather(grad_out, "exp", axis=0, tiled=True),
        lax.all_gather(gates, "exp", axis=0, tiled=True),
    )
    gate_pick = (
        jnp.take(gate_home, row_index, axis=0).astype(jnp.float32).reshape(capacity, BLOCK, 2)
    )
    slot_hot = (list_slot[:, None] == jnp.arange(2, dtype=jnp.int32)[None, :]).astype(jnp.float32)
    slot_hot = slot_hot * live[:, None].astype(jnp.float32)
    gate_column = jnp.sum(gate_pick * slot_hot[:, None, :], axis=2).reshape(used_count)
    x_piece = jnp.take(lax.all_gather(x_home, "hid", axis=1, tiled=True), row_index, axis=0)
    dy_piece = jnp.take(lax.all_gather(dy_home, "hid", axis=1, tiled=True), row_index, axis=0)
    pre_gate = jnp.dot(x_piece, w_gate[0], preferred_element_type=jnp.float32)
    pre_up = jnp.dot(x_piece, w_up[0], preferred_element_type=jnp.float32)
    d_hidden = lax.dot_general(dy_piece, w_down[0], CONTRACT_LAST, preferred_element_type=jnp.float32)
    sigmoid_gate = jax.nn.sigmoid(pre_gate)
    activated = pre_gate * sigmoid_gate
    score_part = jnp.sum(activated * pre_up * d_hidden, axis=1)
    score = lax.psum(score_part, "hid")
    scaled = gate_column[:, None] * d_hidden
    d_pre_gate = (scaled * pre_up * sigmoid_gate * (1.0 + pre_gate * (1.0 - sigmoid_gate))).astype(
        jnp.bfloat16
    )
    d_pre_up = (scaled * activated).astype(jnp.bfloat16)
    first = lax.dot_general(w_gate[0], d_pre_gate, CONTRACT_LAST, preferred_element_type=jnp.float32)
    owned = lax.psum_scatter(
        first
        + lax.dot_general(w_up[0], d_pre_up, CONTRACT_LAST, preferred_element_type=jnp.float32),
        "hid",
        scatter_dimension=0,
        tiled=True,
    )
    return combined(owned, score, list_block, live, slot_hot, tok_dev, width_dev, capacity)


def solution(mesh):
    placed = (
        P(("grp", "exp"), "hid"),
        P(("grp", "exp"), "hid"),
        P(("grp", "exp"), None),
        P("grp", None),
        P("exp", None, "hid"),
        P("exp", None, "hid"),
        P("exp", "hid", None),
    )
    body = fast_local if (mesh.shape["exp"], mesh.shape["hid"]) == (4, 4) else local
    return jax.shard_map(
        body,
        mesh=mesh,
        in_specs=placed,
        out_specs=(P(("grp", "exp"), "hid"), P(("grp", "exp"), None)),
        check_vma=False,
    )
```

```python
import functools
import jax
import jax.numpy as jnp
from jax import lax
from jax.experimental import pallas as pl
from jax.experimental.pallas import tpu as pltpu
from jax.sharding import PartitionSpec as P

BLOCK = 128


HIGHEST = lax.Precision.HIGHEST
CONTRACT_LAST = (((1,), (1,)), ((), ()))
MESH = pl.DeviceIdType.MESH


def passed_along(block, axis, distance):
    devices = range(lax.axis_size(axis))
    route = [((i - distance) % len(devices), i) for i in devices]
    return lax.ppermute(block, axis, route)


def routing(block_experts, own_index):
    blocks_all = block_experts.shape[0]
    capacity = blocks_all // 2
    matched = block_experts == own_index
    chosen = jnp.any(matched, axis=1)
    slot_of = matched[:, 1].astype(jnp.int32)
    order = jnp.arange(blocks_all, dtype=jnp.int32)
    position = jnp.sum((chosen[None, :] & (order[None, :] < order[:, None])).astype(jnp.int32), axis=1)
    placed = (position[None, :] == jnp.arange(capacity, dtype=jnp.int32)[:, None]) & chosen[None, :]
    placed_int = placed.astype(jnp.int32)
    list_block = jnp.sum(placed_int * jnp.arange(blocks_all, dtype=jnp.int32)[None, :], axis=1)
    list_slot = jnp.sum(placed_int * slot_of[None, :], axis=1)
    live = jnp.any(placed, axis=1)
    return list_block, list_slot, live


def layer_kernel(width, be_ref, tok_ref, dy_ref, gate_ref, w1_ref, w3_ref, w2_ref, out_ref, grad_gate_ref,
                 xb, db, gb, w1, w3, w2, xp, dp, pg, pu, dh, dpg_ref, dpu_ref, gcol, score_ref,
                 dense, cr, xs, xr, zs, ro, ri, sd, sr, szs, szr,
                 s_zi, s_zo, s_x, s_c, s_ex, s_xh, s_ch, rsem, hsem, wsem, lsem,
                 css, crs, xss, xrs, zss, ros, ris, gs, gr, gcs, gcr, gzs, gzr):
    nz, ne = 4, 4
    z = lax.axis_index("hid")
    e = lax.axis_index("exp")
    core = lax.rem(e, 2)
    side = e // 2
    mate = e + 1 - 2 * core
    across = lax.rem(e + 2, ne)
    mate_across = lax.rem(mate + 2, ne)
    upper = z // 2
    at_end = (z == 0) | (z == nz - 1)
    in_middle = (z == 1) | (z == 2)
    inward = z + 1 - 2 * upper
    outward = z - 1 + 2 * upper
    own_q = z + upper * (nz - 1 - 2 * z)
    bufs = (xb, db)
    own_refs = (tok_ref, dy_ref)
    picks = (xp, dp)
    hidden = w1.shape[2]
    tok = xb.shape[2]
    half = xr.shape[2]

    def real(q):
        return q + upper * (nz - 1 - 2 * q)

    order = (own_q, 1 - own_q, 2, 3)

    def load(ref, buf, j, i, slot):
        rows = pl.ds(pl.multiple_of(real(order[i]) * width, width), width)
        src = ref.at[0, :, rows] if j == 2 else ref.at[0, rows, :]
        return pltpu.make_async_copy(src, buf.at[slot], wsem.at[slot, j])

    def load_x(i, slot):
        return load(w1_ref, w1, 0, i, slot), load(w3_ref, w3, 1, i, slot)

    def load_d(i, slot):
        return load(w2_ref, w2, 2, i, slot)

    def remote(src, dst, ssem, rsem_, dev):
        return pltpu.make_async_remote_copy(
            src_ref=src, dst_ref=dst, send_sem=ssem, recv_sem=rsem_, device_id=dev, device_id_type=MESH)

    def send(a, q, eq, ssem, dev, src=None):
        zq = real(q)
        place = bufs[a].at[zq, eq]
        return remote(place if src is None else src, place, ssem, rsem.at[a, zq, eq], dev)

    def to_in(a, q, n, src=None):
        return send(a, q, e, s_zi.at[a, n], {"hid": inward}, src)

    def to_out(a, q, n, src=None):
        return send(a, q, e, s_zo.at[a, n], {"hid": outward}, src)

    def over_x(a, q, src=None):
        return send(a, q, e, s_x.at[a, real(q)], {"exp": across}, src)

    def to_mate(a, q, eq, k, src=None):
        return send(a, q, eq, s_c.at[a, real(q), k], {"exp": mate}, src)

    def across_in(a):
        return send(a, 0, across, s_ex.at[a], {"hid": inward})

    def part_of(a, q, eq, r):
        return bufs[a].at[real(q), eq, pl.ds(r * (tok // 2), tok // 2)]

    def send_part(a, q, eq, r, ssem, rsem_, dev):
        return remote(part_of(a, q, eq, r), part_of(a, q, eq, r), ssem, rsem_, dev)

    def part_in(a, r):
        return send_part(a, 0, e, r, s_zi.at[a, 1 + r], hsem.at[a, r, 0], {"hid": inward})

    def part_out(a, r):
        return send_part(a, 3, e, r, s_zo.at[a, 2 + r], hsem.at[a, r, 0], {"hid": outward})

    def part_x(a, r):
        return send_part(a, 3, e, r, s_xh.at[a, r], hsem.at[a, r, 1], {"exp": across})

    def part_mate(a, r):
        return send_part(a, 3, across, r, s_ch.at[a, r], rsem.at[a, real(3), across], {"exp": mate})

    def across_out(a):
        return send_part(a, 3, across, 1, s_ex.at[a], hsem.at[a, 1, 1], {"hid": outward})

    def part_arrived(a, r, c):
        send_part(a, 3, across if c else e, r, s_ex.at[a], hsem.at[a, r, c], {"exp": mate}).wait_recv()

    def arrived(a, q, eq):
        send(a, q, eq, s_ex.at[a], {"exp": mate}).wait_recv()

    partners = (mate, across, mate_across)

    def gate_send(k):
        return remote(gb.at[e], gb.at[e], gs.at[k], gr.at[e], {"exp": partners[k]})

    def gate_arrived(k):
        remote(gb.at[partners[k]], gb.at[partners[k]], gs.at[k], gr.at[partners[k]], {"exp": mate}).wait_recv()

    own = (
        pltpu.make_async_copy(tok_ref, xb.at[z, e], lsem.at[0]),
        pltpu.make_async_copy(dy_ref, db.at[z, e], lsem.at[1]),
    )
    for c in own:
        c.start()
    for i in range(2):
        for c in load_x(i, i):
            c.start()
        load_d(i, i).start()

    barrier = pltpu.get_barrier_semaphore()
    for dev in partners:
        pl.semaphore_signal(barrier, inc=1, device_id={"exp": dev}, device_id_type=MESH)
    for k in range(nz - 1):
        pl.semaphore_signal(barrier, inc=1, device_id={"hid": lax.rem(z + 1 + k, nz)}, device_id_type=MESH)
    gb[e] = jnp.concatenate([gate_ref[...].astype(jnp.float32), jnp.zeros((6, tok), jnp.float32)], axis=0)
    pl.semaphore_wait(barrier, nz + 2)

    for a in range(2):
        to_in(a, own_q, 0, own_refs[a]).start()

        @pl.when(in_middle)
        def _():
            to_out(a, own_q, 0, own_refs[a]).start()

        over_x(a, own_q, own_refs[a]).start()
        to_mate(a, own_q, e, 0, own_refs[a]).start()
    for k in range(3):
        gate_send(k).start()

    first, first_slot = jnp.int32(-1), jnp.int32(0)
    last, last_slot = jnp.int32(-1), jnp.int32(0)
    for b in range(ne):
        one, two = be_ref[0, b] == e, be_ref[1, b] == e
        here = one | two
        column = two.astype(jnp.int32)
        fresh = here & (first < 0)
        later = here & (first >= 0)
        last, last_slot = jnp.where(later, b, last), jnp.where(later, column, last_slot)
        first, first_slot = jnp.where(fresh, b, first), jnp.where(fresh, column, first_slot)
    listed = ((first, first_slot), (last, last_slot))
    homes = (e, mate, across, mate_across)
    shares = [[(block == home).astype(jnp.float32) for home in homes] for block, _ in listed]

    def pick(a, i):
        q = order[i]
        arrived(a, q, mate)
        arrived(a, q, mate_across)
        zq = real(q)
        for n, (block, _) in enumerate(listed):
            rows = bufs[a][zq, ne - 1]
            for home in range(ne - 1):
                rows = jnp.where(block == home, bufs[a][zq, home], rows)
            picks[a][n * tok : (n + 1) * tok, :] = rows

    def relay(step, a):
        @pl.when(at_end)
        def _():
            if step < 2:
                arrived(a, step + 1, e)
                over_x(a, step + 1).start()
                to_mate(a, step + 1, e, 0).start()
            if step == 2:
                part_arrived(a, 0, 0)
                part_x(a, 0).start()
            if step < 3:
                arrived(a, step, across)
                if step == 0:
                    across_in(a).start()
                to_mate(a, step, across, 1).start()
            if step == 2:
                part_arrived(a, 1, 0)
                to_mate(a, 3, e, 0).start()
            if step == 3:
                for r in range(2):
                    part_arrived(a, r, 1)
                    part_mate(a, r).start()

        if step < 3:
            @pl.when(in_middle)
            def _():
                if step == 0:
                    arrived(a, 0, e)
                    for r in range(2):
                        part_in(a, r).start()
                    to_mate(a, 0, e, 0).start()
                    arrived(a, 2, e)
                    to_out(a, 2, 1).start()
                    over_x(a, 2).start()
                    to_mate(a, 2, e, 0).start()
                    arrived(a, 1, across)
                    to_mate(a, 1, across, 1).start()
                if step == 1:
                    for r in range(2):
                        part_arrived(a, r, 0)
                        part_out(a, r).start()
                        part_x(a, r).start()
                    to_mate(a, 3, e, 0).start()
                    arrived(a, 2, across)
                    to_mate(a, 2, across, 1).start()
                    arrived(a, 0, across)
                    to_mate(a, 0, across, 1).start()
                if step == 2:
                    for r in range(2):
                        part_arrived(a, r, 1)
                    across_out(a).start()
                    to_mate(a, 3, across, 1).start()

    def forward_x(i):
        slot = i % 2
        pick(0, i)
        for c in load_x(i, slot):
            c.wait()

        for total_ref, w in ((pg, w1), (pu, w3)):
            term = jnp.dot(xp[...], w[slot], preferred_element_type=jnp.float32)
            total_ref[...] = term if i == 0 else total_ref[...] + term

        if i + 2 < nz:
            for c in load_x(i + 2, slot):
                c.start()

    def forward_d(i):
        slot = i % 2
        pick(1, i)
        load_d(i, slot).wait()

        term = lax.dot_general(dp[...], w2[slot], CONTRACT_LAST, preferred_element_type=jnp.float32)
        dh[...] = term if i == 0 else dh[...] + term

        if i + 2 < nz:
            load_d(i + 2, slot).start()

    def gate_columns():
        for k in range(3):
            gate_arrived(k)
        eye = lax.broadcasted_iota(jnp.int32, (tok, tok), 0) == lax.broadcasted_iota(jnp.int32, (tok, tok), 1)
        for n, (block, column) in enumerate(listed):
            row = jnp.zeros((1, tok), jnp.float32)
            for home in range(ne):
                for k in range(2):
                    chosen = ((block == home) & (column == k)).astype(jnp.float32)
                    row = row + chosen * gb[home, k : k + 1, :]
            col = jnp.sum(jnp.where(eye, jnp.broadcast_to(row, (tok, tok)), 0.0), axis=1, keepdims=True)
            gcol[n * tok : (n + 1) * tok, :] = jnp.broadcast_to(col, (tok, 128))

    for c in own:
        c.wait()
    score_ref[...] = jnp.zeros_like(score_ref)
    for step in range(3):
        relay(step, 0)
        forward_x(step)
        relay(step, 1)
        forward_d(step)
        if step == 0:
            gate_columns()

    WIDE = 512

    def last_dots(t):
        cols = pl.ds(t * WIDE, WIDE)
        dh[:, cols] += lax.dot_general(dp[...], w2[1, cols, :], CONTRACT_LAST, preferred_element_type=jnp.float32)

    def pointwise(t):
        for c in range(WIDE // 128):
            cols = pl.ds(t * WIDE + c * 128, 128)
            for r in range(0, 2 * tok, 64):
                rows = pl.ds(r, 64)
                g = pg[rows, cols]
                u = pu[rows, cols]
                h = dh[rows, cols]
                sig = 1.0 / (1.0 + jnp.exp(-g))
                act = g * sig
                score_ref[rows, :] += act * u * h
                scaled = gcol[rows, :] * h
                dpg_ref[rows, cols] = (scaled * u * sig * (1.0 + g * (1.0 - sig))).astype(jnp.bfloat16)
                dpu_ref[rows, cols] = (scaled * act).astype(jnp.bfloat16)

    def last_x(t):
        cols = pl.ds(t * (hidden // 2), hidden // 2)
        pg[:, cols] += jnp.dot(xp[...], w1[1, :, cols], preferred_element_type=jnp.float32)
        pu[:, cols] += jnp.dot(xp[...], w3[1, :, cols], preferred_element_type=jnp.float32)

    relay(3, 0)
    pick(0, 3)
    for c in load_x(3, 1):
        c.wait()
    last_x(0)
    relay(3, 1)
    last_x(1)
    pick(1, 3)
    load_d(3, 1).wait()
    last_dots(0)

    for t in range(1, hidden // WIDE):
        last_dots(t)
        pointwise(t - 1)
    pointwise(hidden // WIDE - 1)

    def again(j, slot):
        zq = real(own_q + (3 - j) * (1 - 2 * own_q))
        rows = pl.ds(pl.multiple_of(zq * width, width), width)
        return (
            pltpu.make_async_copy(w1_ref.at[0, rows, :], w1.at[slot], wsem.at[slot, 0]),
            pltpu.make_async_copy(w3_ref.at[0, rows, :], w3.at[slot], wsem.at[slot, 1]),
        )

    def score_send(k):
        return remote(sd.at[k + 1], sr.at[k], gcs.at[k], gcr.at[k], {"exp": partners[k]})

    def gate_z(k):
        return remote(szs, szr.at[z], gzs.at[k], gzr.at[z], {"hid": lax.rem(z + 1 + k, nz)})

    eye = lax.broadcasted_iota(jnp.int32, (tok, tok), 0) == lax.broadcasted_iota(jnp.int32, (tok, tok), 1)
    line = lax.broadcasted_iota(jnp.int32, (8, tok), 0)
    placed = []
    for n, (_, column) in enumerate(listed):
        col = jnp.sum(score_ref[n * tok : (n + 1) * tok, :], axis=1, keepdims=True)
        row = jnp.sum(jnp.where(eye, jnp.broadcast_to(col, (tok, tok)), 0.0), axis=0, keepdims=True)
        placed.append(jnp.where(line == column, jnp.broadcast_to(row, (8, tok)), 0.0))
    for k in range(ne):
        sd[k] = shares[0][k] * placed[0] + shares[1][k] * placed[1]
    for k in range(3):
        score_send(k).start()

    def core_send(k):
        return remote(dense.at[k, 1], cr.at[k], css.at[k], crs.at[k], {"exp": mate})

    def x_send(k):
        return remote(xs.at[k], xr.at[k], xss.at[k], xrs.at[k], {"exp": across})

    def from_end(k):
        return remote(zs.at[k], ro.at[k], zss.at[k], ros.at[k], {"hid": inward})

    def from_middle(k):
        return remote(zs.at[k], ri.at[k], zss.at[k], ris.at[k], {"hid": inward})

    def to_end(k):
        return remote(zs.at[k], ri.at[k], zss.at[k], ris.at[k], {"hid": outward})

    def multiply(k):
        j = k // 2
        slot = lax.rem(j + 1, 2)

        @pl.when((lax.rem(k, 2) == 0) & (j >= 2))
        def _():
            for c in again(j, slot):
                c.wait()

        rows = pl.ds(pl.multiple_of(lax.rem(k, 2) * half, half), half)
        grad = lax.dot_general(dpg_ref[...], w1[slot, rows, :], CONTRACT_LAST, preferred_element_type=jnp.float32)
        grad += lax.dot_general(dpu_ref[...], w3[slot, rows, :], CONTRACT_LAST, preferred_element_type=jnp.float32)
        for c in range(2):
            for far in range(2):
                home = c + 2 * far
                dense[k, c, far] = (
                    shares[0][home] * grad[:tok] + shares[1][home] * grad[tok:]
                ).astype(jnp.bfloat16)

        core_send(k).start()

        @pl.when((lax.rem(k, 2) == 1) & (j < 2))
        def _():
            for c in again(j + 2, slot):
                c.start()

    def to_x(k):
        core_send(k).wait_recv()
        both = dense[k, 0, 1].astype(jnp.float32) + cr[k, 1].astype(jnp.float32)
        xs[k] = both.astype(jnp.bfloat16)
        x_send(k).start()

    def total(k):
        x_send(k).wait_recv()
        return dense[k, 0, 0].astype(jnp.float32) + cr[k, 0].astype(jnp.float32) + xr[k].astype(jnp.float32)

    def to_z(k):
        share = total(k)

        @pl.when(at_end)
        def _():
            zs[k] = share.astype(jnp.bfloat16)
            from_end(k).start()

        @pl.when(in_middle & (k < 4))
        def _():
            from_end(k).wait_recv()
            zs[k] = (share + ro[k].astype(jnp.float32)).astype(jnp.bfloat16)
            from_middle(k).start()

        @pl.when(in_middle & (k >= 4))
        def _():
            from_middle(k - 4).wait_recv()
            zs[k] = (share + ri[k - 4].astype(jnp.float32)).astype(jnp.bfloat16)
            to_end(k).start()

    @pl.loop(0, 8)
    def _(k):
        multiply(k)

        @pl.when(k >= 1)
        def _():
            to_x(k - 1)

        @pl.when(k == 2)
        def _():
            mine = sd[0]
            for i in range(3):
                score_send(i).wait_recv()
                mine += sr[i]
            szs[...] = mine
            szr[z] = mine
            for i in range(nz - 1):
                gate_z(i).start()

        @pl.when((k == 4) | (k == 6))
        def _():
            to_z((k - 4) // 2)

    to_x(7)

    @pl.loop(2, 6)
    def _(k):
        to_z(k)

    for k in (6, 7):
        share = total(k)
        cols = pl.ds((k - 6) * half, half)

        @pl.when(at_end)
        def _():
            to_end(k - 2).wait_recv()
            out_ref[:, cols] = (share + ri[k - 2].astype(jnp.float32)).astype(jnp.bfloat16)

        @pl.when(in_middle)
        def _():
            from_end(k - 2).wait_recv()
            from_middle(k - 4).wait_recv()
            out_ref[:, cols] = (
                share + ro[k - 2].astype(jnp.float32) + ri[k - 4].astype(jnp.float32)
            ).astype(jnp.bfloat16)

    for k in range(nz - 1):
        source = lax.rem(z + 1 + k, nz)
        remote(szs, szr.at[source], gzs.at[k], gzr.at[source], {"hid": source}).wait_recv()
    gate_total = szr[0]
    for q in range(1, nz):
        gate_total += szr[q]
    grad_gate_ref[...] = gate_total[:2]

    for k in range(3):
        gate_send(k).wait_send()
        score_send(k).wait_send()
        gate_z(k).wait_send()

    @pl.loop(0, 8)
    def _(k):
        core_send(k).wait_send()
        x_send(k).wait_send()

        @pl.when(k < 6)
        def _():
            from_end(k).wait_send()

    for a in range(2):
        to_in(a, own_q, 0).wait_send()

        @pl.when(at_end)
        def _():
            across_in(a).wait_send()
            for q in range(3):
                over_x(a, q).wait_send()
                to_mate(a, q, across, 1).wait_send()
            part_x(a, 0).wait_send()
            for r in range(2):
                part_mate(a, r).wait_send()

        @pl.when(in_middle)
        def _():
            to_out(a, 1, 0).wait_send()
            to_out(a, 2, 1).wait_send()
            over_x(a, 1).wait_send()
            over_x(a, 2).wait_send()
            for r in range(2):
                part_in(a, r).wait_send()
                part_out(a, r).wait_send()
                part_x(a, r).wait_send()
            across_out(a).wait_send()
            for q in range(4):
                to_mate(a, q, across, 1).wait_send()

        for q in range(4):
            to_mate(a, q, e, 0).wait_send()


def layer(block_experts, tokens, grad_out, gates, w_gate, w_up, w_down):
    nz, ne = 4, 4
    tok, width = tokens.shape
    hidden = w_gate.shape[2]
    used = 2 * BLOCK
    half = width // 2
    hbm = pl.BlockSpec(memory_space=pl.ANY)
    vmem = pl.BlockSpec(memory_space=pltpu.VMEM)
    smem = pl.BlockSpec(memory_space=pltpu.SMEM)
    bf16, f32 = jnp.bfloat16, jnp.float32
    dma = pltpu.SemaphoreType.DMA
    return pl.pallas_call(
        functools.partial(layer_kernel, width),
        out_shape=(
            pltpu.VMEM((tok, width), bf16),
            pltpu.VMEM((2, tok), f32),
        ),
        in_specs=[smem, hbm, hbm, vmem, hbm, hbm, hbm],
        out_specs=(vmem, vmem),
        scratch_shapes=[
            pltpu.VMEM((nz, ne, tok, width), bf16),
            pltpu.VMEM((nz, ne, tok, width), bf16),
            pltpu.VMEM((ne, 8, tok), f32),
            pltpu.VMEM((2, width, hidden), bf16),
            pltpu.VMEM((2, width, hidden), bf16),
            pltpu.VMEM((2, hidden, width), bf16),
            pltpu.VMEM((used, width), bf16),
            pltpu.VMEM((used, width), bf16),
            pltpu.VMEM((used, hidden), f32),
            pltpu.VMEM((used, hidden), f32),
            pltpu.VMEM((used, hidden), f32),
            pltpu.VMEM((used, hidden), bf16),
            pltpu.VMEM((used, hidden), bf16),
            pltpu.VMEM((used, 128), f32),
            pltpu.VMEM((used, 128), f32),
            pltpu.VMEM((8, 2, 2, tok, half), bf16),
            pltpu.VMEM((8, 2, tok, half), bf16),
            pltpu.VMEM((8, tok, half), bf16),
            pltpu.VMEM((8, tok, half), bf16),
            pltpu.VMEM((6, tok, half), bf16),
            pltpu.VMEM((6, tok, half), bf16),
            pltpu.VMEM((6, tok, half), bf16),
            pltpu.VMEM((ne, 8, tok), f32),
            pltpu.VMEM((3, 8, tok), f32),
            pltpu.VMEM((8, tok), f32),
            pltpu.VMEM((nz, 8, tok), f32),
            dma((2, 3)),
            dma((2, 4)),
            dma((2, nz)),
            dma((2, nz, 2)),
            dma((2,)),
            dma((2, 2)),
            dma((2, 2)),
            dma((2, nz, ne)),
            dma((2, 2, 2)),
            dma((2, 3)),
            dma((2,)),
            dma((8,)),
            dma((8,)),
            dma((8,)),
            dma((8,)),
            dma((6,)),
            dma((6,)),
            dma((6,)),
            dma((3,)),
            dma((ne,)),
            dma((3,)),
            dma((3,)),
            dma((3,)),
            dma((nz,)),
        ],
        compiler_params=pltpu.CompilerParams(
            collective_id=0, has_side_effects=True, vmem_limit_bytes=60 * 1024 * 1024
        ),
        name="layer",
    )(block_experts, tokens, grad_out, gates, w_gate, w_up, w_down)


def finish_kernel(grad_ref, gate_ref, grad_out_ref, gate_out_ref, sems):
    copies = (
        pltpu.make_async_copy(grad_ref, grad_out_ref, sems.at[0]),
        pltpu.make_async_copy(gate_ref, gate_out_ref, sems.at[1]),
    )
    for c in copies:
        c.start()
    for c in copies:
        c.wait()


def finish(grad, gate_rows):
    vmem = pl.BlockSpec(memory_space=pltpu.VMEM)
    hbm = pl.BlockSpec(memory_space=pl.ANY)
    return pl.pallas_call(
        finish_kernel,
        out_shape=(
            jax.ShapeDtypeStruct(grad.shape, grad.dtype),
            jax.ShapeDtypeStruct(gate_rows.shape, gate_rows.dtype),
        ),
        in_specs=[vmem, vmem],
        out_specs=(hbm, hbm),
        scratch_shapes=[pltpu.SemaphoreType.DMA((2,))],
        compiler_params=pltpu.CompilerParams(vmem_limit_bytes=1024 * 1024),
        name="finish",
    )(grad, gate_rows)


def fast_local(tokens, grad_out, gates, block_experts, w_gate, w_up, w_down):
    grad, gate_rows = layer(block_experts.T, tokens, grad_out, gates.T, w_gate, w_up, w_down)
    grad, gate_rows = finish(grad, gate_rows)
    return grad, gate_rows.T


def combined(owned, score, list_block, live, slot_hot, tok_dev, width_dev, capacity):
    n_experts = lax.axis_size("exp")
    own_index = lax.axis_index("exp")
    per_home = tok_dev // BLOCK
    result_cols = owned.reshape(width_dev, capacity, BLOCK)
    score_blocks = score.reshape(capacity, BLOCK)

    def share(home):
        wanted = home * per_home + jnp.arange(per_home, dtype=jnp.int32)
        select = ((list_block[None, :] == wanted[:, None]) & live[None, :]).astype(jnp.float32)
        grad_part = jnp.einsum("bi,dir->dbr", select, result_cols, precision=HIGHEST).reshape(
            width_dev, tok_dev
        )
        gate_part = jnp.einsum(
            "bi,ik,ir->kbr", select, slot_hot, score_blocks, precision=HIGHEST
        ).reshape(2, tok_dev)
        return (grad_part, gate_part)

    zero_totals = (
        jnp.zeros((width_dev, tok_dev), jnp.float32),
        jnp.zeros((2, tok_dev), jnp.float32),
    )

    def single_turn(step, totals):
        grad_part, gate_part = share((own_index + 1 + step) % n_experts)
        return passed_along((totals[0] + grad_part, totals[1] + gate_part), "exp", -1)

    totals = lax.fori_loop(0, n_experts - 1, single_turn, zero_totals)
    grad_part, gate_part = share(own_index)
    grad_total = totals[0] + grad_part
    gate_total = totals[1] + gate_part
    return (grad_total.T.astype(jnp.bfloat16), gate_total.T)


def local(tokens, grad_out, gates, block_experts, w_gate, w_up, w_down):
    own_index = lax.axis_index("exp")
    tok_dev, width_dev = tokens.shape
    blocks_all = block_experts.shape[0]
    capacity = blocks_all // 2
    used_count = capacity * BLOCK
    list_block, list_slot, live = routing(block_experts, own_index)
    row_index = (list_block[:, None] * BLOCK + jnp.arange(BLOCK, dtype=jnp.int32)[None, :]).reshape(
        used_count
    )
    x_home, dy_home, gate_home = (
        lax.all_gather(tokens, "exp", axis=0, tiled=True),
        lax.all_gather(grad_out, "exp", axis=0, tiled=True),
        lax.all_gather(gates, "exp", axis=0, tiled=True),
    )
    gate_pick = (
        jnp.take(gate_home, row_index, axis=0).astype(jnp.float32).reshape(capacity, BLOCK, 2)
    )
    slot_hot = (list_slot[:, None] == jnp.arange(2, dtype=jnp.int32)[None, :]).astype(jnp.float32)
    slot_hot = slot_hot * live[:, None].astype(jnp.float32)
    gate_column = jnp.sum(gate_pick * slot_hot[:, None, :], axis=2).reshape(used_count)
    x_piece = jnp.take(lax.all_gather(x_home, "hid", axis=1, tiled=True), row_index, axis=0)
    dy_piece = jnp.take(lax.all_gather(dy_home, "hid", axis=1, tiled=True), row_index, axis=0)
    pre_gate = jnp.dot(x_piece, w_gate[0], preferred_element_type=jnp.float32)
    pre_up = jnp.dot(x_piece, w_up[0], preferred_element_type=jnp.float32)
    d_hidden = lax.dot_general(dy_piece, w_down[0], CONTRACT_LAST, preferred_element_type=jnp.float32)
    sigmoid_gate = jax.nn.sigmoid(pre_gate)
    activated = pre_gate * sigmoid_gate
    score_part = jnp.sum(activated * pre_up * d_hidden, axis=1)
    score = lax.psum(score_part, "hid")
    scaled = gate_column[:, None] * d_hidden
    d_pre_gate = (scaled * pre_up * sigmoid_gate * (1.0 + pre_gate * (1.0 - sigmoid_gate))).astype(
        jnp.bfloat16
    )
    d_pre_up = (scaled * activated).astype(jnp.bfloat16)
    first = lax.dot_general(w_gate[0], d_pre_gate, CONTRACT_LAST, preferred_element_type=jnp.float32)
    owned = lax.psum_scatter(
        first
        + lax.dot_general(w_up[0], d_pre_up, CONTRACT_LAST, preferred_element_type=jnp.float32),
        "hid",
        scatter_dimension=0,
        tiled=True,
    )
    return combined(owned, score, list_block, live, slot_hot, tok_dev, width_dev, capacity)


def solution(mesh):
    placed = (
        P(("grp", "exp"), "hid"),
        P(("grp", "exp"), "hid"),
        P(("grp", "exp"), None),
        P("grp", None),
        P("exp", None, "hid"),
        P("exp", None, "hid"),
        P("exp", "hid", None),
    )
    body = fast_local if (mesh.shape["exp"], mesh.shape["hid"]) == (4, 4) else local
    return jax.shard_map(
        body,
        mesh=mesh,
        in_specs=placed,
        out_specs=(P(("grp", "exp"), "hid"), P(("grp", "exp"), None)),
        check_vma=False,
    )
```

```python
import functools
import jax
import jax.numpy as jnp
from jax import lax
from jax.experimental import pallas as pl
from jax.experimental.pallas import tpu as pltpu
from jax.sharding import PartitionSpec as P

BLOCK = 128


HIGHEST = lax.Precision.HIGHEST
CONTRACT_LAST = (((1,), (1,)), ((), ()))
MESH = pl.DeviceIdType.MESH


def passed_along(block, axis, distance):
    devices = range(lax.axis_size(axis))
    route = [((i - distance) % len(devices), i) for i in devices]
    return lax.ppermute(block, axis, route)


def routing(block_experts, own_index):
    blocks_all = block_experts.shape[0]
    capacity = blocks_all // 2
    matched = block_experts == own_index
    chosen = jnp.any(matched, axis=1)
    slot_of = matched[:, 1].astype(jnp.int32)
    order = jnp.arange(blocks_all, dtype=jnp.int32)
    position = jnp.sum((chosen[None, :] & (order[None, :] < order[:, None])).astype(jnp.int32), axis=1)
    placed = (position[None, :] == jnp.arange(capacity, dtype=jnp.int32)[:, None]) & chosen[None, :]
    placed_int = placed.astype(jnp.int32)
    list_block = jnp.sum(placed_int * jnp.arange(blocks_all, dtype=jnp.int32)[None, :], axis=1)
    list_slot = jnp.sum(placed_int * slot_of[None, :], axis=1)
    live = jnp.any(placed, axis=1)
    return list_block, list_slot, live


def layer_kernel(width, be_ref, tok_ref, dy_ref, gate_ref, w1_ref, w3_ref, w2_ref, out_ref, grad_gate_ref,
                 xb, db, gb, w1, w3, w2, xp, dp, pg, pu, dh, dpg_ref, dpu_ref, gcol, score_ref,
                 dense, cr, xs, xr, zs, ro, ri, sd, sr, szs, szr,
                 s_zi, s_zo, s_x, s_c, s_ex, s_xh, s_ch, rsem, hsem, wsem, lsem,
                 css, crs, xss, xrs, zss, ros, ris, gs, gr, gcs, gcr, gzs, gzr):
    nz, ne = 4, 4
    z = lax.axis_index("hid")
    e = lax.axis_index("exp")
    core = lax.rem(e, 2)
    side = e // 2
    mate = e + 1 - 2 * core
    across = lax.rem(e + 2, ne)
    mate_across = lax.rem(mate + 2, ne)
    upper = z // 2
    at_end = (z == 0) | (z == nz - 1)
    in_middle = (z == 1) | (z == 2)
    inward = z + 1 - 2 * upper
    outward = z - 1 + 2 * upper
    own_q = z + upper * (nz - 1 - 2 * z)
    bufs = (xb, db)
    own_refs = (tok_ref, dy_ref)
    picks = (xp, dp)
    hidden = w1.shape[2]
    tok = xb.shape[2]
    col = 256
    partners = (mate, across, mate_across)

    barrier = pltpu.get_barrier_semaphore()
    pl.semaphore_signal(barrier, inc=1, device_id={"hid": inward}, device_id_type=MESH)
    for dev in partners:
        pl.semaphore_signal(barrier, inc=1, device_id={"exp": dev}, device_id_type=MESH)

    @pl.when(in_middle)
    def _():
        pl.semaphore_signal(barrier, inc=1, device_id={"hid": outward}, device_id_type=MESH)

    def real(q):
        return q + upper * (nz - 1 - 2 * q)

    order = (own_q, 1 - own_q, 2, 3)

    def load(ref, buf, j, i, slot):
        rows = pl.ds(pl.multiple_of(real(order[i]) * width, width), width)
        src = ref.at[0, :, rows] if j == 2 else ref.at[0, rows, :]
        return pltpu.make_async_copy(src, buf.at[slot], wsem.at[slot, j])

    def load_x(i, slot):
        return load(w1_ref, w1, 0, i, slot), load(w3_ref, w3, 1, i, slot)

    def load_d(i, slot):
        return load(w2_ref, w2, 2, i, slot)

    def remote(src, dst, ssem, rsem_, dev):
        return pltpu.make_async_remote_copy(
            src_ref=src, dst_ref=dst, send_sem=ssem, recv_sem=rsem_, device_id=dev, device_id_type=MESH)

    def send(a, q, eq, ssem, dev, src=None):
        zq = real(q)
        place = bufs[a].at[zq, eq]
        return remote(place if src is None else src, place, ssem, rsem.at[a, zq, eq], dev)

    def to_in(a, q, n, src=None):
        return send(a, q, e, s_zi.at[a, n], {"hid": inward}, src)

    def to_out(a, q, n, src=None):
        return send(a, q, e, s_zo.at[a, n], {"hid": outward}, src)

    def over_x(a, q, src=None):
        return send(a, q, e, s_x.at[a, real(q)], {"exp": across}, src)

    def to_mate(a, q, eq, k, src=None):
        return send(a, q, eq, s_c.at[a, real(q), k], {"exp": mate}, src)

    def across_in(a):
        return send(a, 0, across, s_ex.at[a], {"hid": inward})

    def part_of(a, q, eq, r):
        return bufs[a].at[real(q), eq, pl.ds(r * (tok // 2), tok // 2)]

    def send_part(a, q, eq, r, ssem, rsem_, dev):
        return remote(part_of(a, q, eq, r), part_of(a, q, eq, r), ssem, rsem_, dev)

    def part_in(a, r):
        return send_part(a, 0, e, r, s_zi.at[a, 1 + r], hsem.at[a, r, 0], {"hid": inward})

    def part_out(a, r):
        return send_part(a, 3, e, r, s_zo.at[a, 2 + r], hsem.at[a, r, 0], {"hid": outward})

    def part_x(a, r):
        return send_part(a, 3, e, r, s_xh.at[a, r], hsem.at[a, r, 1], {"exp": across})

    def part_mate(a, r):
        return send_part(a, 3, across, r, s_ch.at[a, r], rsem.at[a, real(3), across], {"exp": mate})

    def across_out(a):
        return send_part(a, 3, across, 1, s_ex.at[a], hsem.at[a, 1, 1], {"hid": outward})

    def part_arrived(a, r, c):
        send_part(a, 3, across if c else e, r, s_ex.at[a], hsem.at[a, r, c], {"exp": mate}).wait_recv()

    def arrived(a, q, eq):
        send(a, q, eq, s_ex.at[a], {"exp": mate}).wait_recv()

    def gate_send(k):
        return remote(gb.at[e], gb.at[e], gs.at[k], gr.at[e], {"exp": partners[k]})

    def gate_arrived(k):
        remote(gb.at[partners[k]], gb.at[partners[k]], gs.at[k], gr.at[partners[k]], {"exp": mate}).wait_recv()

    own = (
        pltpu.make_async_copy(tok_ref, xb.at[z, e], lsem.at[0]),
        pltpu.make_async_copy(dy_ref, db.at[z, e], lsem.at[1]),
    )
    for c in own:
        c.start()
    for i in range(2):
        for c in load_x(i, i):
            c.start()
        load_d(i, i).start()

    gb[e] = jnp.concatenate([gate_ref[...].astype(jnp.float32), jnp.zeros((6, tok), jnp.float32)], axis=0)
    pl.semaphore_wait(barrier, 4 + lax.rem((z + 1) // 2, 2))

    for a in range(2):
        to_in(a, own_q, 0, own_refs[a]).start()

        @pl.when(in_middle)
        def _():
            to_out(a, own_q, 0, own_refs[a]).start()

        over_x(a, own_q, own_refs[a]).start()
        to_mate(a, own_q, e, 0, own_refs[a]).start()
    for k in range(3):
        gate_send(k).start()

    first, first_slot = jnp.int32(-1), jnp.int32(0)
    last, last_slot = jnp.int32(-1), jnp.int32(0)
    for b in range(ne):
        one, two = be_ref[0, b] == e, be_ref[1, b] == e
        here = one | two
        column = two.astype(jnp.int32)
        fresh = here & (first < 0)
        later = here & (first >= 0)
        last, last_slot = jnp.where(later, b, last), jnp.where(later, column, last_slot)
        first, first_slot = jnp.where(fresh, b, first), jnp.where(fresh, column, first_slot)
    listed = ((first, first_slot), (last, last_slot))
    homes = (e, mate, across, mate_across)
    shares = [[(block == home).astype(jnp.float32) for home in homes] for block, _ in listed]

    def pick(a, i):
        q = order[i]
        arrived(a, q, mate)
        arrived(a, q, mate_across)
        zq = real(q)
        for n, (block, _) in enumerate(listed):
            rows = bufs[a][zq, ne - 1]
            for home in range(ne - 1):
                rows = jnp.where(block == home, bufs[a][zq, home], rows)
            picks[a][n * tok : (n + 1) * tok, :] = rows

    def relay(step, a):
        @pl.when(at_end)
        def _():
            if step < 2:
                arrived(a, step + 1, e)
                over_x(a, step + 1).start()
                to_mate(a, step + 1, e, 0).start()
            if step == 2:
                part_arrived(a, 0, 0)
                part_x(a, 0).start()
            if step < 3:
                arrived(a, step, across)
                if step == 0:
                    across_in(a).start()
                to_mate(a, step, across, 1).start()
            if step == 2:
                part_arrived(a, 1, 0)
                to_mate(a, 3, e, 0).start()
            if step == 3:
                for r in range(2):
                    part_arrived(a, r, 1)
                    part_mate(a, r).start()

        if step < 3:
            @pl.when(in_middle)
            def _():
                if step == 0:
                    arrived(a, 0, e)
                    for r in range(2):
                        part_in(a, r).start()
                    to_mate(a, 0, e, 0).start()
                    arrived(a, 2, e)
                    to_out(a, 2, 1).start()
                    over_x(a, 2).start()
                    to_mate(a, 2, e, 0).start()
                    arrived(a, 1, across)
                    to_mate(a, 1, across, 1).start()
                if step == 1:
                    for r in range(2):
                        part_arrived(a, r, 0)
                        part_out(a, r).start()
                        part_x(a, r).start()
                    to_mate(a, 3, e, 0).start()
                    arrived(a, 2, across)
                    to_mate(a, 2, across, 1).start()
                    arrived(a, 0, across)
                    to_mate(a, 0, across, 1).start()
                if step == 2:
                    for r in range(2):
                        part_arrived(a, r, 1)
                    across_out(a).start()
                    to_mate(a, 3, across, 1).start()

    def forward_x(i):
        slot = i % 2
        pick(0, i)
        for c in load_x(i, slot):
            c.wait()

        for total_ref, w in ((pg, w1), (pu, w3)):
            term = jnp.dot(xp[...], w[slot], preferred_element_type=jnp.float32)
            total_ref[...] = term if i == 0 else total_ref[...] + term

        if i + 2 < nz:
            for c in load_x(i + 2, slot):
                c.start()

    def forward_d(i):
        slot = i % 2
        pick(1, i)
        load_d(i, slot).wait()

        term = lax.dot_general(dp[...], w2[slot], CONTRACT_LAST, preferred_element_type=jnp.float32)
        dh[...] = term if i == 0 else dh[...] + term

        if i + 2 < nz:
            load_d(i + 2, slot).start()

    def gate_columns():
        for k in range(3):
            gate_arrived(k)
        eye = lax.broadcasted_iota(jnp.int32, (tok, tok), 0) == lax.broadcasted_iota(jnp.int32, (tok, tok), 1)
        for n, (block, column) in enumerate(listed):
            row = jnp.zeros((1, tok), jnp.float32)
            for home in range(ne):
                for k in range(2):
                    chosen = ((block == home) & (column == k)).astype(jnp.float32)
                    row = row + chosen * gb[home, k : k + 1, :]
            col = jnp.sum(jnp.where(eye, jnp.broadcast_to(row, (tok, tok)), 0.0), axis=1, keepdims=True)
            gcol[n * tok : (n + 1) * tok, :] = jnp.broadcast_to(col, (tok, 128))

    for c in own:
        c.wait()
    score_ref[...] = jnp.zeros_like(score_ref)
    for step in range(3):
        relay(step, 0)
        forward_x(step)
        relay(step, 1)
        forward_d(step)
        if step == 0:
            gate_columns()

    WIDE = 512

    def last_dots(t):
        cols = pl.ds(t * WIDE, WIDE)
        dh[:, cols] += lax.dot_general(dp[...], w2[1, cols, :], CONTRACT_LAST, preferred_element_type=jnp.float32)

    def pointwise(t):
        for c in range(WIDE // 128):
            cols = pl.ds(t * WIDE + c * 128, 128)
            for r in range(0, 2 * tok, 64):
                rows = pl.ds(r, 64)
                g = pg[rows, cols]
                u = pu[rows, cols]
                h = dh[rows, cols]
                sig = 1.0 / (1.0 + jnp.exp(-g))
                act = g * sig
                score_ref[rows, :] += act * u * h
                scaled = gcol[rows, :] * h
                dpg_ref[rows, cols] = (scaled * u * sig * (1.0 + g * (1.0 - sig))).astype(jnp.bfloat16)
                dpu_ref[rows, cols] = (scaled * act).astype(jnp.bfloat16)

    def last_x(t):
        cols = pl.ds(t * (hidden // 2), hidden // 2)
        pg[:, cols] += jnp.dot(xp[...], w1[1, :, cols], preferred_element_type=jnp.float32)
        pu[:, cols] += jnp.dot(xp[...], w3[1, :, cols], preferred_element_type=jnp.float32)

    relay(3, 0)
    pick(0, 3)
    for c in load_x(3, 1):
        c.wait()
    last_x(0)
    relay(3, 1)
    last_x(1)
    pick(1, 3)
    load_d(3, 1).wait()
    def first_term(t):
        cols = pl.ds(t * WIDE, WIDE)
        term = lax.dot_general(dpg_ref[:, cols], w1[1, :col, cols], CONTRACT_LAST, preferred_element_type=jnp.float32)
        return term + lax.dot_general(
            dpu_ref[:, cols], w3[1, :col, cols], CONTRACT_LAST, preferred_element_type=jnp.float32)

    last_dots(0)
    last_dots(1)
    pointwise(0)
    grad = first_term(0)
    for t in range(2, hidden // WIDE):
        last_dots(t)
        pointwise(t - 1)
        grad += first_term(t - 1)
    pointwise(hidden // WIDE - 1)
    grad += first_term(hidden // WIDE - 1)

    def again(j, slot):
        zq = real(own_q + (3 - j) * (1 - 2 * own_q))
        rows = pl.ds(pl.multiple_of(zq * width, width), width)
        return (
            pltpu.make_async_copy(w1_ref.at[0, rows, :], w1.at[slot], wsem.at[slot, 0]),
            pltpu.make_async_copy(w3_ref.at[0, rows, :], w3.at[slot], wsem.at[slot, 1]),
        )

    def core_send(p, n):
        return remote(dense.at[pl.ds(p, n), 1], cr.at[pl.ds(p, n)], css.at[p], crs.at[p], {"exp": mate})

    def x_send(p, n):
        return remote(xs.at[pl.ds(p, n)], xr.at[pl.ds(p, n)], xss.at[p], xrs.at[p], {"exp": across})

    def from_end(k):
        return remote(zs.at[k], ro.at[k], zss.at[k], ros.at[k], {"hid": inward})

    def from_middle(k):
        return remote(zs.at[k], ri.at[k], zss.at[k], ris.at[k], {"hid": inward})

    def to_end(k):
        return remote(zs.at[k], ri.at[k], zss.at[k], ris.at[k], {"hid": outward})

    def spread(p, grad):
        for c in range(2):
            for far in range(2):
                home = c + 2 * far
                dense[p, c, far] = (shares[0][home] * grad[:tok] + shares[1][home] * grad[tok:]).astype(jnp.bfloat16)

    def product(slot, rows):
        grad = lax.dot_general(dpg_ref[...], w1[slot, rows, :], CONTRACT_LAST, preferred_element_type=jnp.float32)
        return grad + lax.dot_general(dpu_ref[...], w3[slot, rows, :], CONTRACT_LAST, preferred_element_type=jnp.float32)

    def multiply(k):
        j = k // 2
        slot = lax.rem(j + 1, 2)

        @pl.when((lax.rem(k, 2) == 0) & (j >= 2))
        def _():
            for c in again(j, slot):
                c.wait()

        grad = product(slot, pl.ds(pl.multiple_of(lax.rem(k, 2) * 2 * col, 2 * col), 2 * col))
        for i in range(2):
            spread(2 * k + i, grad[:, i * col : (i + 1) * col])
        core_send(2 * k, 2).start()

        @pl.when(k == 3)
        def _():
            for c in again(3, 0):
                c.start()

    def to_x(p, n):
        core_send(p, n).wait_recv()
        part = pl.ds(p, n)
        xs[part] = (dense[part, 0, 1].astype(jnp.float32) + cr[part, 1].astype(jnp.float32)).astype(jnp.bfloat16)
        x_send(p, n).start()

    def total(k):
        @pl.when(k < 2)
        def _():
            for i in range(2):
                x_send(2 * k + i, 1).wait_recv()

        @pl.when(k >= 2)
        def _():
            x_send(2 * k, 2).wait_recv()

        part = pl.ds(2 * k, 2)
        return dense[part, 0, 0].astype(jnp.float32) + cr[part, 0].astype(jnp.float32) + xr[part].astype(jnp.float32)

    def end_to_z(k):
        zs[k] = total(k).astype(jnp.bfloat16)
        from_end(k).start()

    def middle_to_z(k):
        share = total(k)

        @pl.when(k < 4)
        def _():
            from_end(k).wait_recv()
            zs[k] = (share + ro[k].astype(jnp.float32)).astype(jnp.bfloat16)
            from_middle(k).start()

        @pl.when(k >= 4)
        def _():
            from_middle(k - 4).wait_recv()
            zs[k] = (share + ri[k - 4].astype(jnp.float32)).astype(jnp.bfloat16)
            to_end(k).start()

    def score_send(k):
        return remote(sd.at[k + 1], sr.at[k], gcs.at[k], gcr.at[k], {"exp": partners[k]})

    def score_in():
        return remote(szs.at[0], szr.at[upper], gzs.at[0], gzr.at[0], {"hid": inward})

    def scores_from_middle():
        return remote(szs.at[0], szr.at[2], gzs.at[0], gzr.at[1], {"hid": inward})

    def scores_out():
        return remote(szs.at[1], szr.at[2], gzs.at[1], gzr.at[1], {"hid": outward})

    spread(0, grad)
    core_send(0, 1).start()

    @pl.loop(1, 4)
    def _(p):
        spread(p, product(1, pl.ds(pl.multiple_of(p * col, col), col)))
        core_send(p, 1).start()
        to_x(p - 1, 1)

    for c in again(2, 1):
        c.start()

    @pl.loop(2, 8)
    def _(k):
        multiply(k)

        @pl.when(k == 2)
        def _():
            to_x(3, 1)

        @pl.when(k > 2)
        def _():
            to_x(2 * k - 2, 2)

        @pl.when(k == 3)
        def _():
            eye = lax.broadcasted_iota(jnp.int32, (tok, tok), 0) == lax.broadcasted_iota(jnp.int32, (tok, tok), 1)
            line = lax.broadcasted_iota(jnp.int32, (8, tok), 0)
            placed = []
            for n, (_, column) in enumerate(listed):
                tall = jnp.sum(score_ref[n * tok : (n + 1) * tok, :], axis=1, keepdims=True)
                row = jnp.sum(jnp.where(eye, jnp.broadcast_to(tall, (tok, tok)), 0.0), axis=0, keepdims=True)
                placed.append(jnp.where(line == column, jnp.broadcast_to(row, (8, tok)), 0.0))
            for i in range(ne):
                sd[i] = shares[0][i] * placed[0] + shares[1][i] * placed[1]
            for i in range(3):
                score_send(i).start()

        @pl.when(at_end & (k >= 5))
        def _():
            end_to_z(k - 5)

        @pl.when(in_middle & (k >= 6))
        def _():
            middle_to_z(k - 6)

    to_x(14, 2)
    mine = sd[0]
    for i in range(3):
        score_send(i).wait_recv()
        mine += sr[i]

    @pl.when(at_end)
    def _():
        szs[0] = mine
        score_in().start()

        @pl.loop(3, 6)
        def _(k):
            end_to_z(k)

    @pl.when(in_middle)
    def _():
        middle_to_z(2)
        score_in().wait_recv()
        szs[0] = mine + szr[upper]
        scores_from_middle().start()

        @pl.loop(3, 6)
        def _(k):
            middle_to_z(k)

        scores_from_middle().wait_recv()
        szs[1] = szs[0] + szr[2]
        scores_out().start()
        grad_gate_ref[...] = szs[1, :2]

    for k in (6, 7):
        share = total(k)

        @pl.when(at_end)
        def _():
            to_end(k - 2).wait_recv()
            done = share + ri[k - 2].astype(jnp.float32)
            for i in range(2):
                cols = pl.ds((2 * (k - 6) + i) * col, col)
                out_ref[:, cols] = done[i].astype(jnp.bfloat16)

        @pl.when(in_middle)
        def _():
            from_end(k - 2).wait_recv()
            from_middle(k - 4).wait_recv()
            done = share + ro[k - 2].astype(jnp.float32) + ri[k - 4].astype(jnp.float32)
            for i in range(2):
                cols = pl.ds((2 * (k - 6) + i) * col, col)
                out_ref[:, cols] = done[i].astype(jnp.bfloat16)

    @pl.when(at_end)
    def _():
        scores_out().wait_recv()
        grad_gate_ref[...] = szr[2, :2]
        score_in().wait_send()

    @pl.when(in_middle)
    def _():
        scores_from_middle().wait_send()
        scores_out().wait_send()

    for k in range(3):
        gate_send(k).wait_send()
        score_send(k).wait_send()

    @pl.loop(0, 4)
    def _(p):
        core_send(p, 1).wait_send()
        x_send(p, 1).wait_send()

    @pl.loop(2, 8)
    def _(k):
        core_send(2 * k, 2).wait_send()
        x_send(2 * k, 2).wait_send()
        from_end(k - 2).wait_send()

    for a in range(2):
        to_in(a, own_q, 0).wait_send()

        @pl.when(at_end)
        def _():
            across_in(a).wait_send()
            for q in range(3):
                over_x(a, q).wait_send()
                to_mate(a, q, across, 1).wait_send()
            part_x(a, 0).wait_send()
            for r in range(2):
                part_mate(a, r).wait_send()

        @pl.when(in_middle)
        def _():
            to_out(a, 1, 0).wait_send()
            to_out(a, 2, 1).wait_send()
            over_x(a, 1).wait_send()
            over_x(a, 2).wait_send()
            for r in range(2):
                part_in(a, r).wait_send()
                part_out(a, r).wait_send()
                part_x(a, r).wait_send()
            across_out(a).wait_send()
            for q in range(4):
                to_mate(a, q, across, 1).wait_send()

        for q in range(4):
            to_mate(a, q, e, 0).wait_send()


def layer(block_experts, tokens, grad_out, gates, w_gate, w_up, w_down):
    nz, ne = 4, 4
    tok, width = tokens.shape
    hidden = w_gate.shape[2]
    used = 2 * BLOCK
    hbm = pl.BlockSpec(memory_space=pl.ANY)
    vmem = pl.BlockSpec(memory_space=pltpu.VMEM)
    smem = pl.BlockSpec(memory_space=pltpu.SMEM)
    bf16, f32 = jnp.bfloat16, jnp.float32
    dma = pltpu.SemaphoreType.DMA
    return pl.pallas_call(
        functools.partial(layer_kernel, width),
        out_shape=(
            pltpu.VMEM((tok, width), bf16),
            pltpu.VMEM((2, tok), f32),
        ),
        in_specs=[smem, hbm, hbm, vmem, hbm, hbm, hbm],
        out_specs=(vmem, vmem),
        scratch_shapes=[
            pltpu.VMEM((nz, ne, tok, width), bf16),
            pltpu.VMEM((nz, ne, tok, width), bf16),
            pltpu.VMEM((ne, 8, tok), f32),
            pltpu.VMEM((2, width, hidden), bf16),
            pltpu.VMEM((2, width, hidden), bf16),
            pltpu.VMEM((2, hidden, width), bf16),
            pltpu.VMEM((used, width), bf16),
            pltpu.VMEM((used, width), bf16),
            pltpu.VMEM((used, hidden), f32),
            pltpu.VMEM((used, hidden), f32),
            pltpu.VMEM((used, hidden), f32),
            pltpu.VMEM((used, hidden), bf16),
            pltpu.VMEM((used, hidden), bf16),
            pltpu.VMEM((used, 128), f32),
            pltpu.VMEM((used, 128), f32),
            pltpu.VMEM((16, 2, 2, tok, 256), bf16),
            pltpu.VMEM((16, 2, tok, 256), bf16),
            pltpu.VMEM((16, tok, 256), bf16),
            pltpu.VMEM((16, tok, 256), bf16),
            pltpu.VMEM((6, 2, tok, 256), bf16),
            pltpu.VMEM((6, 2, tok, 256), bf16),
            pltpu.VMEM((6, 2, tok, 256), bf16),
            pltpu.VMEM((ne, 8, tok), f32),
            pltpu.VMEM((3, 8, tok), f32),
            pltpu.VMEM((2, 8, tok), f32),
            pltpu.VMEM((3, 8, tok), f32),
            dma((2, 3)),
            dma((2, 4)),
            dma((2, nz)),
            dma((2, nz, 2)),
            dma((2,)),
            dma((2, 2)),
            dma((2, 2)),
            dma((2, nz, ne)),
            dma((2, 2, 2)),
            dma((2, 3)),
            dma((2,)),
            dma((16,)),
            dma((16,)),
            dma((16,)),
            dma((16,)),
            dma((6,)),
            dma((6,)),
            dma((6,)),
            dma((3,)),
            dma((ne,)),
            dma((3,)),
            dma((3,)),
            dma((2,)),
            dma((2,)),
        ],
        compiler_params=pltpu.CompilerParams(
            collective_id=0, has_side_effects=True, vmem_limit_bytes=60 * 1024 * 1024
        ),
        name="layer",
    )(block_experts, tokens, grad_out, gates, w_gate, w_up, w_down)


def finish_kernel(grad_ref, gate_ref, grad_out_ref, gate_out_ref, sems):
    copies = (
        pltpu.make_async_copy(grad_ref, grad_out_ref, sems.at[0]),
        pltpu.make_async_copy(gate_ref, gate_out_ref, sems.at[1]),
    )
    for c in copies:
        c.start()
    for c in copies:
        c.wait()


def finish(grad, gate_rows):
    vmem = pl.BlockSpec(memory_space=pltpu.VMEM)
    hbm = pl.BlockSpec(memory_space=pl.ANY)
    return pl.pallas_call(
        finish_kernel,
        out_shape=(
            jax.ShapeDtypeStruct(grad.shape, grad.dtype),
            jax.ShapeDtypeStruct(gate_rows.shape, gate_rows.dtype),
        ),
        in_specs=[vmem, vmem],
        out_specs=(hbm, hbm),
        scratch_shapes=[pltpu.SemaphoreType.DMA((2,))],
        compiler_params=pltpu.CompilerParams(vmem_limit_bytes=1024 * 1024),
        name="finish",
    )(grad, gate_rows)


def fast_local(tokens, grad_out, gates, block_experts, w_gate, w_up, w_down):
    grad, gate_rows = layer(block_experts.T, tokens, grad_out, gates.T, w_gate, w_up, w_down)
    grad, gate_rows = finish(grad, gate_rows)
    return grad, gate_rows.T


def combined(owned, score, list_block, live, slot_hot, tok_dev, width_dev, capacity):
    n_experts = lax.axis_size("exp")
    own_index = lax.axis_index("exp")
    per_home = tok_dev // BLOCK
    result_cols = owned.reshape(width_dev, capacity, BLOCK)
    score_blocks = score.reshape(capacity, BLOCK)

    def share(home):
        wanted = home * per_home + jnp.arange(per_home, dtype=jnp.int32)
        select = ((list_block[None, :] == wanted[:, None]) & live[None, :]).astype(jnp.float32)
        grad_part = jnp.einsum("bi,dir->dbr", select, result_cols, precision=HIGHEST).reshape(
            width_dev, tok_dev
        )
        gate_part = jnp.einsum(
            "bi,ik,ir->kbr", select, slot_hot, score_blocks, precision=HIGHEST
        ).reshape(2, tok_dev)
        return (grad_part, gate_part)

    zero_totals = (
        jnp.zeros((width_dev, tok_dev), jnp.float32),
        jnp.zeros((2, tok_dev), jnp.float32),
    )

    def single_turn(step, totals):
        grad_part, gate_part = share((own_index + 1 + step) % n_experts)
        return passed_along((totals[0] + grad_part, totals[1] + gate_part), "exp", -1)

    totals = lax.fori_loop(0, n_experts - 1, single_turn, zero_totals)
    grad_part, gate_part = share(own_index)
    grad_total = totals[0] + grad_part
    gate_total = totals[1] + gate_part
    return (grad_total.T.astype(jnp.bfloat16), gate_total.T)


def local(tokens, grad_out, gates, block_experts, w_gate, w_up, w_down):
    own_index = lax.axis_index("exp")
    tok_dev, width_dev = tokens.shape
    blocks_all = block_experts.shape[0]
    capacity = blocks_all // 2
    used_count = capacity * BLOCK
    list_block, list_slot, live = routing(block_experts, own_index)
    row_index = (list_block[:, None] * BLOCK + jnp.arange(BLOCK, dtype=jnp.int32)[None, :]).reshape(
        used_count
    )
    x_home, dy_home, gate_home = (
        lax.all_gather(tokens, "exp", axis=0, tiled=True),
        lax.all_gather(grad_out, "exp", axis=0, tiled=True),
        lax.all_gather(gates, "exp", axis=0, tiled=True),
    )
    gate_pick = (
        jnp.take(gate_home, row_index, axis=0).astype(jnp.float32).reshape(capacity, BLOCK, 2)
    )
    slot_hot = (list_slot[:, None] == jnp.arange(2, dtype=jnp.int32)[None, :]).astype(jnp.float32)
    slot_hot = slot_hot * live[:, None].astype(jnp.float32)
    gate_column = jnp.sum(gate_pick * slot_hot[:, None, :], axis=2).reshape(used_count)
    x_piece = jnp.take(lax.all_gather(x_home, "hid", axis=1, tiled=True), row_index, axis=0)
    dy_piece = jnp.take(lax.all_gather(dy_home, "hid", axis=1, tiled=True), row_index, axis=0)
    pre_gate = jnp.dot(x_piece, w_gate[0], preferred_element_type=jnp.float32)
    pre_up = jnp.dot(x_piece, w_up[0], preferred_element_type=jnp.float32)
    d_hidden = lax.dot_general(dy_piece, w_down[0], CONTRACT_LAST, preferred_element_type=jnp.float32)
    sigmoid_gate = jax.nn.sigmoid(pre_gate)
    activated = pre_gate * sigmoid_gate
    score_part = jnp.sum(activated * pre_up * d_hidden, axis=1)
    score = lax.psum(score_part, "hid")
    scaled = gate_column[:, None] * d_hidden
    d_pre_gate = (scaled * pre_up * sigmoid_gate * (1.0 + pre_gate * (1.0 - sigmoid_gate))).astype(
        jnp.bfloat16
    )
    d_pre_up = (scaled * activated).astype(jnp.bfloat16)
    first = lax.dot_general(w_gate[0], d_pre_gate, CONTRACT_LAST, preferred_element_type=jnp.float32)
    owned = lax.psum_scatter(
        first
        + lax.dot_general(w_up[0], d_pre_up, CONTRACT_LAST, preferred_element_type=jnp.float32),
        "hid",
        scatter_dimension=0,
        tiled=True,
    )
    return combined(owned, score, list_block, live, slot_hot, tok_dev, width_dev, capacity)


def solution(mesh):
    placed = (
        P(("grp", "exp"), "hid"),
        P(("grp", "exp"), "hid"),
        P(("grp", "exp"), None),
        P("grp", None),
        P("exp", None, "hid"),
        P("exp", None, "hid"),
        P("exp", "hid", None),
    )
    body = fast_local if (mesh.shape["exp"], mesh.shape["hid"]) == (4, 4) else local
    return jax.shard_map(
        body,
        mesh=mesh,
        in_specs=placed,
        out_specs=(P(("grp", "exp"), "hid"), P(("grp", "exp"), None)),
        check_vma=False,
    )
```

```python
import functools
import jax
import jax.numpy as jnp
from jax import lax
from jax.experimental import pallas as pl
from jax.experimental.pallas import tpu as pltpu
from jax.sharding import PartitionSpec as P

BLOCK = 128


HIGHEST = lax.Precision.HIGHEST
CONTRACT_LAST = (((1,), (1,)), ((), ()))
MESH = pl.DeviceIdType.MESH


def passed_along(block, axis, distance):
    devices = range(lax.axis_size(axis))
    route = [((i - distance) % len(devices), i) for i in devices]
    return lax.ppermute(block, axis, route)


def routing(block_experts, own_index):
    blocks_all = block_experts.shape[0]
    capacity = blocks_all // 2
    matched = block_experts == own_index
    chosen = jnp.any(matched, axis=1)
    slot_of = matched[:, 1].astype(jnp.int32)
    order = jnp.arange(blocks_all, dtype=jnp.int32)
    position = jnp.sum((chosen[None, :] & (order[None, :] < order[:, None])).astype(jnp.int32), axis=1)
    placed = (position[None, :] == jnp.arange(capacity, dtype=jnp.int32)[:, None]) & chosen[None, :]
    placed_int = placed.astype(jnp.int32)
    list_block = jnp.sum(placed_int * jnp.arange(blocks_all, dtype=jnp.int32)[None, :], axis=1)
    list_slot = jnp.sum(placed_int * slot_of[None, :], axis=1)
    live = jnp.any(placed, axis=1)
    return list_block, list_slot, live


def layer_kernel(width, be_ref, tok_ref, dy_ref, gate_ref, w1_ref, w3_ref, w2_ref, out_ref, grad_gate_ref,
                 xb, db, gb, w1, w3, w2, xp, dp, pg, pu, dh, dpg_ref, dpu_ref, gcol, score_ref,
                 dense, cr, xs, xr, zs, ro, ri, sd, sr, szs, szr,
                 s_zi, s_zo, s_x, s_c, s_ex, s_xh, s_ch, rsem, hsem, wsem, lsem,
                 css, crs, xss, xrs, zss, ros, ris, gs, gr, gcs, gcr, gzs, gzr):
    nz, ne = 4, 4
    z = lax.axis_index("hid")
    e = lax.axis_index("exp")
    core = lax.rem(e, 2)
    side = e // 2
    mate = e + 1 - 2 * core
    across = lax.rem(e + 2, ne)
    mate_across = lax.rem(mate + 2, ne)
    upper = z // 2
    at_end = (z == 0) | (z == nz - 1)
    in_middle = (z == 1) | (z == 2)
    inward = z + 1 - 2 * upper
    outward = z - 1 + 2 * upper
    own_q = z + upper * (nz - 1 - 2 * z)
    bufs = (xb, db)
    own_refs = (tok_ref, dy_ref)
    picks = (xp, dp)
    hidden = w1.shape[2]
    tok = xb.shape[2]
    col = 256
    parts = 6
    partners = (mate, across, mate_across)

    barrier = pltpu.get_barrier_semaphore()
    pl.semaphore_signal(barrier, inc=1, device_id={"hid": inward}, device_id_type=MESH)
    for dev in partners:
        pl.semaphore_signal(barrier, inc=1, device_id={"exp": dev}, device_id_type=MESH)

    @pl.when(in_middle)
    def _():
        pl.semaphore_signal(barrier, inc=1, device_id={"hid": outward}, device_id_type=MESH)

    def real(q):
        return q + upper * (nz - 1 - 2 * q)

    order = (own_q, 1 - own_q, 2, 3)

    def load(ref, buf, j, i, slot):
        rows = pl.ds(pl.multiple_of(real(order[i]) * width, width), width)
        src = ref.at[0, :, rows] if j == 2 else ref.at[0, rows, :]
        return pltpu.make_async_copy(src, buf.at[slot], wsem.at[slot, j])

    def load_x(i, slot):
        return load(w1_ref, w1, 0, i, slot), load(w3_ref, w3, 1, i, slot)

    def load_d(i, slot):
        return load(w2_ref, w2, 2, i, slot)

    def remote(src, dst, ssem, rsem_, dev):
        return pltpu.make_async_remote_copy(
            src_ref=src, dst_ref=dst, send_sem=ssem, recv_sem=rsem_, device_id=dev, device_id_type=MESH)

    def send(a, q, eq, ssem, dev, src=None):
        zq = real(q)
        place = bufs[a].at[zq, eq]
        return remote(place if src is None else src, place, ssem, rsem.at[a, zq, eq], dev)

    def to_in(a, q, n, src=None):
        return send(a, q, e, s_zi.at[a, n], {"hid": inward}, src)

    def to_out(a, q, n, src=None):
        return send(a, q, e, s_zo.at[a, n], {"hid": outward}, src)

    def over_x(a, q, src=None):
        return send(a, q, e, s_x.at[a, real(q)], {"exp": across}, src)

    def to_mate(a, q, eq, k, src=None):
        return send(a, q, eq, s_c.at[a, real(q), k], {"exp": mate}, src)

    def across_in(a):
        return send(a, 0, across, s_ex.at[a], {"hid": inward})

    def part_of(a, q, eq, r):
        return bufs[a].at[real(q), eq, pl.ds(r * (tok // 2), tok // 2)]

    def send_part(a, q, eq, r, ssem, rsem_, dev):
        return remote(part_of(a, q, eq, r), part_of(a, q, eq, r), ssem, rsem_, dev)

    def part_in(a, r):
        return send_part(a, 0, e, r, s_zi.at[a, 1 + r], hsem.at[a, r, 0], {"hid": inward})

    def part_out(a, r):
        return send_part(a, 3, e, r, s_zo.at[a, 2 + r], hsem.at[a, r, 0], {"hid": outward})

    def part_x(a, r):
        return send_part(a, 3, e, r, s_xh.at[a, r], hsem.at[a, r, 1], {"exp": across})

    def part_mate(a, r):
        return send_part(a, 3, across, r, s_ch.at[a, r], rsem.at[a, real(3), across], {"exp": mate})

    def across_out(a):
        return send_part(a, 3, across, 1, s_ex.at[a], hsem.at[a, 1, 1], {"hid": outward})

    def part_arrived(a, r, c):
        send_part(a, 3, across if c else e, r, s_ex.at[a], hsem.at[a, r, c], {"exp": mate}).wait_recv()

    def arrived(a, q, eq):
        send(a, q, eq, s_ex.at[a], {"exp": mate}).wait_recv()

    def gate_send(k):
        return remote(gb.at[e], gb.at[e], gs.at[k], gr.at[e], {"exp": partners[k]})

    def gate_arrived(k):
        remote(gb.at[partners[k]], gb.at[partners[k]], gs.at[k], gr.at[partners[k]], {"exp": mate}).wait_recv()

    own = (
        pltpu.make_async_copy(tok_ref, xb.at[z, e], lsem.at[0]),
        pltpu.make_async_copy(dy_ref, db.at[z, e], lsem.at[1]),
    )
    for c in own:
        c.start()
    for i in range(2):
        for c in load_x(i, i):
            c.start()
        load_d(i, i).start()

    gb[e] = jnp.concatenate([gate_ref[...].astype(jnp.float32), jnp.zeros((6, tok), jnp.float32)], axis=0)
    pl.semaphore_wait(barrier, 4 + lax.rem((z + 1) // 2, 2))

    for a in range(2):
        to_in(a, own_q, 0, own_refs[a]).start()

        @pl.when(in_middle)
        def _():
            to_out(a, own_q, 0, own_refs[a]).start()

        over_x(a, own_q, own_refs[a]).start()
        to_mate(a, own_q, e, 0, own_refs[a]).start()
    for k in range(3):
        gate_send(k).start()

    first, first_slot = jnp.int32(-1), jnp.int32(0)
    last, last_slot = jnp.int32(-1), jnp.int32(0)
    for b in range(ne):
        one, two = be_ref[0, b] == e, be_ref[1, b] == e
        here = one | two
        column = two.astype(jnp.int32)
        fresh = here & (first < 0)
        later = here & (first >= 0)
        last, last_slot = jnp.where(later, b, last), jnp.where(later, column, last_slot)
        first, first_slot = jnp.where(fresh, b, first), jnp.where(fresh, column, first_slot)
    listed = ((first, first_slot), (last, last_slot))
    homes = (e, mate, across, mate_across)
    shares = [[(block == home).astype(jnp.float32) for home in homes] for block, _ in listed]

    def pick(a, i):
        q = order[i]
        arrived(a, q, mate)
        arrived(a, q, mate_across)
        zq = real(q)
        for n, (block, _) in enumerate(listed):
            rows = bufs[a][zq, ne - 1]
            for home in range(ne - 1):
                rows = jnp.where(block == home, bufs[a][zq, home], rows)
            picks[a][n * tok : (n + 1) * tok, :] = rows

    def relay(step, a):
        @pl.when(at_end)
        def _():
            if step < 2:
                arrived(a, step + 1, e)
                over_x(a, step + 1).start()
                to_mate(a, step + 1, e, 0).start()
            if step == 2:
                part_arrived(a, 0, 0)
                part_x(a, 0).start()
            if step < 3:
                arrived(a, step, across)
                if step == 0:
                    across_in(a).start()
                to_mate(a, step, across, 1).start()
            if step == 2:
                part_arrived(a, 1, 0)
                to_mate(a, 3, e, 0).start()
            if step == 3:
                for r in range(2):
                    part_arrived(a, r, 1)
                    part_mate(a, r).start()

        if step < 3:
            @pl.when(in_middle)
            def _():
                if step == 0:
                    arrived(a, 0, e)
                    for r in range(2):
                        part_in(a, r).start()
                    to_mate(a, 0, e, 0).start()
                    arrived(a, 2, e)
                    to_out(a, 2, 1).start()
                    over_x(a, 2).start()
                    to_mate(a, 2, e, 0).start()
                    arrived(a, 1, across)
                    to_mate(a, 1, across, 1).start()
                if step == 1:
                    for r in range(2):
                        part_arrived(a, r, 0)
                        part_out(a, r).start()
                        part_x(a, r).start()
                    to_mate(a, 3, e, 0).start()
                    arrived(a, 2, across)
                    to_mate(a, 2, across, 1).start()
                    arrived(a, 0, across)
                    to_mate(a, 0, across, 1).start()
                if step == 2:
                    for r in range(2):
                        part_arrived(a, r, 1)
                    across_out(a).start()
                    to_mate(a, 3, across, 1).start()

    def forward_x(i):
        slot = i % 2
        pick(0, i)
        for c in load_x(i, slot):
            c.wait()

        for total_ref, w in ((pg, w1), (pu, w3)):
            term = jnp.dot(xp[...], w[slot], preferred_element_type=jnp.float32)
            total_ref[...] = term if i == 0 else total_ref[...] + term

        if i + 2 < nz:
            for c in load_x(i + 2, slot):
                c.start()

    def forward_d(i):
        slot = i % 2
        pick(1, i)
        load_d(i, slot).wait()

        term = lax.dot_general(dp[...], w2[slot], CONTRACT_LAST, preferred_element_type=jnp.float32)
        dh[...] = term if i == 0 else dh[...] + term

        if i + 2 < nz:
            load_d(i + 2, slot).start()

    def gate_columns():
        for k in range(3):
            gate_arrived(k)
        eye = lax.broadcasted_iota(jnp.int32, (tok, tok), 0) == lax.broadcasted_iota(jnp.int32, (tok, tok), 1)
        for n, (block, column) in enumerate(listed):
            row = jnp.zeros((1, tok), jnp.float32)
            for home in range(ne):
                for k in range(2):
                    chosen = ((block == home) & (column == k)).astype(jnp.float32)
                    row = row + chosen * gb[home, k : k + 1, :]
            col = jnp.sum(jnp.where(eye, jnp.broadcast_to(row, (tok, tok)), 0.0), axis=1, keepdims=True)
            gcol[n * tok : (n + 1) * tok, :] = jnp.broadcast_to(col, (tok, 128))

    for c in own:
        c.wait()
    score_ref[...] = jnp.zeros_like(score_ref)
    for step in range(3):
        relay(step, 0)
        forward_x(step)
        relay(step, 1)
        forward_d(step)
        if step == 0:
            gate_columns()

    WIDE = 512

    def last_dots(t):
        cols = pl.ds(t * WIDE, WIDE)
        dh[:, cols] += lax.dot_general(dp[...], w2[1, cols, :], CONTRACT_LAST, preferred_element_type=jnp.float32)

    def pointwise(t):
        for c in range(WIDE // 128):
            cols = pl.ds(t * WIDE + c * 128, 128)
            for r in range(0, 2 * tok, 64):
                rows = pl.ds(r, 64)
                g = pg[rows, cols]
                u = pu[rows, cols]
                h = dh[rows, cols]
                sig = 1.0 / (1.0 + jnp.exp(-g))
                act = g * sig
                score_ref[rows, :] += act * u * h
                scaled = gcol[rows, :] * h
                dpg_ref[rows, cols] = (scaled * u * sig * (1.0 + g * (1.0 - sig))).astype(jnp.bfloat16)
                dpu_ref[rows, cols] = (scaled * act).astype(jnp.bfloat16)

    def last_x(t):
        cols = pl.ds(t * (hidden // 2), hidden // 2)
        pg[:, cols] += jnp.dot(xp[...], w1[1, :, cols], preferred_element_type=jnp.float32)
        pu[:, cols] += jnp.dot(xp[...], w3[1, :, cols], preferred_element_type=jnp.float32)

    relay(3, 0)
    pick(0, 3)
    for c in load_x(3, 1):
        c.wait()
    last_x(0)
    relay(3, 1)
    last_x(1)
    pick(1, 3)
    load_d(3, 1).wait()
    def first_term(t):
        cols = pl.ds(t * WIDE, WIDE)
        term = lax.dot_general(dpg_ref[:, cols], w1[1, :col, cols], CONTRACT_LAST, preferred_element_type=jnp.float32)
        return term + lax.dot_general(
            dpu_ref[:, cols], w3[1, :col, cols], CONTRACT_LAST, preferred_element_type=jnp.float32)

    last_dots(0)
    last_dots(1)
    pointwise(0)
    grad = first_term(0)
    for t in range(2, hidden // WIDE):
        last_dots(t)
        pointwise(t - 1)
        grad += first_term(t - 1)
    pointwise(hidden // WIDE - 1)
    grad += first_term(hidden // WIDE - 1)

    def again(j, slot):
        zq = real(own_q + (3 - j) * (1 - 2 * own_q))
        rows = pl.ds(pl.multiple_of(zq * width, width), width)
        return (
            pltpu.make_async_copy(w1_ref.at[0, rows, :], w1.at[slot], wsem.at[slot, 0]),
            pltpu.make_async_copy(w3_ref.at[0, rows, :], w3.at[slot], wsem.at[slot, 1]),
        )

    def core_send(p, n):
        return remote(dense.at[pl.ds(p, n), 1], cr.at[pl.ds(p, n)], css.at[p], crs.at[p], {"exp": mate})

    def x_send(p, n):
        return remote(xs.at[pl.ds(p, n)], xr.at[pl.ds(p, n)], xss.at[p], xrs.at[p], {"exp": across})

    def from_end(k):
        return remote(zs.at[k], ro.at[k], zss.at[k], ros.at[k], {"hid": inward})

    def from_middle(k):
        return remote(zs.at[k], ri.at[k], zss.at[k], ris.at[k], {"hid": inward})

    def to_end(k):
        return remote(zs.at[k], ri.at[k], zss.at[k], ris.at[k], {"hid": outward})

    def spread(p, grad):
        for c in range(2):
            for far in range(2):
                home = c + 2 * far
                dense[p, c, far] = (shares[0][home] * grad[:tok] + shares[1][home] * grad[tok:]).astype(jnp.bfloat16)

    def product(slot, rows):
        grad = lax.dot_general(dpg_ref[...], w1[slot, rows, :], CONTRACT_LAST, preferred_element_type=jnp.float32)
        return grad + lax.dot_general(dpu_ref[...], w3[slot, rows, :], CONTRACT_LAST, preferred_element_type=jnp.float32)

    def multiply(k):
        j = k // 2
        slot = lax.rem(j + 1, 2)

        @pl.when((lax.rem(k, 2) == 0) & (j >= 2))
        def _():
            for c in again(j, slot):
                c.wait()

        grad = product(slot, pl.ds(pl.multiple_of(lax.rem(k, 2) * 2 * col, 2 * col), 2 * col))
        for i in range(2):
            spread(2 * k + i, grad[:, i * col : (i + 1) * col])
        core_send(2 * k, 2).start()

        @pl.when(k == 3)
        def _():
            for c in again(3, 0):
                c.start()

    def to_x(p, n):
        core_send(p, n).wait_recv()
        part = pl.ds(p, n)
        xs[part] = (dense[part, 0, 1].astype(jnp.float32) + cr[part, 1].astype(jnp.float32)).astype(jnp.bfloat16)
        x_send(p, n).start()

    def total(k):
        @pl.when(k < parts // 2)
        def _():
            for i in range(2):
                x_send(2 * k + i, 1).wait_recv()

        @pl.when(k >= parts // 2)
        def _():
            x_send(2 * k, 2).wait_recv()

        part = pl.ds(2 * k, 2)
        return dense[part, 0, 0].astype(jnp.float32) + cr[part, 0].astype(jnp.float32) + xr[part].astype(jnp.float32)

    def end_to_z(k):
        zs[k] = total(k).astype(jnp.bfloat16)
        from_end(k).start()

    def middle_to_z(k):
        share = total(k)

        @pl.when(k < 4)
        def _():
            from_end(k).wait_recv()
            zs[k] = (share + ro[k].astype(jnp.float32)).astype(jnp.bfloat16)
            from_middle(k).start()

        @pl.when(k >= 4)
        def _():
            from_middle(k - 4).wait_recv()
            zs[k] = (share + ri[k - 4].astype(jnp.float32)).astype(jnp.bfloat16)
            to_end(k).start()

    def score_send(k):
        return remote(sd.at[k + 1], sr.at[k], gcs.at[k], gcr.at[k], {"exp": partners[k]})

    def score_in():
        return remote(szs.at[0], szr.at[upper], gzs.at[0], gzr.at[0], {"hid": inward})

    def scores_from_middle():
        return remote(szs.at[0], szr.at[2], gzs.at[0], gzr.at[1], {"hid": inward})

    def scores_out():
        return remote(szs.at[1], szr.at[2], gzs.at[1], gzr.at[1], {"hid": outward})

    spread(0, grad)
    core_send(0, 1).start()

    @pl.loop(1, parts)
    def _(p):
        rows = pl.ds(pl.multiple_of(lax.rem(p, 4) * col, col), col)
        spread(p, product(1 - p // 4, rows))
        core_send(p, 1).start()
        to_x(p - 1, 1)

        @pl.when(p == 3)
        def _():
            for c in again(2, 1):
                c.start()

    @pl.when(at_end)
    def _():
        end_to_z(0)

    @pl.loop(parts // 2, 8)
    def _(k):
        multiply(k)

        @pl.when(k == parts // 2)
        def _():
            to_x(parts - 1, 1)

        @pl.when(k > parts // 2)
        def _():
            to_x(2 * k - 2, 2)

        @pl.when(at_end & (lax.rem(k, 3) > 0))
        def _():
            end_to_z((2 * k - 4) // 3)

        @pl.when(k == 4)
        def _():
            eye = lax.broadcasted_iota(jnp.int32, (tok, tok), 0) == lax.broadcasted_iota(jnp.int32, (tok, tok), 1)
            line = lax.broadcasted_iota(jnp.int32, (8, tok), 0)
            placed = []
            for n, (_, column) in enumerate(listed):
                tall = jnp.sum(score_ref[n * tok : (n + 1) * tok, :], axis=1, keepdims=True)
                row = jnp.sum(jnp.where(eye, jnp.broadcast_to(tall, (tok, tok)), 0.0), axis=0, keepdims=True)
                placed.append(jnp.where(line == column, jnp.broadcast_to(row, (8, tok)), 0.0))
            for i in range(ne):
                sd[i] = shares[0][i] * placed[0] + shares[1][i] * placed[1]
            for i in range(3):
                score_send(i).start()

        @pl.when(k == 6)
        def _():
            mine = sd[0]
            for i in range(3):
                score_send(i).wait_recv()
                mine += sr[i]
            szs[0] = mine

            @pl.when(at_end)
            def _():
                score_in().start()

        @pl.when(in_middle & (k == 7))
        def _():
            middle_to_z(0)

    to_x(14, 2)

    @pl.when(at_end)
    def _():
        end_to_z(4)
        end_to_z(5)

    @pl.when(in_middle)
    def _():
        middle_to_z(1)
        score_in().wait_recv()
        szs[0] += szr[upper]
        scores_from_middle().start()
        middle_to_z(2)
        middle_to_z(4)
        middle_to_z(3)
        scores_from_middle().wait_recv()
        szs[1] = szs[0] + szr[2]
        scores_out().start()
        grad_gate_ref[...] = szs[1, :2]
        middle_to_z(5)

    for k in (6, 7):
        share = total(k)

        @pl.when(at_end)
        def _():
            to_end(k - 2).wait_recv()
            done = share + ri[k - 2].astype(jnp.float32)
            for i in range(2):
                cols = pl.ds((2 * (k - 6) + i) * col, col)
                out_ref[:, cols] = done[i].astype(jnp.bfloat16)

        @pl.when(in_middle)
        def _():
            from_end(k - 2).wait_recv()
            from_middle(k - 4).wait_recv()
            done = share + ro[k - 2].astype(jnp.float32) + ri[k - 4].astype(jnp.float32)
            for i in range(2):
                cols = pl.ds((2 * (k - 6) + i) * col, col)
                out_ref[:, cols] = done[i].astype(jnp.bfloat16)

    @pl.when(at_end)
    def _():
        scores_out().wait_recv()
        grad_gate_ref[...] = szr[2, :2]
        score_in().wait_send()

    @pl.when(in_middle)
    def _():
        scores_from_middle().wait_send()
        scores_out().wait_send()

    for k in range(3):
        gate_send(k).wait_send()
        score_send(k).wait_send()

    @pl.loop(0, parts)
    def _(p):
        core_send(p, 1).wait_send()
        x_send(p, 1).wait_send()

    @pl.loop(parts // 2, 8)
    def _(k):
        core_send(2 * k, 2).wait_send()
        x_send(2 * k, 2).wait_send()

    @pl.loop(0, 6)
    def _(k):
        from_end(k).wait_send()

    for a in range(2):
        to_in(a, own_q, 0).wait_send()

        @pl.when(at_end)
        def _():
            across_in(a).wait_send()
            for q in range(3):
                over_x(a, q).wait_send()
                to_mate(a, q, across, 1).wait_send()
            part_x(a, 0).wait_send()
            for r in range(2):
                part_mate(a, r).wait_send()

        @pl.when(in_middle)
        def _():
            to_out(a, 1, 0).wait_send()
            to_out(a, 2, 1).wait_send()
            over_x(a, 1).wait_send()
            over_x(a, 2).wait_send()
            for r in range(2):
                part_in(a, r).wait_send()
                part_out(a, r).wait_send()
                part_x(a, r).wait_send()
            across_out(a).wait_send()
            for q in range(4):
                to_mate(a, q, across, 1).wait_send()

        for q in range(4):
            to_mate(a, q, e, 0).wait_send()


def layer(block_experts, tokens, grad_out, gates, w_gate, w_up, w_down):
    nz, ne = 4, 4
    tok, width = tokens.shape
    hidden = w_gate.shape[2]
    used = 2 * BLOCK
    hbm = pl.BlockSpec(memory_space=pl.ANY)
    vmem = pl.BlockSpec(memory_space=pltpu.VMEM)
    smem = pl.BlockSpec(memory_space=pltpu.SMEM)
    bf16, f32 = jnp.bfloat16, jnp.float32
    dma = pltpu.SemaphoreType.DMA
    return pl.pallas_call(
        functools.partial(layer_kernel, width),
        out_shape=(
            pltpu.VMEM((tok, width), bf16),
            pltpu.VMEM((2, tok), f32),
        ),
        in_specs=[smem, hbm, hbm, vmem, hbm, hbm, hbm],
        out_specs=(vmem, vmem),
        scratch_shapes=[
            pltpu.VMEM((nz, ne, tok, width), bf16),
            pltpu.VMEM((nz, ne, tok, width), bf16),
            pltpu.VMEM((ne, 8, tok), f32),
            pltpu.VMEM((2, width, hidden), bf16),
            pltpu.VMEM((2, width, hidden), bf16),
            pltpu.VMEM((2, hidden, width), bf16),
            pltpu.VMEM((used, width), bf16),
            pltpu.VMEM((used, width), bf16),
            pltpu.VMEM((used, hidden), f32),
            pltpu.VMEM((used, hidden), f32),
            pltpu.VMEM((used, hidden), f32),
            pltpu.VMEM((used, hidden), bf16),
            pltpu.VMEM((used, hidden), bf16),
            pltpu.VMEM((used, 128), f32),
            pltpu.VMEM((used, 128), f32),
            pltpu.VMEM((16, 2, 2, tok, 256), bf16),
            pltpu.VMEM((16, 2, tok, 256), bf16),
            pltpu.VMEM((16, tok, 256), bf16),
            pltpu.VMEM((16, tok, 256), bf16),
            pltpu.VMEM((6, 2, tok, 256), bf16),
            pltpu.VMEM((6, 2, tok, 256), bf16),
            pltpu.VMEM((6, 2, tok, 256), bf16),
            pltpu.VMEM((ne, 8, tok), f32),
            pltpu.VMEM((3, 8, tok), f32),
            pltpu.VMEM((2, 8, tok), f32),
            pltpu.VMEM((3, 8, tok), f32),
            dma((2, 3)),
            dma((2, 4)),
            dma((2, nz)),
            dma((2, nz, 2)),
            dma((2,)),
            dma((2, 2)),
            dma((2, 2)),
            dma((2, nz, ne)),
            dma((2, 2, 2)),
            dma((2, 3)),
            dma((2,)),
            dma((16,)),
            dma((16,)),
            dma((16,)),
            dma((16,)),
            dma((6,)),
            dma((6,)),
            dma((6,)),
            dma((3,)),
            dma((ne,)),
            dma((3,)),
            dma((3,)),
            dma((2,)),
            dma((2,)),
        ],
        compiler_params=pltpu.CompilerParams(
            collective_id=0, has_side_effects=True, vmem_limit_bytes=60 * 1024 * 1024
        ),
        name="layer",
    )(block_experts, tokens, grad_out, gates, w_gate, w_up, w_down)


def finish_kernel(grad_ref, gate_ref, grad_out_ref, gate_out_ref, sems):
    copies = (
        pltpu.make_async_copy(grad_ref, grad_out_ref, sems.at[0]),
        pltpu.make_async_copy(gate_ref, gate_out_ref, sems.at[1]),
    )
    for c in copies:
        c.start()
    for c in copies:
        c.wait()


def finish(grad, gate_rows):
    vmem = pl.BlockSpec(memory_space=pltpu.VMEM)
    hbm = pl.BlockSpec(memory_space=pl.ANY)
    return pl.pallas_call(
        finish_kernel,
        out_shape=(
            jax.ShapeDtypeStruct(grad.shape, grad.dtype),
            jax.ShapeDtypeStruct(gate_rows.shape, gate_rows.dtype),
        ),
        in_specs=[vmem, vmem],
        out_specs=(hbm, hbm),
        scratch_shapes=[pltpu.SemaphoreType.DMA((2,))],
        compiler_params=pltpu.CompilerParams(vmem_limit_bytes=1024 * 1024),
        name="finish",
    )(grad, gate_rows)


def fast_local(tokens, grad_out, gates, block_experts, w_gate, w_up, w_down):
    grad, gate_rows = layer(block_experts.T, tokens, grad_out, gates.T, w_gate, w_up, w_down)
    grad, gate_rows = finish(grad, gate_rows)
    return grad, gate_rows.T


def combined(owned, score, list_block, live, slot_hot, tok_dev, width_dev, capacity):
    n_experts = lax.axis_size("exp")
    own_index = lax.axis_index("exp")
    per_home = tok_dev // BLOCK
    result_cols = owned.reshape(width_dev, capacity, BLOCK)
    score_blocks = score.reshape(capacity, BLOCK)

    def share(home):
        wanted = home * per_home + jnp.arange(per_home, dtype=jnp.int32)
        select = ((list_block[None, :] == wanted[:, None]) & live[None, :]).astype(jnp.float32)
        grad_part = jnp.einsum("bi,dir->dbr", select, result_cols, precision=HIGHEST).reshape(
            width_dev, tok_dev
        )
        gate_part = jnp.einsum(
            "bi,ik,ir->kbr", select, slot_hot, score_blocks, precision=HIGHEST
        ).reshape(2, tok_dev)
        return (grad_part, gate_part)

    zero_totals = (
        jnp.zeros((width_dev, tok_dev), jnp.float32),
        jnp.zeros((2, tok_dev), jnp.float32),
    )

    def single_turn(step, totals):
        grad_part, gate_part = share((own_index + 1 + step) % n_experts)
        return passed_along((totals[0] + grad_part, totals[1] + gate_part), "exp", -1)

    totals = lax.fori_loop(0, n_experts - 1, single_turn, zero_totals)
    grad_part, gate_part = share(own_index)
    grad_total = totals[0] + grad_part
    gate_total = totals[1] + gate_part
    return (grad_total.T.astype(jnp.bfloat16), gate_total.T)


def local(tokens, grad_out, gates, block_experts, w_gate, w_up, w_down):
    own_index = lax.axis_index("exp")
    tok_dev, width_dev = tokens.shape
    blocks_all = block_experts.shape[0]
    capacity = blocks_all // 2
    used_count = capacity * BLOCK
    list_block, list_slot, live = routing(block_experts, own_index)
    row_index = (list_block[:, None] * BLOCK + jnp.arange(BLOCK, dtype=jnp.int32)[None, :]).reshape(
        used_count
    )
    x_home, dy_home, gate_home = (
        lax.all_gather(tokens, "exp", axis=0, tiled=True),
        lax.all_gather(grad_out, "exp", axis=0, tiled=True),
        lax.all_gather(gates, "exp", axis=0, tiled=True),
    )
    gate_pick = (
        jnp.take(gate_home, row_index, axis=0).astype(jnp.float32).reshape(capacity, BLOCK, 2)
    )
    slot_hot = (list_slot[:, None] == jnp.arange(2, dtype=jnp.int32)[None, :]).astype(jnp.float32)
    slot_hot = slot_hot * live[:, None].astype(jnp.float32)
    gate_column = jnp.sum(gate_pick * slot_hot[:, None, :], axis=2).reshape(used_count)
    x_piece = jnp.take(lax.all_gather(x_home, "hid", axis=1, tiled=True), row_index, axis=0)
    dy_piece = jnp.take(lax.all_gather(dy_home, "hid", axis=1, tiled=True), row_index, axis=0)
    pre_gate = jnp.dot(x_piece, w_gate[0], preferred_element_type=jnp.float32)
    pre_up = jnp.dot(x_piece, w_up[0], preferred_element_type=jnp.float32)
    d_hidden = lax.dot_general(dy_piece, w_down[0], CONTRACT_LAST, preferred_element_type=jnp.float32)
    sigmoid_gate = jax.nn.sigmoid(pre_gate)
    activated = pre_gate * sigmoid_gate
    score_part = jnp.sum(activated * pre_up * d_hidden, axis=1)
    score = lax.psum(score_part, "hid")
    scaled = gate_column[:, None] * d_hidden
    d_pre_gate = (scaled * pre_up * sigmoid_gate * (1.0 + pre_gate * (1.0 - sigmoid_gate))).astype(
        jnp.bfloat16
    )
    d_pre_up = (scaled * activated).astype(jnp.bfloat16)
    first = lax.dot_general(w_gate[0], d_pre_gate, CONTRACT_LAST, preferred_element_type=jnp.float32)
    owned = lax.psum_scatter(
        first
        + lax.dot_general(w_up[0], d_pre_up, CONTRACT_LAST, preferred_element_type=jnp.float32),
        "hid",
        scatter_dimension=0,
        tiled=True,
    )
    return combined(owned, score, list_block, live, slot_hot, tok_dev, width_dev, capacity)


def solution(mesh):
    placed = (
        P(("grp", "exp"), "hid"),
        P(("grp", "exp"), "hid"),
        P(("grp", "exp"), None),
        P("grp", None),
        P("exp", None, "hid"),
        P("exp", None, "hid"),
        P("exp", "hid", None),
    )
    body = fast_local if (mesh.shape["exp"], mesh.shape["hid"]) == (4, 4) else local
    return jax.shard_map(
        body,
        mesh=mesh,
        in_specs=placed,
        out_specs=(P(("grp", "exp"), "hid"), P(("grp", "exp"), None)),
        check_vma=False,
    )
```

```python
import functools
import jax
import jax.numpy as jnp
from jax import lax
from jax.experimental import pallas as pl
from jax.experimental.pallas import tpu as pltpu
from jax.sharding import PartitionSpec as P

BLOCK = 128


HIGHEST = lax.Precision.HIGHEST
CONTRACT_LAST = (((1,), (1,)), ((), ()))
MESH = pl.DeviceIdType.MESH


def passed_along(block, axis, distance):
    devices = range(lax.axis_size(axis))
    route = [((i - distance) % len(devices), i) for i in devices]
    return lax.ppermute(block, axis, route)


def routing(block_experts, own_index):
    blocks_all = block_experts.shape[0]
    capacity = blocks_all // 2
    matched = block_experts == own_index
    chosen = jnp.any(matched, axis=1)
    slot_of = matched[:, 1].astype(jnp.int32)
    order = jnp.arange(blocks_all, dtype=jnp.int32)
    position = jnp.sum((chosen[None, :] & (order[None, :] < order[:, None])).astype(jnp.int32), axis=1)
    placed = (position[None, :] == jnp.arange(capacity, dtype=jnp.int32)[:, None]) & chosen[None, :]
    placed_int = placed.astype(jnp.int32)
    list_block = jnp.sum(placed_int * jnp.arange(blocks_all, dtype=jnp.int32)[None, :], axis=1)
    list_slot = jnp.sum(placed_int * slot_of[None, :], axis=1)
    live = jnp.any(placed, axis=1)
    return list_block, list_slot, live


def layer_kernel(width, be_ref, tok_ref, dy_ref, gate_ref, w1_ref, w3_ref, w2_ref, out_ref, grad_gate_ref,
                 xb, db, gb, w1, w3, w2, xp, dp, pg, pu, dh, dpg_ref, dpu_ref, gcol, score_ref,
                 dense, cr, xs, xr, zs, ro, ri, sd, sr, szs, szr,
                 s_zi, s_zo, s_x, s_c, s_ex, s_xh, s_ch, rsem, hsem, wsem, lsem,
                 css, crs, xss, xrs, zss, ros, ris, gs, gr, gcs, gcr, gzs, gzr):
    nz, ne = 4, 4
    z = lax.axis_index("hid")
    e = lax.axis_index("exp")
    core = lax.rem(e, 2)
    side = e // 2
    mate = e + 1 - 2 * core
    across = lax.rem(e + 2, ne)
    mate_across = lax.rem(mate + 2, ne)
    upper = z // 2
    at_end = (z == 0) | (z == nz - 1)
    in_middle = (z == 1) | (z == 2)
    inward = z + 1 - 2 * upper
    outward = z - 1 + 2 * upper
    own_q = z + upper * (nz - 1 - 2 * z)
    bufs = (xb, db)
    own_refs = (tok_ref, dy_ref)
    picks = (xp, dp)
    hidden = w1.shape[2]
    tok = xb.shape[2]
    col = 256
    parts = 6
    partners = (mate, across, mate_across)

    barrier = pltpu.get_barrier_semaphore()
    pl.semaphore_signal(barrier, inc=1, device_id={"hid": inward}, device_id_type=MESH)
    for dev in partners:
        pl.semaphore_signal(barrier, inc=1, device_id={"exp": dev}, device_id_type=MESH)

    @pl.when(in_middle)
    def _():
        pl.semaphore_signal(barrier, inc=1, device_id={"hid": outward}, device_id_type=MESH)

    def real(q):
        return q + upper * (nz - 1 - 2 * q)

    order = (own_q, 1 - own_q, 2, 3)

    def load(ref, buf, j, i, slot):
        rows = pl.ds(pl.multiple_of(real(order[i]) * width, width), width)
        src = ref.at[0, :, rows] if j == 2 else ref.at[0, rows, :]
        return pltpu.make_async_copy(src, buf.at[slot], wsem.at[slot, j])

    def load_x(i, slot):
        return load(w1_ref, w1, 0, i, slot), load(w3_ref, w3, 1, i, slot)

    def load_d(i, slot):
        return load(w2_ref, w2, 2, i, slot)

    def remote(src, dst, ssem, rsem_, dev):
        return pltpu.make_async_remote_copy(
            src_ref=src, dst_ref=dst, send_sem=ssem, recv_sem=rsem_, device_id=dev, device_id_type=MESH)

    def send(a, q, eq, ssem, dev, src=None):
        zq = real(q)
        place = bufs[a].at[zq, eq]
        return remote(place if src is None else src, place, ssem, rsem.at[a, zq, eq], dev)

    def to_in(a, q, n, src=None):
        return send(a, q, e, s_zi.at[a, n], {"hid": inward}, src)

    def to_out(a, q, n, src=None):
        return send(a, q, e, s_zo.at[a, n], {"hid": outward}, src)

    def over_x(a, q, src=None):
        return send(a, q, e, s_x.at[a, real(q)], {"exp": across}, src)

    def to_mate(a, q, eq, k, src=None):
        return send(a, q, eq, s_c.at[a, real(q), k], {"exp": mate}, src)

    def across_in(a):
        return send(a, 0, across, s_ex.at[a], {"hid": inward})

    def part_of(a, q, eq, r):
        return bufs[a].at[real(q), eq, pl.ds(r * (tok // 2), tok // 2)]

    def send_part(a, q, eq, r, ssem, rsem_, dev):
        return remote(part_of(a, q, eq, r), part_of(a, q, eq, r), ssem, rsem_, dev)

    def part_in(a, r):
        return send_part(a, 0, e, r, s_zi.at[a, 1 + r], hsem.at[a, r, 0], {"hid": inward})

    def part_out(a, r):
        return send_part(a, 3, e, r, s_zo.at[a, 2 + r], hsem.at[a, r, 0], {"hid": outward})

    def part_x(a, r):
        return send_part(a, 3, e, r, s_xh.at[a, r], hsem.at[a, r, 1], {"exp": across})

    def part_mate(a, r):
        return send_part(a, 3, across, r, s_ch.at[a, r], rsem.at[a, real(3), across], {"exp": mate})

    def across_out(a):
        return send_part(a, 3, across, 1, s_ex.at[a], hsem.at[a, 1, 1], {"hid": outward})

    def part_arrived(a, r, c):
        send_part(a, 3, across if c else e, r, s_ex.at[a], hsem.at[a, r, c], {"exp": mate}).wait_recv()

    def arrived(a, q, eq):
        send(a, q, eq, s_ex.at[a], {"exp": mate}).wait_recv()

    def gate_send(k):
        return remote(gb.at[e], gb.at[e], gs.at[k], gr.at[e], {"exp": partners[k]})

    def gate_arrived(k):
        remote(gb.at[partners[k]], gb.at[partners[k]], gs.at[k], gr.at[partners[k]], {"exp": mate}).wait_recv()

    own = (
        pltpu.make_async_copy(tok_ref, xb.at[z, e], lsem.at[0]),
        pltpu.make_async_copy(dy_ref, db.at[z, e], lsem.at[1]),
    )
    for c in own:
        c.start()
    for i in range(2):
        for c in load_x(i, i):
            c.start()
        load_d(i, i).start()

    gb[e] = jnp.concatenate([gate_ref[...].astype(jnp.float32), jnp.zeros((6, tok), jnp.float32)], axis=0)
    pl.semaphore_wait(barrier, 4 + lax.rem((z + 1) // 2, 2))

    for a in range(2):
        to_in(a, own_q, 0, own_refs[a]).start()

        @pl.when(in_middle)
        def _():
            to_out(a, own_q, 0, own_refs[a]).start()

        over_x(a, own_q, own_refs[a]).start()
        to_mate(a, own_q, e, 0, own_refs[a]).start()
    for k in range(3):
        gate_send(k).start()

    first, first_slot = jnp.int32(-1), jnp.int32(0)
    last, last_slot = jnp.int32(-1), jnp.int32(0)
    for b in range(ne):
        one, two = be_ref[0, b] == e, be_ref[1, b] == e
        here = one | two
        column = two.astype(jnp.int32)
        fresh = here & (first < 0)
        later = here & (first >= 0)
        last, last_slot = jnp.where(later, b, last), jnp.where(later, column, last_slot)
        first, first_slot = jnp.where(fresh, b, first), jnp.where(fresh, column, first_slot)
    listed = ((first, first_slot), (last, last_slot))
    homes = (e, mate, across, mate_across)
    shares = [[(block == home).astype(jnp.float32) for home in homes] for block, _ in listed]

    def pick(a, i):
        q = order[i]
        arrived(a, q, mate)
        arrived(a, q, mate_across)
        zq = real(q)
        for n, (block, _) in enumerate(listed):
            rows = bufs[a][zq, ne - 1]
            for home in range(ne - 1):
                rows = jnp.where(block == home, bufs[a][zq, home], rows)
            picks[a][n * tok : (n + 1) * tok, :] = rows

    def relay(step, a):
        @pl.when(at_end)
        def _():
            if step < 2:
                arrived(a, step + 1, e)
                over_x(a, step + 1).start()
                to_mate(a, step + 1, e, 0).start()
            if step == 2:
                part_arrived(a, 0, 0)
                part_x(a, 0).start()
            if step < 3:
                arrived(a, step, across)
                if step == 0:
                    across_in(a).start()
                to_mate(a, step, across, 1).start()
            if step == 2:
                part_arrived(a, 1, 0)
                to_mate(a, 3, e, 0).start()
            if step == 3:
                for r in range(2):
                    part_arrived(a, r, 1)
                    part_mate(a, r).start()

        if step < 3:
            @pl.when(in_middle)
            def _():
                if step == 0:
                    arrived(a, 0, e)
                    for r in range(2):
                        part_in(a, r).start()
                    to_mate(a, 0, e, 0).start()
                    arrived(a, 2, e)
                    to_out(a, 2, 1).start()
                    over_x(a, 2).start()
                    to_mate(a, 2, e, 0).start()
                    arrived(a, 1, across)
                    to_mate(a, 1, across, 1).start()
                if step == 1:
                    for r in range(2):
                        part_arrived(a, r, 0)
                        part_out(a, r).start()
                        part_x(a, r).start()
                    to_mate(a, 3, e, 0).start()
                    arrived(a, 2, across)
                    to_mate(a, 2, across, 1).start()
                    arrived(a, 0, across)
                    to_mate(a, 0, across, 1).start()
                if step == 2:
                    for r in range(2):
                        part_arrived(a, r, 1)
                    across_out(a).start()
                    to_mate(a, 3, across, 1).start()

    def forward_x(i):
        slot = i % 2
        pick(0, i)
        for c in load_x(i, slot):
            c.wait()

        for total_ref, w in ((pg, w1), (pu, w3)):
            term = jnp.dot(xp[...], w[slot], preferred_element_type=jnp.float32)
            total_ref[...] = term if i == 0 else total_ref[...] + term

        if i + 2 < nz:
            for c in load_x(i + 2, slot):
                c.start()

    def forward_d(i):
        slot = i % 2
        pick(1, i)
        load_d(i, slot).wait()

        term = lax.dot_general(dp[...], w2[slot], CONTRACT_LAST, preferred_element_type=jnp.float32)
        dh[...] = term if i == 0 else dh[...] + term

        if i + 2 < nz:
            load_d(i + 2, slot).start()

    def gate_columns():
        for k in range(3):
            gate_arrived(k)
        eye = lax.broadcasted_iota(jnp.int32, (tok, tok), 0) == lax.broadcasted_iota(jnp.int32, (tok, tok), 1)
        for n, (block, column) in enumerate(listed):
            row = jnp.zeros((1, tok), jnp.float32)
            for home in range(ne):
                for k in range(2):
                    chosen = ((block == home) & (column == k)).astype(jnp.float32)
                    row = row + chosen * gb[home, k : k + 1, :]
            col = jnp.sum(jnp.where(eye, jnp.broadcast_to(row, (tok, tok)), 0.0), axis=1, keepdims=True)
            gcol[n * tok : (n + 1) * tok, :] = jnp.broadcast_to(col, (tok, 128))

    for c in own:
        c.wait()
    score_ref[...] = jnp.zeros_like(score_ref)
    for step in range(3):
        relay(step, 0)
        forward_x(step)
        relay(step, 1)
        forward_d(step)
        if step == 0:
            gate_columns()

    WIDE = 512

    def last_dots(t):
        cols = pl.ds(t * WIDE, WIDE)
        dh[:, cols] += lax.dot_general(dp[...], w2[1, cols, :], CONTRACT_LAST, preferred_element_type=jnp.float32)

    def pointwise(t):
        for c in range(WIDE // 128):
            cols = pl.ds(t * WIDE + c * 128, 128)
            for r in range(0, 2 * tok, 64):
                rows = pl.ds(r, 64)
                g = pg[rows, cols]
                u = pu[rows, cols]
                h = dh[rows, cols]
                sig = 1.0 / (1.0 + jnp.exp(-g))
                act = g * sig
                score_ref[rows, :] += act * u * h
                scaled = gcol[rows, :] * h
                dpg_ref[rows, cols] = (scaled * u * sig * (1.0 + g * (1.0 - sig))).astype(jnp.bfloat16)
                dpu_ref[rows, cols] = (scaled * act).astype(jnp.bfloat16)

    def last_x(t):
        cols = pl.ds(t * (hidden // 2), hidden // 2)
        pg[:, cols] += jnp.dot(xp[...], w1[1, :, cols], preferred_element_type=jnp.float32)
        pu[:, cols] += jnp.dot(xp[...], w3[1, :, cols], preferred_element_type=jnp.float32)

    relay(3, 0)
    pick(0, 3)
    for c in load_x(3, 1):
        c.wait()
    last_x(0)
    relay(3, 1)
    last_x(1)
    pick(1, 3)
    load_d(3, 1).wait()
    last_dots(0)
    for t in range(1, hidden // WIDE):
        last_dots(t)
        pointwise(t - 1)
    pointwise(hidden // WIDE - 1)

    def again(j, slot):
        zq = real(own_q + (3 - j) * (1 - 2 * own_q))
        rows = pl.ds(pl.multiple_of(zq * width, width), width)
        return (
            pltpu.make_async_copy(w1_ref.at[0, rows, :], w1.at[slot], wsem.at[slot, 0]),
            pltpu.make_async_copy(w3_ref.at[0, rows, :], w3.at[slot], wsem.at[slot, 1]),
        )

    def core_send(p, n):
        return remote(dense.at[pl.ds(p, n), 1], cr.at[pl.ds(p, n)], css.at[p], crs.at[p], {"exp": mate})

    def x_send(p, n):
        return remote(xs.at[pl.ds(p, n)], xr.at[pl.ds(p, n)], xss.at[p], xrs.at[p], {"exp": across})

    def from_end(k):
        return remote(zs.at[k], ro.at[k], zss.at[k], ros.at[k], {"hid": inward})

    def from_middle(k):
        return remote(zs.at[k], ri.at[k], zss.at[k], ris.at[k], {"hid": inward})

    def to_end(k):
        return remote(zs.at[k], ri.at[k], zss.at[k], ris.at[k], {"hid": outward})

    def spread(p, grad):
        for c in range(2):
            for far in range(2):
                home = c + 2 * far
                dense[p, c, far] = (shares[0][home] * grad[:tok] + shares[1][home] * grad[tok:]).astype(jnp.bfloat16)

    def product(slot, rows):
        grad = lax.dot_general(dpg_ref[...], w1[slot, rows, :], CONTRACT_LAST, preferred_element_type=jnp.float32)
        return grad + lax.dot_general(dpu_ref[...], w3[slot, rows, :], CONTRACT_LAST, preferred_element_type=jnp.float32)

    def multiply(k):
        j = k // 2
        slot = lax.rem(j + 1, 2)

        @pl.when((lax.rem(k, 2) == 0) & (j >= 2))
        def _():
            for c in again(j, slot):
                c.wait()

        grad = product(slot, pl.ds(pl.multiple_of(lax.rem(k, 2) * 2 * col, 2 * col), 2 * col))
        for i in range(2):
            spread(2 * k + i, grad[:, i * col : (i + 1) * col])
        core_send(2 * k, 2).start()

        @pl.when(k == 3)
        def _():
            for c in again(3, 0):
                c.start()

    def to_x(p, n):
        core_send(p, n).wait_recv()
        part = pl.ds(p, n)
        xs[part] = (dense[part, 0, 1].astype(jnp.float32) + cr[part, 1].astype(jnp.float32)).astype(jnp.bfloat16)
        x_send(p, n).start()

    def total(k):
        @pl.when(k < parts // 2)
        def _():
            for i in range(2):
                x_send(2 * k + i, 1).wait_recv()

        @pl.when(k >= parts // 2)
        def _():
            x_send(2 * k, 2).wait_recv()

        part = pl.ds(2 * k, 2)
        return dense[part, 0, 0].astype(jnp.float32) + cr[part, 0].astype(jnp.float32) + xr[part].astype(jnp.float32)

    def end_to_z(k):
        zs[k] = total(k).astype(jnp.bfloat16)
        from_end(k).start()

    def middle_to_z(k):
        share = total(k)

        @pl.when(k < 4)
        def _():
            from_end(k).wait_recv()
            zs[k] = (share + ro[k].astype(jnp.float32)).astype(jnp.bfloat16)
            from_middle(k).start()

        @pl.when(k >= 4)
        def _():
            from_middle(k - 4).wait_recv()
            zs[k] = (share + ri[k - 4].astype(jnp.float32)).astype(jnp.bfloat16)
            to_end(k).start()

    def score_send(k):
        return remote(sd.at[k + 1], sr.at[k], gcs.at[k], gcr.at[k], {"exp": partners[k]})

    def score_in():
        return remote(szs.at[0], szr.at[upper], gzs.at[0], gzr.at[0], {"hid": inward})

    def scores_from_middle():
        return remote(szs.at[0], szr.at[2], gzs.at[0], gzr.at[1], {"hid": inward})

    def scores_out():
        return remote(szs.at[1], szr.at[2], gzs.at[1], gzr.at[1], {"hid": outward})

    spread(0, product(1, pl.ds(0, col)))
    core_send(0, 1).start()

    @pl.loop(1, parts)
    def _(p):
        rows = pl.ds(pl.multiple_of(lax.rem(p, 4) * col, col), col)
        spread(p, product(1 - p // 4, rows))
        core_send(p, 1).start()
        to_x(p - 1, 1)

        @pl.when(p == 3)
        def _():
            for c in again(2, 1):
                c.start()

    @pl.when(at_end)
    def _():
        end_to_z(0)

    @pl.loop(parts // 2, 8)
    def _(k):
        multiply(k)

        @pl.when(k == parts // 2)
        def _():
            to_x(parts - 1, 1)

        @pl.when(k > parts // 2)
        def _():
            to_x(2 * k - 2, 2)

        @pl.when(at_end & (lax.rem(k, 3) > 0))
        def _():
            end_to_z((2 * k - 4) // 3)

        @pl.when(k == 4)
        def _():
            eye = lax.broadcasted_iota(jnp.int32, (tok, tok), 0) == lax.broadcasted_iota(jnp.int32, (tok, tok), 1)
            line = lax.broadcasted_iota(jnp.int32, (8, tok), 0)
            placed = []
            for n, (_, column) in enumerate(listed):
                tall = jnp.sum(score_ref[n * tok : (n + 1) * tok, :], axis=1, keepdims=True)
                row = jnp.sum(jnp.where(eye, jnp.broadcast_to(tall, (tok, tok)), 0.0), axis=0, keepdims=True)
                placed.append(jnp.where(line == column, jnp.broadcast_to(row, (8, tok)), 0.0))
            for i in range(ne):
                sd[i] = shares[0][i] * placed[0] + shares[1][i] * placed[1]
            for i in range(3):
                score_send(i).start()

        @pl.when(k == 6)
        def _():
            mine = sd[0]
            for i in range(3):
                score_send(i).wait_recv()
                mine += sr[i]
            szs[0] = mine

            @pl.when(at_end)
            def _():
                score_in().start()

        @pl.when(in_middle & (k == 7))
        def _():
            middle_to_z(0)

    to_x(14, 2)

    @pl.when(at_end)
    def _():
        end_to_z(4)
        end_to_z(5)

    @pl.when(in_middle)
    def _():
        middle_to_z(1)
        score_in().wait_recv()
        szs[0] += szr[upper]
        scores_from_middle().start()
        middle_to_z(2)
        middle_to_z(4)
        middle_to_z(3)
        scores_from_middle().wait_recv()
        szs[1] = szs[0] + szr[2]
        scores_out().start()
        grad_gate_ref[...] = szs[1, :2]
        middle_to_z(5)

    for k in (6, 7):
        share = total(k)

        @pl.when(at_end)
        def _():
            to_end(k - 2).wait_recv()
            done = share + ri[k - 2].astype(jnp.float32)
            for i in range(2):
                cols = pl.ds((2 * (k - 6) + i) * col, col)
                out_ref[:, cols] = done[i].astype(jnp.bfloat16)

        @pl.when(in_middle)
        def _():
            from_end(k - 2).wait_recv()
            from_middle(k - 4).wait_recv()
            done = share + ro[k - 2].astype(jnp.float32) + ri[k - 4].astype(jnp.float32)
            for i in range(2):
                cols = pl.ds((2 * (k - 6) + i) * col, col)
                out_ref[:, cols] = done[i].astype(jnp.bfloat16)

    @pl.when(at_end)
    def _():
        scores_out().wait_recv()
        grad_gate_ref[...] = szr[2, :2]
        score_in().wait_send()

    @pl.when(in_middle)
    def _():
        scores_from_middle().wait_send()
        scores_out().wait_send()

    for k in range(3):
        gate_send(k).wait_send()
        score_send(k).wait_send()

    @pl.loop(0, parts)
    def _(p):
        core_send(p, 1).wait_send()
        x_send(p, 1).wait_send()

    @pl.loop(parts // 2, 8)
    def _(k):
        core_send(2 * k, 2).wait_send()
        x_send(2 * k, 2).wait_send()

    @pl.loop(0, 6)
    def _(k):
        from_end(k).wait_send()

    for a in range(2):
        to_in(a, own_q, 0).wait_send()

        @pl.when(at_end)
        def _():
            across_in(a).wait_send()
            for q in range(3):
                over_x(a, q).wait_send()
                to_mate(a, q, across, 1).wait_send()
            part_x(a, 0).wait_send()
            for r in range(2):
                part_mate(a, r).wait_send()

        @pl.when(in_middle)
        def _():
            to_out(a, 1, 0).wait_send()
            to_out(a, 2, 1).wait_send()
            over_x(a, 1).wait_send()
            over_x(a, 2).wait_send()
            for r in range(2):
                part_in(a, r).wait_send()
                part_out(a, r).wait_send()
                part_x(a, r).wait_send()
            across_out(a).wait_send()
            for q in range(4):
                to_mate(a, q, across, 1).wait_send()

        for q in range(4):
            to_mate(a, q, e, 0).wait_send()


def layer(block_experts, tokens, grad_out, gates, w_gate, w_up, w_down):
    nz, ne = 4, 4
    tok, width = tokens.shape
    hidden = w_gate.shape[2]
    used = 2 * BLOCK
    hbm = pl.BlockSpec(memory_space=pl.ANY)
    vmem = pl.BlockSpec(memory_space=pltpu.VMEM)
    smem = pl.BlockSpec(memory_space=pltpu.SMEM)
    bf16, f32 = jnp.bfloat16, jnp.float32
    dma = pltpu.SemaphoreType.DMA
    return pl.pallas_call(
        functools.partial(layer_kernel, width),
        out_shape=(
            pltpu.VMEM((tok, width), bf16),
            pltpu.VMEM((2, tok), f32),
        ),
        in_specs=[smem, hbm, hbm, vmem, hbm, hbm, hbm],
        out_specs=(vmem, vmem),
        scratch_shapes=[
            pltpu.VMEM((nz, ne, tok, width), bf16),
            pltpu.VMEM((nz, ne, tok, width), bf16),
            pltpu.VMEM((ne, 8, tok), f32),
            pltpu.VMEM((2, width, hidden), bf16),
            pltpu.VMEM((2, width, hidden), bf16),
            pltpu.VMEM((2, hidden, width), bf16),
            pltpu.VMEM((used, width), bf16),
            pltpu.VMEM((used, width), bf16),
            pltpu.VMEM((used, hidden), f32),
            pltpu.VMEM((used, hidden), f32),
            pltpu.VMEM((used, hidden), f32),
            pltpu.VMEM((used, hidden), bf16),
            pltpu.VMEM((used, hidden), bf16),
            pltpu.VMEM((used, 128), f32),
            pltpu.VMEM((used, 128), f32),
            pltpu.VMEM((16, 2, 2, tok, 256), bf16),
            pltpu.VMEM((16, 2, tok, 256), bf16),
            pltpu.VMEM((16, tok, 256), bf16),
            pltpu.VMEM((16, tok, 256), bf16),
            pltpu.VMEM((6, 2, tok, 256), bf16),
            pltpu.VMEM((6, 2, tok, 256), bf16),
            pltpu.VMEM((6, 2, tok, 256), bf16),
            pltpu.VMEM((ne, 8, tok), f32),
            pltpu.VMEM((3, 8, tok), f32),
            pltpu.VMEM((2, 8, tok), f32),
            pltpu.VMEM((3, 8, tok), f32),
            dma((2, 3)),
            dma((2, 4)),
            dma((2, nz)),
            dma((2, nz, 2)),
            dma((2,)),
            dma((2, 2)),
            dma((2, 2)),
            dma((2, nz, ne)),
            dma((2, 2, 2)),
            dma((2, 3)),
            dma((2,)),
            dma((16,)),
            dma((16,)),
            dma((16,)),
            dma((16,)),
            dma((6,)),
            dma((6,)),
            dma((6,)),
            dma((3,)),
            dma((ne,)),
            dma((3,)),
            dma((3,)),
            dma((2,)),
            dma((2,)),
        ],
        compiler_params=pltpu.CompilerParams(
            collective_id=0, has_side_effects=True, vmem_limit_bytes=60 * 1024 * 1024
        ),
        name="layer",
    )(block_experts, tokens, grad_out, gates, w_gate, w_up, w_down)


def finish_kernel(grad_ref, gate_ref, grad_out_ref, gate_out_ref, sems):
    copies = (
        pltpu.make_async_copy(grad_ref, grad_out_ref, sems.at[0]),
        pltpu.make_async_copy(gate_ref, gate_out_ref, sems.at[1]),
    )
    for c in copies:
        c.start()
    for c in copies:
        c.wait()


def finish(grad, gate_rows):
    vmem = pl.BlockSpec(memory_space=pltpu.VMEM)
    hbm = pl.BlockSpec(memory_space=pl.ANY)
    return pl.pallas_call(
        finish_kernel,
        out_shape=(
            jax.ShapeDtypeStruct(grad.shape, grad.dtype),
            jax.ShapeDtypeStruct(gate_rows.shape, gate_rows.dtype),
        ),
        in_specs=[vmem, vmem],
        out_specs=(hbm, hbm),
        scratch_shapes=[pltpu.SemaphoreType.DMA((2,))],
        compiler_params=pltpu.CompilerParams(vmem_limit_bytes=1024 * 1024),
        name="finish",
    )(grad, gate_rows)


def fast_local(tokens, grad_out, gates, block_experts, w_gate, w_up, w_down):
    grad, gate_rows = layer(block_experts.T, tokens, grad_out, gates.T, w_gate, w_up, w_down)
    grad, gate_rows = finish(grad, gate_rows)
    return grad, gate_rows.T


def combined(owned, score, list_block, live, slot_hot, tok_dev, width_dev, capacity):
    n_experts = lax.axis_size("exp")
    own_index = lax.axis_index("exp")
    per_home = tok_dev // BLOCK
    result_cols = owned.reshape(width_dev, capacity, BLOCK)
    score_blocks = score.reshape(capacity, BLOCK)

    def share(home):
        wanted = home * per_home + jnp.arange(per_home, dtype=jnp.int32)
        select = ((list_block[None, :] == wanted[:, None]) & live[None, :]).astype(jnp.float32)
        grad_part = jnp.einsum("bi,dir->dbr", select, result_cols, precision=HIGHEST).reshape(
            width_dev, tok_dev
        )
        gate_part = jnp.einsum(
            "bi,ik,ir->kbr", select, slot_hot, score_blocks, precision=HIGHEST
        ).reshape(2, tok_dev)
        return (grad_part, gate_part)

    zero_totals = (
        jnp.zeros((width_dev, tok_dev), jnp.float32),
        jnp.zeros((2, tok_dev), jnp.float32),
    )

    def single_turn(step, totals):
        grad_part, gate_part = share((own_index + 1 + step) % n_experts)
        return passed_along((totals[0] + grad_part, totals[1] + gate_part), "exp", -1)

    totals = lax.fori_loop(0, n_experts - 1, single_turn, zero_totals)
    grad_part, gate_part = share(own_index)
    grad_total = totals[0] + grad_part
    gate_total = totals[1] + gate_part
    return (grad_total.T.astype(jnp.bfloat16), gate_total.T)


def local(tokens, grad_out, gates, block_experts, w_gate, w_up, w_down):
    own_index = lax.axis_index("exp")
    tok_dev, width_dev = tokens.shape
    blocks_all = block_experts.shape[0]
    capacity = blocks_all // 2
    used_count = capacity * BLOCK
    list_block, list_slot, live = routing(block_experts, own_index)
    row_index = (list_block[:, None] * BLOCK + jnp.arange(BLOCK, dtype=jnp.int32)[None, :]).reshape(
        used_count
    )
    x_home, dy_home, gate_home = (
        lax.all_gather(tokens, "exp", axis=0, tiled=True),
        lax.all_gather(grad_out, "exp", axis=0, tiled=True),
        lax.all_gather(gates, "exp", axis=0, tiled=True),
    )
    gate_pick = (
        jnp.take(gate_home, row_index, axis=0).astype(jnp.float32).reshape(capacity, BLOCK, 2)
    )
    slot_hot = (list_slot[:, None] == jnp.arange(2, dtype=jnp.int32)[None, :]).astype(jnp.float32)
    slot_hot = slot_hot * live[:, None].astype(jnp.float32)
    gate_column = jnp.sum(gate_pick * slot_hot[:, None, :], axis=2).reshape(used_count)
    x_piece = jnp.take(lax.all_gather(x_home, "hid", axis=1, tiled=True), row_index, axis=0)
    dy_piece = jnp.take(lax.all_gather(dy_home, "hid", axis=1, tiled=True), row_index, axis=0)
    pre_gate = jnp.dot(x_piece, w_gate[0], preferred_element_type=jnp.float32)
    pre_up = jnp.dot(x_piece, w_up[0], preferred_element_type=jnp.float32)
    d_hidden = lax.dot_general(dy_piece, w_down[0], CONTRACT_LAST, preferred_element_type=jnp.float32)
    sigmoid_gate = jax.nn.sigmoid(pre_gate)
    activated = pre_gate * sigmoid_gate
    score_part = jnp.sum(activated * pre_up * d_hidden, axis=1)
    score = lax.psum(score_part, "hid")
    scaled = gate_column[:, None] * d_hidden
    d_pre_gate = (scaled * pre_up * sigmoid_gate * (1.0 + pre_gate * (1.0 - sigmoid_gate))).astype(
        jnp.bfloat16
    )
    d_pre_up = (scaled * activated).astype(jnp.bfloat16)
    first = lax.dot_general(w_gate[0], d_pre_gate, CONTRACT_LAST, preferred_element_type=jnp.float32)
    owned = lax.psum_scatter(
        first
        + lax.dot_general(w_up[0], d_pre_up, CONTRACT_LAST, preferred_element_type=jnp.float32),
        "hid",
        scatter_dimension=0,
        tiled=True,
    )
    return combined(owned, score, list_block, live, slot_hot, tok_dev, width_dev, capacity)


def solution(mesh):
    placed = (
        P(("grp", "exp"), "hid"),
        P(("grp", "exp"), "hid"),
        P(("grp", "exp"), None),
        P("grp", None),
        P("exp", None, "hid"),
        P("exp", None, "hid"),
        P("exp", "hid", None),
    )
    body = fast_local if (mesh.shape["exp"], mesh.shape["hid"]) == (4, 4) else local
    return jax.shard_map(
        body,
        mesh=mesh,
        in_specs=placed,
        out_specs=(P(("grp", "exp"), "hid"), P(("grp", "exp"), None)),
        check_vma=False,
    )
```
